128 devices in a mesh: rows: 8 (over z, core), cols: 16 (over x, y).
Axes of the slice: x: 4, y: 4, z: 4, core: 2. Of those that a mesh axis runs over, the one named last changes fastest.
Arguments:
- pixels: bfloat16 [3, 1024, 4096], P(None, 'rows', 'cols'), may hold values from -6 to 6
- patch_weight: bfloat16 [48, 256], replicated, may hold values from -0.875 to 0.875
- patch_bias: float32 [256], replicated, may hold values from -4 to 4
- conv_kernel: float32 [49, 256], replicated, may hold values from -0.875 to 0.875
- norm_gain: float32 [256], replicated, may hold values from 0.1 to 1.9
- kv_weight: bfloat16 [256, 2048], replicated, may hold values from -0.375 to 0.375
- latents: bfloat16 [256, 1024], replicated, may hold values from -80 to 80, as said below
- d_attended: bfloat16 [256, 1024], replicated, may hold values from -6 to 6
Outputs:
- attended: float32 [256, 1024], replicated
- grad_latents: float32 [256, 1024], replicated
- grad_kv_weight: float32 [256, 2048], replicated
- grad_norm_gain: float32 [256], replicated
- grad_conv_kernel: float32 [49, 256], replicated
- grad_patch_weight: float32 [48, 256], replicated
- grad_patch_bias: float32 [256], replicated
The draws below stay inside these ranges and needn't reach their ends.
Inputs may be any that keep to these rules, and one draw needn't show every extreme that they name: `latents`: each latent row has its own scale.
All inputs are finite; a program needn't handle non-finite values.
Results may differ from the reference program's by a relative error of at most 0.035.
The reference program's roundings to bfloat16 on the way count: a program that leaves them out, or rounds other values in their place, can miss the bound.
Values may be sent and summed in bfloat16 or wider, within the bound.
No kernel may reach another device: no remote copies, remote signals or barrier semaphores. Data moves between devices by JAX's collectives and lax.ppermute only.
A program may use at most 576 MiB of HBM per device.

```python
import math
import jax
import jax.numpy as jnp
from jax import lax

PATCH = 4
KSIZE = 7
IN_CHANNELS = 3
CHANNELS = 256
HEADS = 8
DIM = 1024
LATENTS = 256
IMG_H = 1024
IMG_W = 4096


def draw_latents(key, part):
    key_rows = jax.random.fold_in(key, 11)
    key_vals = jax.random.fold_in(key, 12)
    row_scale = jnp.exp(jax.random.uniform(key_rows, (LATENTS, 1), jnp.float32, math.log(0.3), math.log(3.0)))
    entries = jax.random.truncated_normal(key_vals, -4.0, 4.0, (LATENTS, DIM), jnp.float32)
    return (entries * row_scale).astype(jnp.bfloat16)


def block_levels(stream_key, extent, shards, smallest, top_value):
    def one(position, parts):
        draws = jax.random.uniform(jax.random.fold_in(jax.random.fold_in(stream_key, 6), position), (parts,), jnp.float32, smallest / len(shards), top_value / len(shards))
        return jnp.repeat(jnp.exp(draws), extent[position] // parts).reshape((-1,) + (1,) * (len(extent) - position - 1))

    factor_of = one(*shards[0])
    for cut in shards[1:]:
        factor_of = factor_of * one(*cut)
    return factor_of


def gaussian(own_key, dims, spread, reach, shards=(), held_as=jnp.bfloat16):
    values = jax.random.normal(own_key, dims, jnp.float32) * spread
    if len(shards) > 0:
        values = block_levels(own_key, dims, shards, -0.22, 0.18) * values
    return jnp.clip(values, min=-reach, max=reach).astype(held_as)


def setup_inputs(seed: int = 0) -> dict:
    keys = jax.random.split(jax.random.key(seed), 9)
    pixels = gaussian(keys[0], (IN_CHANNELS, IMG_H, IMG_W), 1.0, 6.0, ((1, 8), (2, 16)))
    patch_weight = gaussian(keys[1], (IN_CHANNELS * PATCH * PATCH, CHANNELS), (IN_CHANNELS * PATCH * PATCH) ** -0.5, 0.875)
    patch_bias = gaussian(keys[2], (CHANNELS,), 1.0, 4.0, (), jnp.float32)
    conv_kernel = gaussian(keys[3], (KSIZE * KSIZE, CHANNELS), (KSIZE * KSIZE) ** -0.5, 0.875, (), jnp.float32)
    norm_gain = jnp.clip(1.0 + 0.18 * jax.random.normal(keys[4], (CHANNELS,), jnp.float32), 0.1, 1.9)
    kv_weight = gaussian(keys[5], (CHANNELS, 2 * DIM), CHANNELS ** -0.5, 0.375)
    latents = draw_latents(jax.random.fold_in(keys[8], 71), 0)
    d_attended = gaussian(keys[7], (LATENTS, DIM), 1.0, 6.0)
    return {"pixels": pixels, "patch_weight": patch_weight, "patch_bias": patch_bias, "conv_kernel": conv_kernel, "norm_gain": norm_gain, "kv_weight": kv_weight, "latents": latents, "d_attended": d_attended}


norm_eps = 1e-05

def patch_rows(pixels):
    in_channels, height, image_width = pixels.shape
    blocks = pixels.reshape(in_channels, height // PATCH, PATCH, image_width // PATCH, PATCH)
    blocks = blocks.transpose(1, 3, 0, 2, 4)
    return blocks.reshape(height // PATCH * (image_width // PATCH), in_channels * PATCH * PATCH)

def depthwise(padded, kernel, tile_rows, tile_cols):
    result = jnp.zeros((tile_rows, tile_cols, kernel.shape[1]), jnp.float32)
    for offset_row in range(KSIZE):
        for offset_col in range(KSIZE):
            window = padded[offset_row:offset_row + tile_rows, offset_col:offset_col + tile_cols].astype(jnp.float32)
            result = result + window * kernel[offset_row * KSIZE + offset_col]
    return result

def transposed(padded, kernel, tile_rows, tile_cols):
    result = jnp.zeros((tile_rows, tile_cols, kernel.shape[1]), jnp.float32)
    last = KSIZE - 1
    for offset_row in range(KSIZE):
        for offset_col in range(KSIZE):
            start_row = last - offset_row
            start_col = last - offset_col
            window = padded[start_row:start_row + tile_rows, start_col:start_col + tile_cols].astype(jnp.float32)
            result = result + window * kernel[offset_row * KSIZE + offset_col]
    return result

def kernel_grad(padded, upstream, tile_rows, tile_cols):
    upstream_f = upstream.astype(jnp.float32)
    kernel_terms = []
    for offset_row in range(KSIZE):
        for offset_col in range(KSIZE):
            window = padded[offset_row:offset_row + tile_rows, offset_col:offset_col + tile_cols].astype(jnp.float32)
            kernel_terms.append(lax.optimization_barrier(jnp.sum(window * upstream_f, axis=(0, 1))))
    return jnp.stack(kernel_terms)

def normalize(mixed):
    centre = mixed - lax.optimization_barrier(jnp.mean(mixed, axis=-1, keepdims=True))
    variance = lax.optimization_barrier(jnp.mean(centre * centre, axis=-1, keepdims=True))
    inverse = lax.rsqrt(variance + norm_eps)
    return (centre * inverse, inverse)

def split_heads(matrix, head_count):
    return matrix.reshape(matrix.shape[0], head_count, -1).transpose(1, 0, 2)

def merge_heads(stacked):
    return stacked.transpose(1, 0, 2).reshape(stacked.shape[1], -1)

def head_pass(pieces):
    queries, key_rows, values, upstream = pieces
    score_scale = queries.shape[-1] ** (-0.5)
    scores = jnp.dot(queries, key_rows.T, preferred_element_type=jnp.float32) * score_scale
    top_score = lax.optimization_barrier(jnp.max(scores, axis=1, keepdims=True))
    raised = jnp.exp(scores - top_score)
    sum_exp = lax.optimization_barrier(jnp.sum(raised, axis=1, keepdims=True))
    attended = jnp.dot(raised.astype(jnp.bfloat16), values, preferred_element_type=jnp.float32) / sum_exp
    row_dots = lax.optimization_barrier(jnp.sum(upstream.astype(jnp.float32) * attended, axis=1, keepdims=True))
    probs = raised / sum_exp
    d_probs = jnp.dot(upstream, values.T, preferred_element_type=jnp.float32)
    d_scores = (probs * (d_probs - row_dots) * score_scale).astype(jnp.bfloat16)
    q_grad = jnp.dot(d_scores, key_rows, preferred_element_type=jnp.float32)
    k_grad = jnp.dot(d_scores.T, queries, preferred_element_type=jnp.float32).astype(jnp.bfloat16)
    v_grad = jnp.dot(probs.astype(jnp.bfloat16).T, upstream, preferred_element_type=jnp.float32).astype(jnp.bfloat16)
    return (attended, q_grad, k_grad, v_grad)

def reference(pixels, patch_weight, patch_bias, conv_kernel, norm_gain, kv_weight, latents, d_attended):
    tile_rows = pixels.shape[1] // PATCH
    tile_cols = pixels.shape[2] // PATCH
    channels = patch_weight.shape[1]
    model_dim = latents.shape[1]
    patches = patch_rows(pixels)
    embedded = (jnp.dot(patches, patch_weight, preferred_element_type=jnp.float32) + patch_bias).astype(jnp.bfloat16)
    embedded = embedded.reshape(tile_rows, tile_cols, channels)
    half_width = KSIZE // 2
    padded = jnp.pad(embedded, ((half_width, half_width), (half_width, half_width), (0, 0)))
    mixed = embedded.astype(jnp.float32) + depthwise(padded, conv_kernel, tile_rows, tile_cols)
    centred, inverse = normalize(mixed)
    normed = (centred * norm_gain).astype(jnp.bfloat16).reshape(tile_rows * tile_cols, channels)
    projected = jnp.dot(normed, kv_weight, preferred_element_type=jnp.float32).astype(jnp.bfloat16)
    stacked = lax.map(head_pass, (split_heads(latents, HEADS), split_heads(projected[:, :model_dim], HEADS), split_heads(projected[:, model_dim:], HEADS), split_heads(d_attended, HEADS)))
    attended = merge_heads(stacked[0])
    grad_latents = merge_heads(stacked[1])
    d_projected = jnp.concatenate([merge_heads(stacked[2]), merge_heads(stacked[3])], axis=1)
    grad_kv = jnp.dot(normed.T, d_projected, preferred_element_type=jnp.float32)
    d_normed = jnp.dot(d_projected, kv_weight.T, preferred_element_type=jnp.float32).reshape(tile_rows, tile_cols, channels)
    grad_gain = lax.optimization_barrier(jnp.sum(d_normed * centred, axis=(0, 1)))
    scaled = d_normed * norm_gain
    d_mixed = inverse * (scaled - lax.optimization_barrier(jnp.mean(scaled, axis=-1, keepdims=True)) - centred * lax.optimization_barrier(jnp.mean(scaled * centred, axis=-1, keepdims=True)))
    d_mixed = d_mixed.astype(jnp.bfloat16)
    grad_kernel = kernel_grad(padded, d_mixed, tile_rows, tile_cols)
    d_padded = jnp.pad(d_mixed, ((half_width, half_width), (half_width, half_width), (0, 0)))
    d_embedded = (d_mixed.astype(jnp.float32) + transposed(d_padded, conv_kernel, tile_rows, tile_cols)).astype(jnp.bfloat16)
    d_embedded = d_embedded.reshape(tile_rows * tile_cols, channels)
    grad_patch = jnp.dot(patches.T, d_embedded, preferred_element_type=jnp.float32)
    grad_bias = lax.optimization_barrier(jnp.sum(d_embedded.astype(jnp.float32), axis=0))
    return (attended, grad_latents, grad_kv, grad_gain, grad_kernel, grad_patch, grad_bias)
```

```python
import functools

import jax
import jax.numpy as jnp
from jax import lax
from jax.experimental import pallas as pl
from jax.experimental.pallas import tpu as pltpu
from jax.sharding import PartitionSpec as P

PATCH = 4
KSIZE = 7
HEADS = 8
HALO = 3
norm_eps = 1e-05
BF = jnp.bfloat16
F32 = jnp.float32
NT = (((1,), (1,)), ((), ()))
TN = (((0,), (0,)), ((), ()))
NN = (((1,), (0,)), ((), ()))
ROWS = 32
COLS = 64
CH = 256
TOK = ROWS * COLS
WIDE = 14
VMEM = pltpu.CompilerParams(vmem_limit_bytes=58 << 20)


def dot(a, b, dims=NN):
    return lax.dot_general(a, b, dims, preferred_element_type=F32)


def iota(shape, dim):
    return lax.broadcasted_iota(jnp.int32, shape, dim)


def write_edges(src, top, bot, left, right, corners, l_sc, r_sc, c_sc):
    top[...] = src[0 : HALO * COLS, :]
    bot[...] = src[TOK - HALO * COLS : TOK, :]
    for a in range(ROWS):
        low = src[a * COLS : a * COLS + 32, :].astype(F32)
        high = src[a * COLS + 32 : a * COLS + 64, :].astype(F32)
        for k in range(HALO):
            l_sc[k * ROWS + a : k * ROWS + a + 1, :] = low[8 * k : 8 * k + 1, :]
            r_sc[k * ROWS + a : k * ROWS + a + 1, :] = high[8 * k + 15 : 8 * k + 16, :]
    left[...] = l_sc[...].astype(BF)
    right[...] = r_sc[...].astype(BF)
    c_sc[...] = jnp.zeros_like(c_sc)
    for k in range(HALO):
        for i in range(HALO):
            first = k * ROWS + i
            last = k * ROWS + ROWS - HALO + i
            row = k * HALO + i
            c_sc[0, row : row + 1, :] = l_sc[first : first + 1, :]
            c_sc[1, row : row + 1, :] = r_sc[first : first + 1, :]
            c_sc[2, row : row + 1, :] = l_sc[last : last + 1, :]
            c_sc[3, row : row + 1, :] = r_sc[last : last + 1, :]
    corners[...] = c_sc[...].astype(BF)


EDGE_SHAPES = [
    jax.ShapeDtypeStruct((HALO * COLS, CH), BF),
    jax.ShapeDtypeStruct((HALO * COLS, CH), BF),
    jax.ShapeDtypeStruct((HALO * ROWS, CH), BF),
    jax.ShapeDtypeStruct((HALO * ROWS, CH), BF),
    jax.ShapeDtypeStruct((4, 16, CH), BF),
]
EDGE_SCRATCH = [
    pltpu.VMEM((HALO * ROWS, CH), F32),
    pltpu.VMEM((HALO * ROWS, CH), F32),
    pltpu.VMEM((4, 16, CH), F32),
]


def exchange(edges):
    top, bot, left, right, corners = edges
    n_r, n_c = lax.axis_size("rows"), lax.axis_size("cols")

    def move(x, d_r, d_c):
        pairs = [
            (r * n_c + c, (r + d_r) * n_c + c + d_c)
            for r in range(n_r)
            for c in range(n_c)
            if 0 <= r + d_r < n_r and 0 <= c + d_c < n_c
        ]
        return lax.ppermute(x, ("rows", "cols"), pairs)

    return (
        move(bot, 1, 0),
        move(top, -1, 0),
        move(right, 0, 1),
        move(left, 0, -1),
        move(corners[3], 1, 1),
        move(corners[2], 1, -1),
        move(corners[1], -1, 1),
        move(corners[0], -1, -1),
    )


def assemble(wide, own, halo, l_sc, r_sc, c_sc):
    above, below, left, right, tl, tr, bl, br = halo
    l_sc[...] = left[...].astype(F32)
    r_sc[...] = right[...].astype(F32)
    for n, ref in enumerate((tl, tr, bl, br)):
        c_sc[n] = ref[...].astype(F32)
    sub = iota((8, CH), 0)

    def put(row, x, lefts, rights):
        x = x.astype(F32).reshape(8, 8, CH)
        for cb in range(8):
            wide[row, HALO + cb] = x[cb]
        for k in range(HALO):
            wide[row, k] = jnp.where(sub == 0, lefts[k], pltpu.roll(x[5 + k], 1, 0))
            wide[row, 11 + k] = jnp.where(sub == 7, rights[k], pltpu.roll(x[k], 7, 0))

    for i in range(HALO):
        row = [k * HALO + i for k in range(HALO)]
        put(
            i,
            above[i * COLS : (i + 1) * COLS, :],
            [c_sc[0, n : n + 1, :] for n in row],
            [c_sc[1, n : n + 1, :] for n in row],
        )
        put(
            HALO + ROWS + i,
            below[i * COLS : (i + 1) * COLS, :],
            [c_sc[2, n : n + 1, :] for n in row],
            [c_sc[3, n : n + 1, :] for n in row],
        )

    def body(a, carry):
        put(
            a + HALO,
            own[pl.ds(pl.multiple_of(a * COLS, COLS), COLS), :],
            [l_sc[pl.ds(k * ROWS + a, 1), :] for k in range(HALO)],
            [r_sc[pl.ds(k * ROWS + a, 1), :] for k in range(HALO)],
        )
        return carry

    lax.fori_loop(0, ROWS, body, 0)


def spread_weights(kernel_ref, w_sc):
    for n in range(KSIZE * KSIZE):
        w_sc[n] = jnp.broadcast_to(kernel_ref[n : n + 1, :], (8, CH))


def conv_row(wide, w_sc, a, half, flip):
    lanes = pl.ds(half * 128, 128)
    acc = [wide[a + HALO, HALO + cb, :, lanes] for cb in range(8)]
    for i in range(KSIZE):
        xs = [wide[a + i, c, :, lanes] for c in range(WIDE)]
        for j in range(KSIZE):
            n = i * KSIZE + j
            w = w_sc[KSIZE * KSIZE - 1 - n if flip else n, :, lanes]
            acc = [acc[cb] + xs[cb + j] * w for cb in range(8)]
    return acc


def norm_rows(x):
    centre = x - jnp.sum(x, axis=-1, keepdims=True) * (1.0 / CH)
    variance = jnp.sum(centre * centre, axis=-1, keepdims=True) * (1.0 / CH)
    inverse = lax.rsqrt(variance + norm_eps)
    return centre * inverse, inverse


def embed_kernel(pixels, weights, bias, emb, z_ref, top, bot, left, right, corners, w_sc, l_sc, r_sc, c_sc):
    out = iota((256, 256), 0)
    spread = (((out & 7) * 8 + ((out >> 3) & 7)) * 4 + (out >> 6)) == iota((256, 256), 1)
    spread = jnp.where(spread, 1.0, 0.0).astype(BF)
    by_cell = dot(spread, pixels[...], NT).astype(BF)
    row = iota((512, 384), 0)
    fu = row & 15
    target = (fu >> 2) * 128 + (row >> 4) * 4 + (fu & 3)
    order = jnp.where((target == iota((512, 384), 1)) & (fu < 12), 1.0, 0.0).astype(BF)
    z = dot(by_cell, order, NT).astype(BF)
    for g in range(4):
        for v in range(4):
            z_ref[g * 64 : (g + 1) * 64, v * 128 : (v + 1) * 128] = z[
                v * 64 : (v + 1) * 64, g * 128 : (g + 1) * 128
            ]
    w_sc[...] = jnp.zeros_like(w_sc)
    for v in range(4):
        for a8 in range(8):
            first = v * 128 + a8 * 16
            w_sc[first : first + 16, a8 * CH : (a8 + 1) * CH] = weights[v]
    for a8 in range(8):
        block = dot(z_ref[...], w_sc[:, a8 * CH : (a8 + 1) * CH]) + bias[...]
        block = block.astype(BF)
        for g in range(4):
            a = g * 8 + a8
            emb[a * COLS : (a + 1) * COLS, :] = block[g * 64 : (g + 1) * 64, :]
    write_edges(emb, top, bot, left, right, corners, l_sc, r_sc, c_sc)


def embed(pixels, patch_weight, patch_bias):
    weights = patch_weight.reshape(12, 4, CH).transpose(1, 0, 2)
    weights = jnp.pad(weights, ((0, 0), (0, 4), (0, 0)))
    outs = pl.pallas_call(
        embed_kernel,
        name="embed",
        out_shape=[
            jax.ShapeDtypeStruct((TOK, CH), BF),
            jax.ShapeDtypeStruct((256, 512), BF),
        ]
        + EDGE_SHAPES,
        scratch_shapes=[pltpu.VMEM((512, 2048), BF)] + EDGE_SCRATCH,
        compiler_params=VMEM,
    )(pixels.reshape(384, 256), weights, patch_bias.reshape(1, CH))
    return outs[0], outs[1], outs[2:]


def conv_kernel_body(emb, above, below, lh, rh, tl, tr, bl, br, kern, gain, wide, mixed, normed, w_sc, l_sc, r_sc, c_sc):
    assemble(wide, emb, (above, below, lh, rh, tl, tr, bl, br), l_sc, r_sc, c_sc)
    spread_weights(kern, w_sc)

    def body(a, carry):
        for half in range(2):
            acc = conv_row(wide, w_sc, a, half, False)
            for cb in range(8):
                rows = pl.ds(pl.multiple_of(a * COLS + cb * 8, 8), 8)
                mixed[rows, pl.ds(half * 128, 128)] = acc[cb]
        return carry

    lax.fori_loop(0, ROWS, body, 0)

    def norm_body(a, carry):
        rows = pl.ds(pl.multiple_of(a * COLS, COLS), COLS)
        centred, _ = norm_rows(mixed[rows, :])
        normed[rows, :] = (centred * gain[...]).astype(BF)
        return carry

    lax.fori_loop(0, ROWS, norm_body, 0)


def conv_forward(emb, halo, conv_kernel, gain):
    return pl.pallas_call(
        conv_kernel_body,
        name="conv_forward",
        out_shape=[
            jax.ShapeDtypeStruct((ROWS + 2 * HALO, WIDE, 8, CH), F32),
            jax.ShapeDtypeStruct((TOK, CH), F32),
            jax.ShapeDtypeStruct((TOK, CH), BF),
        ],
        scratch_shapes=[pltpu.VMEM((KSIZE * KSIZE, 8, CH), F32)] + EDGE_SCRATCH,
        compiler_params=VMEM,
    )(emb, *halo, conv_kernel, gain)


CHUNK = 512
SCALE = 128**-0.5


def attend_kernel(normed, wk, wv, q, up, k_out, v_out, weighted, stats, s_sc):
    h = pl.program_id(0)
    w = jnp.concatenate([wk[...], wv[...]], axis=1)
    peak = None
    for c in range(TOK // CHUNK):
        rows = slice(c * CHUNK, (c + 1) * CHUNK)
        kv = dot(normed[rows, :], w).astype(BF)
        k_out[rows, :] = kv[:, :128]
        v_out[rows, :] = kv[:, 128:]
        s = dot(kv[:, :128], q[...], NT) * SCALE
        s_sc[rows, :] = s
        top = jnp.max(s, axis=0, keepdims=True)
        peak = top if peak is None else jnp.maximum(peak, top)
    total = jnp.zeros((1, 256), F32)
    acc = jnp.zeros((128, 256), F32)
    for c in range(TOK // CHUNK):
        rows = slice(c * CHUNK, (c + 1) * CHUNK)
        p = jnp.exp(s_sc[rows, :] - peak)
        total = total + jnp.sum(p, axis=0, keepdims=True)
        acc = acc + dot(v_out[rows, :], p.astype(BF), TN)
    weighted[...] = acc.T
    dots = jnp.sum(acc * up[...].astype(F32).T, axis=0, keepdims=True)
    stats[0, pl.ds(h, 1), :] = peak
    stats[1, pl.ds(h, 1), :] = total
    stats[2, pl.ds(h, 1), :] = dots


def whole(shape):
    return pl.BlockSpec(shape, lambda h: (0,) * len(shape))


def column(rows, width, first=0):
    return pl.BlockSpec((rows, width), lambda h: (0, h + first))


def attend(normed, kv_weight, latents, d_attended):
    return pl.pallas_call(
        attend_kernel,
        name="attend",
        grid=(HEADS,),
        in_specs=[
            whole((TOK, CH)),
            column(CH, 128),
            column(CH, 128, HEADS),
            column(256, 128),
            column(256, 128),
        ],
        out_specs=[
            column(TOK, 128),
            column(TOK, 128),
            column(256, 128),
            whole((3, HEADS, 256)),
        ],
        out_shape=[
            jax.ShapeDtypeStruct((TOK, 1024), BF),
            jax.ShapeDtypeStruct((TOK, 1024), BF),
            jax.ShapeDtypeStruct((256, 1024), F32),
            jax.ShapeDtypeStruct((3, HEADS, 256), F32),
        ],
        scratch_shapes=[pltpu.VMEM((TOK, 256), F32)],
        compiler_params=VMEM,
    )(normed, kv_weight, kv_weight, latents, d_attended)


def attend_grad_kernel(
    normed, k_in, v_in, wk, wv, q, up, lse, dots, mixed, gain,
    q_grad, k_weight, v_weight, d_mixed, gain_grad, top, bot, left, right, corners,
    dn_sc, nt_sc, l_sc, r_sc, c_sc,
):
    h = pl.program_id(0)

    @pl.when(h == 0)
    def _():
        nt_sc[...] = normed[...].astype(F32).T.astype(BF)
        dn_sc[...] = jnp.zeros_like(dn_sc)

    w = jnp.concatenate([wk[...], wv[...]], axis=1)
    level = lse[pl.ds(h, 1), :]
    row_dots = dots[pl.ds(h, 1), :]
    qg = jnp.zeros((128, 256), F32)
    wg = jnp.zeros((256, 256), F32)
    for c in range(TOK // CHUNK):
        rows = slice(c * CHUNK, (c + 1) * CHUNK)
        k = k_in[rows, :]
        p = jnp.exp(dot(k, q[...], NT) * SCALE - level)
        dp = dot(v_in[rows, :], up[...], NT)
        ds = (p * (dp - row_dots) * SCALE).astype(BF)
        qg = qg + dot(k, ds, TN)
        kg = dot(ds, q[...]).astype(BF)
        vg = dot(p.astype(BF), up[...]).astype(BF)
        d_proj = jnp.concatenate([kg, vg], axis=1)
        wg = wg + dot(nt_sc[:, rows], d_proj)
        dn_sc[rows, :] += dot(d_proj, w, NT)
    q_grad[...] = qg.T
    k_weight[...] = wg[:, :128]
    v_weight[...] = wg[:, 128:]

    @pl.when(h == HEADS - 1)
    def _():
        def body(a, total):
            rows = pl.ds(pl.multiple_of(a * COLS, COLS), COLS)
            centred, inverse = norm_rows(mixed[rows, :])
            dn = dn_sc[rows, :]
            total = total + jnp.sum(dn * centred, axis=0, keepdims=True)
            g = dn * gain[...]
            mean = jnp.sum(g, axis=-1, keepdims=True) * (1.0 / CH)
            slope = jnp.sum(g * centred, axis=-1, keepdims=True) * (1.0 / CH)
            d_mixed[rows, :] = (inverse * (g - mean - centred * slope)).astype(BF)
            return total

        gain_grad[...] = lax.fori_loop(0, ROWS, body, jnp.zeros((1, CH), F32))
        write_edges(d_mixed, top, bot, left, right, corners, l_sc, r_sc, c_sc)


def attend_grad(normed, k, v, kv_weight, latents, d_attended, lse, dots, mixed, gain):
    outs = pl.pallas_call(
        attend_grad_kernel,
        name="attend_grad",
        grid=(HEADS,),
        in_specs=[
            whole((TOK, CH)),
            column(TOK, 128),
            column(TOK, 128),
            column(CH, 128),
            column(CH, 128, HEADS),
            column(256, 128),
            column(256, 128),
            whole((HEADS, 256)),
            whole((HEADS, 256)),
            whole((TOK, CH)),
            whole((1, CH)),
        ],
        out_specs=[column(256, 128), column(CH, 128), column(CH, 128), whole((TOK, CH)), whole((1, CH))]
        + [whole(s.shape) for s in EDGE_SHAPES],
        out_shape=[
            jax.ShapeDtypeStruct((256, 1024), F32),
            jax.ShapeDtypeStruct((CH, 1024), F32),
            jax.ShapeDtypeStruct((CH, 1024), F32),
            jax.ShapeDtypeStruct((TOK, CH), BF),
            jax.ShapeDtypeStruct((1, CH), F32),
        ]
        + EDGE_SHAPES,
        scratch_shapes=[pltpu.VMEM((TOK, CH), F32), pltpu.VMEM((CH, TOK), BF)] + EDGE_SCRATCH,
        compiler_params=VMEM,
    )(normed, k, v, kv_weight, kv_weight, latents, d_attended, lse, dots, mixed, gain)
    return outs[:5], outs[5:]


def kernel_grad_body(wide, d_mixed, out, d_sc):
    d_sc[...] = d_mixed[...].astype(F32)
    for half in range(2):
        lanes = pl.ds(half * 128, 128)
        for i in range(KSIZE):

            def body(a, acc):
                xs = [wide[a + i, c, :, lanes] for c in range(WIDE)]
                base = pl.multiple_of(a * COLS, COLS)
                ds = [d_sc[pl.ds(base + cb * 8, 8), lanes] for cb in range(8)]
                acc = list(acc)
                for cb in range(8):
                    for j in range(KSIZE):
                        acc[j] = acc[j] + xs[cb + j] * ds[cb]
                return tuple(acc)

            zero = jnp.zeros((8, 128), F32)
            acc = lax.fori_loop(0, ROWS, body, (zero,) * KSIZE)
            for j in range(KSIZE):
                n = i * KSIZE + j
                out[n : n + 1, lanes] = jnp.sum(acc[j], axis=0, keepdims=True)


def kernel_grad(wide, d_mixed):
    return pl.pallas_call(
        kernel_grad_body,
        name="kernel_grad",
        out_shape=jax.ShapeDtypeStruct((KSIZE * KSIZE, CH), F32),
        scratch_shapes=[pltpu.VMEM((TOK, CH), F32)],
        compiler_params=VMEM,
    )(wide, d_mixed)


def conv_back_body(d_mixed, above, below, lh, rh, tl, tr, bl, br, kern, z, patch_grad, bias_grad, wide, d_sc, w_sc, l_sc, r_sc, c_sc):
    assemble(wide, d_mixed, (above, below, lh, rh, tl, tr, bl, br), l_sc, r_sc, c_sc)
    spread_weights(kern, w_sc)
    zero = jnp.zeros((8, 128), F32)

    def body(a, bias):
        bias = list(bias)
        for half in range(2):
            acc = conv_row(wide, w_sc, a, half, True)
            acc = jnp.concatenate(acc, axis=0).astype(BF)
            d_sc[a & 7, pl.ds(pl.multiple_of((a >> 3) * 64, 64), 64), pl.ds(half * 128, 128)] = acc
            bias[half] = bias[half] + jnp.sum(acc.astype(F32).reshape(8, 8, 128), axis=0)
        return tuple(bias)

    bias = lax.fori_loop(0, ROWS, body, (zero, zero))
    for half in range(2):
        bias_grad[:, half * 128 : (half + 1) * 128] = jnp.sum(bias[half], axis=0, keepdims=True)
    total = [jnp.zeros((16, CH), F32) for _ in range(4)]
    for a8 in range(8):
        part = dot(z[...], d_sc[a8], TN)
        for v in range(4):
            first = v * 128 + a8 * 16
            total[v] = total[v] + part[first : first + 16, :]
    for v in range(4):
        patch_grad[v] = total[v]


def conv_back(d_mixed, halo, conv_kernel, z):
    return pl.pallas_call(
        conv_back_body,
        name="conv_back",
        out_shape=[jax.ShapeDtypeStruct((4, 16, CH), F32), jax.ShapeDtypeStruct((1, CH), F32)],
        scratch_shapes=[
            pltpu.VMEM((ROWS + 2 * HALO, WIDE, 8, CH), F32),
            pltpu.VMEM((8, 256, CH), BF),
            pltpu.VMEM((KSIZE * KSIZE, 8, CH), F32),
        ]
        + EDGE_SCRATCH,
        compiler_params=VMEM,
    )(d_mixed, *halo, conv_kernel, z)


def rings():
    n_r, n_c = lax.axis_size("rows"), lax.axis_size("cols")
    side = 4
    out = []
    for axis, size, inner in (("rows", 2, 1), ("rows", n_r // 2, 2), ("cols", side, 1), ("cols", n_c // side, side)):
        total = lax.axis_size(axis)
        shifts = []
        for d in range(1, size):
            pairs = []
            for i in range(total):
                pos = i // inner % size
                pairs.append((i, i + ((pos + d) % size - pos) * inner))
            shifts.append(pairs)
        out.append((axis, shifts))
    return out


def combine_stats(stats):
    for axis, shifts in rings():
        group = [stats] + [lax.ppermute(stats, axis, pairs) for pairs in shifts]
        peak = functools.reduce(jnp.maximum, [g[0] for g in group])
        factors = [jnp.exp(g[0] - peak) for g in group]
        total = sum(g[1] * f for g, f in zip(group, factors))
        dots = sum(g[2] * f for g, f in zip(group, factors))
        stats = jnp.stack([peak, total, dots])
    return stats


AXES = ("rows", "cols")


def all_sum(x):
    count = lax.axis_size(AXES)
    rows = x.shape[0] // count
    parts = lax.all_to_all(x, AXES, 0, 0, tiled=True)
    mine = jnp.sum(parts.reshape(count, rows, -1), axis=0)
    copies = jnp.broadcast_to(mine[None], (count,) + mine.shape).reshape(x.shape)
    return lax.all_to_all(copies, AXES, 0, 0, tiled=True)


def per_device(
    pixels, patch_weight, patch_bias, conv_kernel, norm_gain, kv_weight, latents, d_attended
):
    gain = norm_gain.reshape(1, CH)
    emb, z, edges = embed(pixels, patch_weight, patch_bias)
    wide, mixed, normed = conv_forward(emb, exchange(edges), conv_kernel, gain)
    k, v, weighted, local = attend(normed, kv_weight, latents, d_attended)
    stats = combine_stats(local)
    lse = stats[0] + jnp.log(stats[1])
    row_dots = stats[2] / stats[1]
    factor = (jnp.exp(local[0] - stats[0]) / stats[1]).T
    attended = (weighted.reshape(256, HEADS, 128) * factor[:, :, None]).reshape(256, 1024)
    (q_grad, k_weight, v_weight, d_mixed, gain_grad), d_edges = attend_grad(
        normed, k, v, kv_weight, latents, d_attended, lse, row_dots, mixed, gain
    )
    big = all_sum(jnp.concatenate([attended, q_grad, k_weight, v_weight], axis=0))
    halo = exchange(d_edges)
    kern = kernel_grad(wide, d_mixed)
    patch, bias = conv_back(d_mixed, halo, conv_kernel, z)
    small = jnp.concatenate([patch.reshape(64, CH), kern, gain_grad, bias], axis=0)
    small = all_sum(jnp.pad(small, ((0, 128 - small.shape[0]), (0, 0))))
    patch = small[:64].reshape(4, 16, CH)[:, :12].transpose(1, 0, 2).reshape(48, CH)
    return (
        big[:256],
        big[256:512],
        jnp.concatenate([big[512:768], big[768:]], axis=1),
        small[64 + 49],
        small[64 : 64 + 49],
        patch,
        small[64 + 50],
    )


def solution(mesh):
    return jax.shard_map(
        per_device,
        mesh=mesh,
        in_specs=(P(None, "rows", "cols"), P(), P(), P(), P(), P(), P(), P()),
        out_specs=(P(), P(), P(), P(), P(), P(), P()),
        check_vma=False,
    )
```

```python
import jax
import jax.numpy as jnp
from jax import lax
from jax.experimental import pallas as pl
from jax.experimental.pallas import tpu as pltpu
from jax.sharding import Mesh
from jax.sharding import PartitionSpec as P

PATCH = 4
KSIZE = 7
HEADS = 8
HALO = 3
norm_eps = 1e-05
BF = jnp.bfloat16
F32 = jnp.float32
NT = (((1,), (1,)), ((), ()))
TN = (((0,), (0,)), ((), ()))
NN = (((1,), (0,)), ((), ()))
ROWS = 32
COLS = 64
CH = 256
TOK = ROWS * COLS
WIDE = 14
WIRE = BF
ROW_AXES = ("z", "core")
COL_AXES = ("x", "y")
VMEM = pltpu.CompilerParams(vmem_limit_bytes=58 << 20)


def dot(a, b, dims=NN):
    return lax.dot_general(a, b, dims, preferred_element_type=F32)


def iota(shape, dim):
    return lax.broadcasted_iota(jnp.int32, shape, dim)


def write_edges(src, top, bot, left, right, l_sc, r_sc, c_sc):
    for a in range(ROWS):
        low = src[a * COLS : a * COLS + 32, :].astype(F32)
        high = src[a * COLS + 32 : a * COLS + 64, :].astype(F32)
        for k in range(HALO):
            l_sc[k * ROWS + a : k * ROWS + a + 1, :] = low[8 * k : 8 * k + 1, :]
            r_sc[k * ROWS + a : k * ROWS + a + 1, :] = high[8 * k + 15 : 8 * k + 16, :]
    left[...] = l_sc[...].astype(BF)
    right[...] = r_sc[...].astype(BF)
    c_sc[...] = jnp.zeros_like(c_sc)
    for k in range(HALO):
        for i in range(HALO):
            first = k * ROWS + i
            last = k * ROWS + ROWS - HALO + i
            row = k * HALO + i
            c_sc[0, row : row + 1, :] = l_sc[first : first + 1, :]
            c_sc[1, row : row + 1, :] = r_sc[first : first + 1, :]
            c_sc[2, row : row + 1, :] = l_sc[last : last + 1, :]
            c_sc[3, row : row + 1, :] = r_sc[last : last + 1, :]
    side = HALO * COLS
    top[:side, :] = src[0:side, :]
    bot[:side, :] = src[TOK - side : TOK, :]
    for n, ref in enumerate((top, bot)):
        ref[side : side + 16, :] = c_sc[2 * n].astype(BF)
        ref[side + 16 : side + 32, :] = c_sc[2 * n + 1].astype(BF)


EDGE_SHAPES = [
    jax.ShapeDtypeStruct((HALO * COLS + 32, CH), BF),
    jax.ShapeDtypeStruct((HALO * COLS + 32, CH), BF),
    jax.ShapeDtypeStruct((HALO * ROWS, CH), BF),
    jax.ShapeDtypeStruct((HALO * ROWS, CH), BF),
]
EDGE_SCRATCH = [
    pltpu.VMEM((HALO * ROWS, CH), F32),
    pltpu.VMEM((HALO * ROWS, CH), F32),
    pltpu.VMEM((4, 16, CH), F32),
]


def exchange_rows(edges):
    top, bot = edges[:2]
    n = lax.axis_size(ROW_AXES)
    above = lax.ppermute(bot, ROW_AXES, [(i, i + 1) for i in range(n - 1)])
    below = lax.ppermute(top, ROW_AXES, [(i + 1, i) for i in range(n - 1)])
    return above, below


def exchange_cols(edges, above, below):
    left, right = edges[2:]
    n = lax.axis_size(COL_AXES)
    side = HALO * COLS
    right = jnp.concatenate([right, above[side + 16 : side + 32], below[side + 16 : side + 32]])
    left = jnp.concatenate([left, above[side : side + 16], below[side : side + 16]])
    from_left = lax.ppermute(right, COL_AXES, [(i, i + 1) for i in range(n - 1)])
    from_right = lax.ppermute(left, COL_AXES, [(i + 1, i) for i in range(n - 1)])
    return from_left, from_right


def assemble(wide, own, halo, l_sc, r_sc, c_sc):
    above, below, left, right = halo
    edge = HALO * ROWS
    l_sc[...] = left[:edge, :].astype(F32)
    r_sc[...] = right[:edge, :].astype(F32)
    for n in range(2):
        c_sc[2 * n] = left[edge + 16 * n : edge + 16 * (n + 1), :].astype(F32)
        c_sc[2 * n + 1] = right[edge + 16 * n : edge + 16 * (n + 1), :].astype(F32)
    sub = iota((8, CH), 0)

    def put(row, x, lefts, rights):
        x = x.astype(F32).reshape(8, 8, CH)
        for cb in range(8):
            wide[row, HALO + cb] = x[cb]
        for k in range(HALO):
            wide[row, k] = jnp.where(sub == 0, lefts[k], pltpu.roll(x[5 + k], 1, 0))
            wide[row, 11 + k] = jnp.where(sub == 7, rights[k], pltpu.roll(x[k], 7, 0))

    for i in range(HALO):
        row = [k * HALO + i for k in range(HALO)]
        put(
            i,
            above[i * COLS : (i + 1) * COLS, :],
            [c_sc[0, n : n + 1, :] for n in row],
            [c_sc[1, n : n + 1, :] for n in row],
        )
        put(
            HALO + ROWS + i,
            below[i * COLS : (i + 1) * COLS, :],
            [c_sc[2, n : n + 1, :] for n in row],
            [c_sc[3, n : n + 1, :] for n in row],
        )

    def body(a, carry):
        put(
            a + HALO,
            own[pl.ds(pl.multiple_of(a * COLS, COLS), COLS), :],
            [l_sc[pl.ds(k * ROWS + a, 1), :] for k in range(HALO)],
            [r_sc[pl.ds(k * ROWS + a, 1), :] for k in range(HALO)],
        )
        return carry

    lax.fori_loop(0, ROWS, body, 0)


def spread_weights(kernel_ref, w_sc):
    for n in range(KSIZE * KSIZE):
        w_sc[n] = jnp.broadcast_to(kernel_ref[n : n + 1, :], (8, CH))


def conv_row(wide, w_sc, a, half, flip):
    lanes = pl.ds(half * 128, 128)
    acc = [wide[a + HALO, HALO + cb, :, lanes] for cb in range(8)]
    for i in range(KSIZE):
        xs = [wide[a + i, c, :, lanes] for c in range(WIDE)]
        for j in range(KSIZE):
            n = i * KSIZE + j
            w = w_sc[KSIZE * KSIZE - 1 - n if flip else n, :, lanes]
            acc = [acc[cb] + xs[cb + j] * w for cb in range(8)]
    return acc


def norm_rows(x):
    centre = x - jnp.sum(x, axis=-1, keepdims=True) * (1.0 / CH)
    variance = jnp.sum(centre * centre, axis=-1, keepdims=True) * (1.0 / CH)
    inverse = lax.rsqrt(variance + norm_eps)
    return centre * inverse, inverse


def embed_kernel(pixels, weights, bias, emb, z_ref, top, bot, left, right, w_sc, l_sc, r_sc, c_sc):
    out = iota((256, 256), 0)
    spread = (((out & 7) * 8 + ((out >> 3) & 7)) * 4 + (out >> 6)) == iota((256, 256), 1)
    spread = jnp.where(spread, 1.0, 0.0).astype(BF)
    by_cell = dot(spread, pixels[...], NT).astype(BF)
    row = iota((512, 384), 0)
    fu = row & 15
    target = (fu >> 2) * 128 + (row >> 4) * 4 + (fu & 3)
    order = jnp.where((target == iota((512, 384), 1)) & (fu < 12), 1.0, 0.0).astype(BF)
    z = dot(by_cell, order, NT).astype(BF)
    for g in range(4):
        for v in range(4):
            z_ref[g * 64 : (g + 1) * 64, v * 128 : (v + 1) * 128] = z[
                v * 64 : (v + 1) * 64, g * 128 : (g + 1) * 128
            ]
    w_sc[...] = jnp.zeros_like(w_sc)
    for v in range(4):
        for a8 in range(8):
            first = v * 128 + a8 * 16
            w_sc[first : first + 16, a8 * CH : (a8 + 1) * CH] = weights[v]
    for a8 in range(8):
        block = dot(z_ref[...], w_sc[:, a8 * CH : (a8 + 1) * CH]) + bias[...]
        block = block.astype(BF)
        for g in range(4):
            a = g * 8 + a8
            emb[a * COLS : (a + 1) * COLS, :] = block[g * 64 : (g + 1) * 64, :]
    write_edges(emb, top, bot, left, right, l_sc, r_sc, c_sc)


def embed(pixels, patch_weight, patch_bias):
    weights = patch_weight.reshape(12, 4, CH).transpose(1, 0, 2)
    weights = jnp.pad(weights, ((0, 0), (0, 4), (0, 0)))
    outs = pl.pallas_call(
        embed_kernel,
        name="embed",
        out_shape=[
            jax.ShapeDtypeStruct((TOK, CH), BF),
            jax.ShapeDtypeStruct((256, 512), BF),
        ]
        + EDGE_SHAPES,
        scratch_shapes=[pltpu.VMEM((512, 2048), BF)] + EDGE_SCRATCH,
        compiler_params=VMEM,
    )(pixels.reshape(384, 256), weights, patch_bias.reshape(1, CH))
    return outs[0], outs[1], outs[2:]


def conv_kernel_body(emb, above, below, lh, rh, kern, gain, wide, mixed, normed, w_sc, l_sc, r_sc, c_sc):
    assemble(wide, emb, (above, below, lh, rh), l_sc, r_sc, c_sc)
    spread_weights(kern, w_sc)

    def body(a, carry):
        for half in range(2):
            acc = conv_row(wide, w_sc, a, half, False)
            for cb in range(8):
                rows = pl.ds(pl.multiple_of(a * COLS + cb * 8, 8), 8)
                mixed[rows, pl.ds(half * 128, 128)] = acc[cb]
        return carry

    lax.fori_loop(0, ROWS, body, 0)

    def norm_body(a, carry):
        rows = pl.ds(pl.multiple_of(a * COLS, COLS), COLS)
        centred, _ = norm_rows(mixed[rows, :])
        normed[rows, :] = (centred * gain[...]).astype(BF)
        return carry

    lax.fori_loop(0, ROWS, norm_body, 0)


def conv_forward(emb, halo, conv_kernel, gain):
    return pl.pallas_call(
        conv_kernel_body,
        name="conv_forward",
        out_shape=[
            jax.ShapeDtypeStruct((ROWS + 2 * HALO, WIDE, 8, CH), F32),
            jax.ShapeDtypeStruct((TOK, CH), F32),
            jax.ShapeDtypeStruct((TOK, CH), BF),
        ],
        scratch_shapes=[pltpu.VMEM((KSIZE * KSIZE, 8, CH), F32)] + EDGE_SCRATCH,
        compiler_params=VMEM,
    )(emb, *halo, conv_kernel, gain)


CHUNK = 512
SCALE = 128**-0.5
COST = pl.CostEstimate(flops=14_000_000_000, transcendentals=0, bytes_accessed=16_000_000)


def attend_kernel(normed, wk, wv, q, up, k_out, v_out, weighted, stats, s_sc):
    h = pl.program_id(0)
    w = jnp.concatenate([wk[...], wv[...]], axis=1)
    peak = None
    for c in range(TOK // CHUNK):
        rows = slice(c * CHUNK, (c + 1) * CHUNK)
        kv = dot(normed[rows, :], w).astype(BF)
        k_out[rows, :] = kv[:, :128]
        v_out[rows, :] = kv[:, 128:]
        s = dot(kv[:, :128], q[...], NT) * SCALE
        s_sc[rows, :] = s
        top = jnp.max(s, axis=0, keepdims=True)
        peak = top if peak is None else jnp.maximum(peak, top)
    total = jnp.zeros((1, 256), F32)
    acc = jnp.zeros((128, 256), F32)
    for c in range(TOK // CHUNK):
        rows = slice(c * CHUNK, (c + 1) * CHUNK)
        p = jnp.exp(s_sc[rows, :] - peak)
        total = total + jnp.sum(p, axis=0, keepdims=True)
        acc = acc + dot(v_out[rows, :], p.astype(BF), TN)
    weighted[0] = acc.T
    dots = jnp.sum(acc * up[...].astype(F32).T, axis=0, keepdims=True)
    stats[0, pl.ds(h, 1), :] = peak
    stats[1, pl.ds(h, 1), :] = total
    stats[2, pl.ds(h, 1), :] = dots


def whole(shape):
    return pl.BlockSpec(shape, lambda h: (0,) * len(shape))


def column(rows, width, first=0):
    return pl.BlockSpec((rows, width), lambda h: (0, h + first))


def attend(normed, kv_weight, latents, d_attended):
    return pl.pallas_call(
        attend_kernel,
        name="attend",
        grid=(HEADS,),
        in_specs=[
            whole((TOK, CH)),
            column(CH, 128),
            column(CH, 128, HEADS),
            column(256, 128),
            column(256, 128),
        ],
        out_specs=[
            column(TOK, 128),
            column(TOK, 128),
            pl.BlockSpec((1, 256, 128), lambda h: (h, 0, 0)),
            whole((3, HEADS, 256)),
        ],
        out_shape=[
            jax.ShapeDtypeStruct((TOK, 1024), BF),
            jax.ShapeDtypeStruct((TOK, 1024), BF),
            jax.ShapeDtypeStruct((HEADS, 256, 128), F32),
            jax.ShapeDtypeStruct((3, HEADS, 256), F32),
        ],
        scratch_shapes=[pltpu.VMEM((TOK, 256), F32)],
        compiler_params=VMEM,
    )(normed, kv_weight, kv_weight, latents, d_attended)


def head_grads(h, normed, k_in, v_in, wk, wv, q, up, lse, dots, grads, dn_sc, nt_sc):
    w = jnp.concatenate([wk[...], wv[...]], axis=1)
    level = lse[pl.ds(h, 1), :]
    row_dots = dots[pl.ds(h, 1), :]
    qg = jnp.zeros((128, 256), F32)
    wg = jnp.zeros((256, 256), F32)
    for c in range(TOK // CHUNK):
        rows = slice(c * CHUNK, (c + 1) * CHUNK)
        k = k_in[rows, :]
        p = jnp.exp(dot(k, q[...], NT) * SCALE - level)
        dp = dot(v_in[rows, :], up[...], NT)
        ds = (p * (dp - row_dots) * SCALE).astype(BF)
        qg = qg + dot(k, ds, TN)
        kg = dot(ds, q[...]).astype(BF)
        vg = dot(p.astype(BF), up[...]).astype(BF)
        d_proj = jnp.concatenate([kg, vg], axis=1)
        wg = wg + dot(nt_sc[:, rows], d_proj)
        dn_sc[rows, :] += dot(d_proj, w, NT)
    grads[0, 0] = qg.T
    grads[1, 0] = wg[:, :128]
    grads[2, 0] = wg[:, 128:]


def first_half_kernel(normed, k_in, v_in, wk, wv, q, up, lse, dots, grads, dn, nt):
    h = pl.program_id(0)

    @pl.when(h == 0)
    def _():
        nt[...] = normed[...].astype(F32).T.astype(BF)
        dn[...] = jnp.zeros_like(dn)

    head_grads(h, normed, k_in, v_in, wk, wv, q, up, lse, dots, grads, dn, nt)


def second_half_kernel(
    nt, k_in, v_in, wk, wv, q, up, lse, dots, dn_in, mixed, gain,
    grads, d_mixed, gain_grad, top, bot, left, right, dn_sc, l_sc, r_sc, c_sc,
):
    h = pl.program_id(0)

    @pl.when(h == 0)
    def _():
        dn_sc[...] = dn_in[...]

    head_grads(h + HEADS // 2, None, k_in, v_in, wk, wv, q, up, lse, dots, grads, dn_sc, nt)

    @pl.when(h == HEADS // 2 - 1)
    def _():
        def body(a, total):
            rows = pl.ds(pl.multiple_of(a * COLS, COLS), COLS)
            centred, inverse = norm_rows(mixed[rows, :])
            dn = dn_sc[rows, :]
            total = total + jnp.sum(dn * centred, axis=0, keepdims=True)
            g = dn * gain[...]
            mean = jnp.sum(g, axis=-1, keepdims=True) * (1.0 / CH)
            slope = jnp.sum(g * centred, axis=-1, keepdims=True) * (1.0 / CH)
            d_mixed[rows, :] = (inverse * (g - mean - centred * slope)).astype(BF)
            return total

        gain_grad[...] = lax.fori_loop(0, ROWS, body, jnp.zeros((1, CH), F32))
        write_edges(d_mixed, top, bot, left, right, l_sc, r_sc, c_sc)


HALF = HEADS // 2


def head_specs(first):
    return [
        column(TOK, 128, first),
        column(TOK, 128, first),
        column(CH, 128, first),
        column(CH, 128, HEADS + first),
        column(256, 128, first),
        column(256, 128, first),
        whole((HEADS, 256)),
        whole((HEADS, 256)),
    ]


GRADS_SPEC = pl.BlockSpec((3, 1, 256, 128), lambda h: (0, h, 0, 0))
GRADS = jax.ShapeDtypeStruct((3, HALF, 256, 128), F32)


def first_half(normed, k, v, kv_weight, latents, d_attended, lse, dots):
    return pl.pallas_call(
        first_half_kernel,
        name="first_half",
        grid=(HALF,),
        in_specs=[whole((TOK, CH))] + head_specs(0),
        out_specs=[GRADS_SPEC, whole((TOK, CH)), whole((CH, TOK))],
        out_shape=[
            GRADS,
            jax.ShapeDtypeStruct((TOK, CH), F32),
            jax.ShapeDtypeStruct((CH, TOK), BF),
        ],
        compiler_params=VMEM,
        cost_estimate=COST,
    )(normed, k, v, kv_weight, kv_weight, latents, d_attended, lse, dots)


def second_half(nt, k, v, kv_weight, latents, d_attended, lse, dots, dn, mixed, gain):
    outs = pl.pallas_call(
        second_half_kernel,
        name="second_half",
        grid=(HALF,),
        in_specs=[whole((CH, TOK))]
        + head_specs(HALF)
        + [whole((TOK, CH)), whole((TOK, CH)), whole((1, CH))],
        out_specs=[GRADS_SPEC, whole((TOK, CH)), whole((1, CH))]
        + [whole(s.shape) for s in EDGE_SHAPES],
        out_shape=[
            GRADS,
            jax.ShapeDtypeStruct((TOK, CH), BF),
            jax.ShapeDtypeStruct((1, CH), F32),
        ]
        + EDGE_SHAPES,
        scratch_shapes=[pltpu.VMEM((TOK, CH), F32)] + EDGE_SCRATCH,
        compiler_params=VMEM,
        cost_estimate=COST,
    )(nt, k, v, kv_weight, kv_weight, latents, d_attended, lse, dots, dn, mixed, gain)
    return outs[:3], outs[3:]


def kernel_grad_body(wide, d_mixed, out, d_sc):
    d_sc[...] = d_mixed[...].astype(F32)
    for half in range(2):
        lanes = pl.ds(half * 128, 128)
        for i in range(KSIZE):

            def body(a, acc):
                xs = [wide[a + i, c, :, lanes] for c in range(WIDE)]
                base = pl.multiple_of(a * COLS, COLS)
                ds = [d_sc[pl.ds(base + cb * 8, 8), lanes] for cb in range(8)]
                acc = list(acc)
                for cb in range(8):
                    for j in range(KSIZE):
                        acc[j] = acc[j] + xs[cb + j] * ds[cb]
                return tuple(acc)

            zero = jnp.zeros((8, 128), F32)
            acc = lax.fori_loop(0, ROWS, body, (zero,) * KSIZE)
            for j in range(KSIZE):
                n = i * KSIZE + j
                out[n : n + 1, lanes] = jnp.sum(acc[j], axis=0, keepdims=True)


def kernel_grad(wide, d_mixed):
    return pl.pallas_call(
        kernel_grad_body,
        name="kernel_grad",
        out_shape=jax.ShapeDtypeStruct((KSIZE * KSIZE, CH), F32),
        scratch_shapes=[pltpu.VMEM((TOK, CH), F32)],
        compiler_params=VMEM,
        cost_estimate=COST,
    )(wide, d_mixed)


def conv_back_body(d_mixed, above, below, lh, rh, kern, z, patch_grad, bias_grad, wide, d_sc, w_sc, l_sc, r_sc, c_sc):
    assemble(wide, d_mixed, (above, below, lh, rh), l_sc, r_sc, c_sc)
    spread_weights(kern, w_sc)
    zero = jnp.zeros((8, 128), F32)

    def body(a, bias):
        bias = list(bias)
        for half in range(2):
            acc = conv_row(wide, w_sc, a, half, True)
            acc = jnp.concatenate(acc, axis=0).astype(BF)
            d_sc[a & 7, pl.ds(pl.multiple_of((a >> 3) * 64, 64), 64), pl.ds(half * 128, 128)] = acc
            bias[half] = bias[half] + jnp.sum(acc.astype(F32).reshape(8, 8, 128), axis=0)
        return tuple(bias)

    bias = lax.fori_loop(0, ROWS, body, (zero, zero))
    for half in range(2):
        bias_grad[:, half * 128 : (half + 1) * 128] = jnp.sum(bias[half], axis=0, keepdims=True)
    total = [jnp.zeros((16, CH), F32) for _ in range(4)]
    for a8 in range(8):
        part = dot(z[...], d_sc[a8], TN)
        for v in range(4):
            first = v * 128 + a8 * 16
            total[v] = total[v] + part[first : first + 16, :]
    for v in range(4):
        patch_grad[v] = total[v]


def conv_back(d_mixed, halo, conv_kernel, z):
    return pl.pallas_call(
        conv_back_body,
        name="conv_back",
        out_shape=[jax.ShapeDtypeStruct((4, 16, CH), F32), jax.ShapeDtypeStruct((1, CH), F32)],
        scratch_shapes=[
            pltpu.VMEM((ROWS + 2 * HALO, WIDE, 8, CH), F32),
            pltpu.VMEM((8, 256, CH), BF),
            pltpu.VMEM((KSIZE * KSIZE, 8, CH), F32),
        ]
        + EDGE_SCRATCH,
        compiler_params=VMEM,
        cost_estimate=COST,
    )(d_mixed, *halo, conv_kernel, z)


CHIPS = ("z", "x", "y")
PAIR = [(0, 1), (1, 0)]


def gather(x, axes):
    n = lax.axis_size(axes)
    copies = jnp.broadcast_to(x[None], (n,) + x.shape)
    return lax.all_to_all(copies, axes, 0, 0, tiled=True)


def combine_stats(stats):
    for axes in (("z", "core"), ("x", "y")):
        group = gather(stats, axes)
        peak = jnp.max(group[:, 0], axis=0)
        factors = jnp.exp(group[:, 0] - peak)
        total = jnp.sum(group[:, 1] * factors, axis=0)
        dots = jnp.sum(group[:, 2] * factors, axis=0)
        stats = jnp.stack([peak, total, dots])
    return stats


def pair_sum(x):
    core = lax.axis_index("core")
    keep = lax.dynamic_index_in_dim(x, core, 0, keepdims=False)
    send = lax.dynamic_index_in_dim(x, 1 - core, 0, keepdims=False)
    return (keep + lax.ppermute(send, "core", PAIR)).astype(WIRE)


def swap(half):
    other = lax.ppermute(half, "core", PAIR)
    first = lax.axis_index("core") == 0
    return jnp.stack([jnp.where(first, half, other), jnp.where(first, other, half)]).astype(F32)


def block_sum(parts):
    return jnp.sum(parts.astype(F32), axis=0)


def copies(x):
    return jnp.broadcast_to(x.astype(WIRE)[None], (64,) + x.shape)


def send(x):
    return lax.all_to_all(x, CHIPS, 0, 0, tiled=True)


def small_sum(x):
    x = x + lax.ppermute(x, "core", PAIR)
    x = jnp.sum(gather(x, ("z",)), axis=0)
    return jnp.sum(gather(x, ("x", "y")), axis=0)


def blocks(x):
    return x.reshape(2, 64, -1, x.shape[-1])


def tie(x, *others):
    return lax.optimization_barrier((x,) + others)


def columns(x):
    return x.transpose(1, 0, 2).reshape(256, -1)


def per_device(
    pixels, patch_weight, patch_bias, conv_kernel, norm_gain, kv_weight, latents, d_attended
):
    gain = norm_gain.reshape(1, CH)
    emb, z, edges = embed(pixels, patch_weight, patch_bias)
    rows = exchange_rows(edges)
    halo = rows + exchange_cols(edges, *rows)
    wide, mixed, normed = conv_forward(emb, halo, conv_kernel, gain)
    k, v, weighted, local = attend(normed, kv_weight, latents, d_attended)
    stats = combine_stats(local)
    lse = stats[0] + jnp.log(stats[1])
    row_dots = stats[2] / stats[1]
    factor = jnp.exp(local[0] - stats[0]) / stats[1]
    attended = pair_sum(blocks((weighted * factor[:, :, None]).reshape(2048, 128)))
    lse, attended = tie(lse, attended)
    attended = send(attended)
    grads_a, dn, nt = first_half(normed, k, v, kv_weight, latents, d_attended, lse, row_dots)
    dn, nt, grads_a, attended = tie(dn, nt, grads_a, attended)
    sums_a = pair_sum(blocks(grads_a.reshape(3072, 128)))
    message = jnp.concatenate([sums_a, copies(block_sum(attended))], axis=1)
    dn, message = tie(dn, message)
    message = send(message)
    (grads_b, d_mixed, gain_grad), d_edges = second_half(
        nt, k, v, kv_weight, latents, d_attended, lse, row_dots, dn, mixed, gain
    )
    grads_b, d_mixed, message, *d_edges = tie(grads_b, d_mixed, message, *d_edges)
    attended = message[:, 24:]
    d_rows = exchange_rows(d_edges)
    sums_b = pair_sum(blocks(grads_b.reshape(3072, 128)))
    message = jnp.concatenate([sums_b, copies(block_sum(message[:, :24]))], axis=1)
    d_mixed, message, *d_rows = tie(d_mixed, message, *d_rows)
    message = send(message)
    d_cols = exchange_cols(d_edges, *d_rows)
    kern = kernel_grad(wide, d_mixed)
    d_mixed, message, kern, *d_cols = tie(d_mixed, message, kern, *d_cols)
    grads_a = message[:, 24:]
    grads_b = copies(block_sum(message[:, :24]))
    d_mixed, grads_b = tie(d_mixed, grads_b)
    grads_b = send(grads_b)
    patch, bias = conv_back(d_mixed, tuple(d_rows) + tuple(d_cols), conv_kernel, z)
    patch, bias, grads_b = tie(patch, bias, grads_b)
    small = jnp.concatenate([patch.reshape(64, CH), kern, gain_grad, bias], axis=0)
    small = small_sum(jnp.pad(small, ((0, 5), (0, 0))))
    attended = swap(attended)
    grads = [
        jnp.concatenate([a, b], axis=0)
        for a, b in zip(
            swap(grads_a).reshape(3, HALF, 256, 128), swap(grads_b).reshape(3, HALF, 256, 128)
        )
    ]
    patch = small[:64].reshape(4, 16, CH)[:, :12].transpose(1, 0, 2).reshape(48, CH)
    return (
        columns(attended.reshape(HEADS, 256, 128)),
        columns(grads[0]),
        columns(jnp.concatenate([grads[1], grads[2]], axis=0)),
        small[64 + 49],
        small[64 : 64 + 49],
        patch,
        small[64 + 50],
    )


def solution(mesh):
    split = Mesh(mesh.devices.reshape(4, 2, 4, 4), ("z", "core", "x", "y"))
    return jax.shard_map(
        per_device,
        mesh=split,
        in_specs=(P(None, ("z", "core"), ("x", "y")), P(), P(), P(), P(), P(), P(), P()),
        out_specs=(P(), P(), P(), P(), P(), P(), P()),
        check_vma=False,
    )
```

```python
import jax
import jax.numpy as jnp
from jax import lax
from jax.experimental import pallas as pl
from jax.experimental.pallas import tpu as pltpu
from jax.sharding import Mesh
from jax.sharding import PartitionSpec as P

PATCH = 4
KSIZE = 7
HEADS = 8
HALO = 3
norm_eps = 1e-05
BF = jnp.bfloat16
F32 = jnp.float32
NT = (((1,), (1,)), ((), ()))
TN = (((0,), (0,)), ((), ()))
NN = (((1,), (0,)), ((), ()))
ROWS = 32
COLS = 64
CH = 256
TOK = ROWS * COLS
WIDE = 14
BLOCK = 256
WIRE = BF
ROW_AXES = ("z", "core")
COL_AXES = ("x", "y")
VMEM = pltpu.CompilerParams(vmem_limit_bytes=58 << 20)


def dot(a, b, dims=NN):
    return lax.dot_general(a, b, dims, preferred_element_type=F32)


def iota(shape, dim):
    return lax.broadcasted_iota(jnp.int32, shape, dim)


def write_edges(src, top, bot, left, right, l_sc, r_sc, c_sc):
    for a in range(ROWS):
        low = src[a * COLS : a * COLS + 32, :].astype(F32)
        high = src[a * COLS + 32 : a * COLS + 64, :].astype(F32)
        for k in range(HALO):
            l_sc[k * ROWS + a : k * ROWS + a + 1, :] = low[8 * k : 8 * k + 1, :]
            r_sc[k * ROWS + a : k * ROWS + a + 1, :] = high[8 * k + 15 : 8 * k + 16, :]
    left[...] = l_sc[...].astype(BF)
    right[...] = r_sc[...].astype(BF)
    c_sc[...] = jnp.zeros_like(c_sc)
    for k in range(HALO):
        for i in range(HALO):
            first = k * ROWS + i
            last = k * ROWS + ROWS - HALO + i
            row = k * HALO + i
            c_sc[0, row : row + 1, :] = l_sc[first : first + 1, :]
            c_sc[1, row : row + 1, :] = r_sc[first : first + 1, :]
            c_sc[2, row : row + 1, :] = l_sc[last : last + 1, :]
            c_sc[3, row : row + 1, :] = r_sc[last : last + 1, :]
    side = HALO * COLS
    top[:side, :] = src[0:side, :]
    bot[:side, :] = src[TOK - side : TOK, :]
    for n, ref in enumerate((top, bot)):
        ref[side : side + 16, :] = c_sc[2 * n].astype(BF)
        ref[side + 16 : side + 32, :] = c_sc[2 * n + 1].astype(BF)


EDGE_SHAPES = [
    jax.ShapeDtypeStruct((HALO * COLS + 32, CH), BF),
    jax.ShapeDtypeStruct((HALO * COLS + 32, CH), BF),
    jax.ShapeDtypeStruct((HALO * ROWS, CH), BF),
    jax.ShapeDtypeStruct((HALO * ROWS, CH), BF),
]
EDGE_SCRATCH = [
    pltpu.VMEM((HALO * ROWS, CH), F32),
    pltpu.VMEM((HALO * ROWS, CH), F32),
    pltpu.VMEM((4, 16, CH), F32),
]


def exchange_rows(edges):
    top, bot = edges[:2]
    n = lax.axis_size(ROW_AXES)
    above = lax.ppermute(bot, ROW_AXES, [(i, i + 1) for i in range(n - 1)])
    below = lax.ppermute(top, ROW_AXES, [(i + 1, i) for i in range(n - 1)])
    return above, below


def exchange_cols(edges, above, below):
    left, right = edges[2:]
    n = lax.axis_size(COL_AXES)
    side = HALO * COLS
    right = jnp.concatenate([right, above[side + 16 : side + 32], below[side + 16 : side + 32]])
    left = jnp.concatenate([left, above[side : side + 16], below[side : side + 16]])
    from_left = lax.ppermute(right, COL_AXES, [(i, i + 1) for i in range(n - 1)])
    from_right = lax.ppermute(left, COL_AXES, [(i + 1, i) for i in range(n - 1)])
    return from_left, from_right


def assemble(wide, own, halo, l_sc, r_sc, c_sc):
    above, below, left, right = halo
    edge = HALO * ROWS
    l_sc[...] = left[:edge, :].astype(F32)
    r_sc[...] = right[:edge, :].astype(F32)
    for n in range(2):
        c_sc[2 * n] = left[edge + 16 * n : edge + 16 * (n + 1), :].astype(F32)
        c_sc[2 * n + 1] = right[edge + 16 * n : edge + 16 * (n + 1), :].astype(F32)
    sub = iota((8, CH), 0)

    def put(row, x, lefts, rights):
        x = x.astype(F32).reshape(8, 8, CH)
        for cb in range(8):
            wide[row, HALO + cb] = x[cb]
        for k in range(HALO):
            wide[row, k] = jnp.where(sub == 0, lefts[k], pltpu.roll(x[5 + k], 1, 0))
            wide[row, 11 + k] = jnp.where(sub == 7, rights[k], pltpu.roll(x[k], 7, 0))

    for i in range(HALO):
        row = [k * HALO + i for k in range(HALO)]
        put(
            i,
            above[i * COLS : (i + 1) * COLS, :],
            [c_sc[0, n : n + 1, :] for n in row],
            [c_sc[1, n : n + 1, :] for n in row],
        )
        put(
            HALO + ROWS + i,
            below[i * COLS : (i + 1) * COLS, :],
            [c_sc[2, n : n + 1, :] for n in row],
            [c_sc[3, n : n + 1, :] for n in row],
        )

    def body(a, carry):
        put(
            a + HALO,
            own[pl.ds(pl.multiple_of(a * COLS, COLS), COLS), :],
            [l_sc[pl.ds(k * ROWS + a, 1), :] for k in range(HALO)],
            [r_sc[pl.ds(k * ROWS + a, 1), :] for k in range(HALO)],
        )
        return carry

    lax.fori_loop(0, ROWS, body, 0)


def spread_weights(kernel_ref, w_sc):
    for n in range(KSIZE * KSIZE):
        w_sc[n] = jnp.broadcast_to(kernel_ref[n : n + 1, :], (8, CH))


def conv_rows(wide, w_sc, a, half, flip):
    lanes = pl.ds(half * 128, 128)
    acc = [[wide[a + r + HALO, HALO + cb, :, lanes] for cb in range(8)] for r in range(2)]
    for i in range(KSIZE + 1):
        xs = [wide[a + i, c, :, lanes] for c in range(WIDE)]
        for r in range(2):
            if not 0 <= i - r < KSIZE:
                continue
            for j in range(KSIZE):
                n = (i - r) * KSIZE + j
                w = w_sc[KSIZE * KSIZE - 1 - n if flip else n, :, lanes]
                acc[r] = [acc[r][cb] + xs[cb + j] * w for cb in range(8)]
    return acc


def norm_rows(x):
    centre = x - jnp.sum(x, axis=-1, keepdims=True) * (1.0 / CH)
    variance = jnp.sum(centre * centre, axis=-1, keepdims=True) * (1.0 / CH)
    inverse = lax.rsqrt(variance + norm_eps)
    return centre * inverse, inverse


def embed_kernel(pixels, weights, bias, emb, z_ref, top, bot, left, right, w_sc, l_sc, r_sc, c_sc):
    out = iota((256, 256), 0)
    spread = (((out & 7) * 8 + ((out >> 3) & 7)) * 4 + (out >> 6)) == iota((256, 256), 1)
    spread = jnp.where(spread, 1.0, 0.0).astype(BF)
    by_cell = dot(spread, pixels[...], NT).astype(BF)
    row = iota((512, 384), 0)
    fu = row & 15
    target = (fu >> 2) * 128 + (row >> 4) * 4 + (fu & 3)
    order = jnp.where((target == iota((512, 384), 1)) & (fu < 12), 1.0, 0.0).astype(BF)
    z = dot(by_cell, order, NT).astype(BF)
    for g in range(4):
        for v in range(4):
            z_ref[g * 64 : (g + 1) * 64, v * 128 : (v + 1) * 128] = z[
                v * 64 : (v + 1) * 64, g * 128 : (g + 1) * 128
            ]
    w_sc[...] = jnp.zeros_like(w_sc)
    for v in range(4):
        for a8 in range(8):
            first = v * 128 + a8 * 16
            w_sc[first : first + 16, a8 * CH : (a8 + 1) * CH] = weights[v]
    for a8 in range(8):
        block = dot(z_ref[...], w_sc[:, a8 * CH : (a8 + 1) * CH]) + bias[...]
        block = block.astype(BF)
        for g in range(4):
            a = g * 8 + a8
            emb[a * COLS : (a + 1) * COLS, :] = block[g * 64 : (g + 1) * 64, :]
    write_edges(emb, top, bot, left, right, l_sc, r_sc, c_sc)


def embed(pixels, patch_weight, patch_bias):
    weights = patch_weight.reshape(12, 4, CH).transpose(1, 0, 2)
    weights = jnp.pad(weights, ((0, 0), (0, 4), (0, 0)))
    outs = pl.pallas_call(
        embed_kernel,
        name="embed",
        out_shape=[
            jax.ShapeDtypeStruct((TOK, CH), BF),
            jax.ShapeDtypeStruct((256, 512), BF),
        ]
        + EDGE_SHAPES,
        scratch_shapes=[pltpu.VMEM((512, 2048), BF)] + EDGE_SCRATCH,
        compiler_params=VMEM,
    )(pixels.reshape(384, 256), weights, patch_bias.reshape(1, CH))
    return outs[0], outs[1], outs[2:]


def conv_kernel_body(emb, above, below, lh, rh, kern, gain, wide, centred, inverse, normed, w_sc, l_sc, r_sc, c_sc):
    assemble(wide, emb, (above, below, lh, rh), l_sc, r_sc, c_sc)
    spread_weights(kern, w_sc)

    def body(n, carry):
        for half in range(2):
            acc = conv_rows(wide, w_sc, 2 * n, half, False)
            for r in range(2):
                for cb in range(8):
                    rows = pl.ds(pl.multiple_of((2 * n + r) * COLS + cb * 8, 8), 8)
                    centred[rows, pl.ds(half * 128, 128)] = acc[r][cb]
        return carry

    lax.fori_loop(0, ROWS // 2, body, 0)

    def norm_body(n, carry):
        rows = pl.ds(pl.multiple_of(n * BLOCK, BLOCK), BLOCK)
        out, inv = norm_rows(centred[rows, :])
        centred[rows, :] = out
        inverse[rows, :] = jnp.broadcast_to(inv, (BLOCK, 128))
        normed[rows, :] = (out * gain[...]).astype(BF)
        return carry

    lax.fori_loop(0, TOK // BLOCK, norm_body, 0)


def conv_forward(emb, halo, conv_kernel, gain):
    return pl.pallas_call(
        conv_kernel_body,
        name="conv_forward",
        out_shape=[
            jax.ShapeDtypeStruct((ROWS + 2 * HALO, WIDE, 8, CH), F32),
            jax.ShapeDtypeStruct((TOK, CH), F32),
            jax.ShapeDtypeStruct((TOK, 128), F32),
            jax.ShapeDtypeStruct((TOK, CH), BF),
        ],
        scratch_shapes=[pltpu.VMEM((KSIZE * KSIZE, 8, CH), F32)] + EDGE_SCRATCH,
        compiler_params=VMEM,
    )(emb, *halo, conv_kernel, gain)


CHUNK = 512
SCALE = 128**-0.5
SCALE2 = SCALE * 1.4426950408889634
COST = pl.CostEstimate(flops=14_000_000_000, transcendentals=0, bytes_accessed=16_000_000)


def attend_kernel(normed, wk, wv, q, up, k_out, v_out, weighted, stats, s_sc):
    h = pl.program_id(0)
    w = jnp.concatenate([wk[...], wv[...]], axis=1)
    peak = None
    for c in range(TOK // CHUNK):
        rows = slice(c * CHUNK, (c + 1) * CHUNK)
        kv = dot(normed[rows, :], w).astype(BF)
        k_out[rows, :] = kv[:, :128]
        v_out[rows, :] = kv[:, 128:]
        s = dot(kv[:, :128], q[...], NT)
        s_sc[rows, :] = s
        top = jnp.max(s, axis=0, keepdims=True)
        peak = top if peak is None else jnp.maximum(peak, top)
    level = peak * SCALE2
    total = jnp.zeros((1, 256), F32)
    acc = jnp.zeros((128, 256), F32)
    for c in range(TOK // CHUNK):
        rows = slice(c * CHUNK, (c + 1) * CHUNK)
        p = jnp.exp2(s_sc[rows, :] * SCALE2 - level)
        total = total + jnp.sum(p, axis=0, keepdims=True)
        acc = acc + dot(v_out[rows, :], p.astype(BF), TN)
    weighted[0] = acc.T
    dots = jnp.sum(acc * up[...].astype(F32).T, axis=0, keepdims=True)
    stats[0, pl.ds(h, 1), :] = level
    stats[1, pl.ds(h, 1), :] = total
    stats[2, pl.ds(h, 1), :] = dots


def whole(shape):
    return pl.BlockSpec(shape, lambda h: (0,) * len(shape))


def column(rows, width, first=0):
    return pl.BlockSpec((rows, width), lambda h: (0, h + first))


def attend(normed, kv_weight, latents, d_attended):
    return pl.pallas_call(
        attend_kernel,
        name="attend",
        grid=(HEADS,),
        in_specs=[
            whole((TOK, CH)),
            column(CH, 128),
            column(CH, 128, HEADS),
            column(256, 128),
            column(256, 128),
        ],
        out_specs=[
            column(TOK, 128),
            column(TOK, 128),
            pl.BlockSpec((1, 256, 128), lambda h: (h, 0, 0)),
            whole((3, HEADS, 256)),
        ],
        out_shape=[
            jax.ShapeDtypeStruct((TOK, 1024), BF),
            jax.ShapeDtypeStruct((TOK, 1024), BF),
            jax.ShapeDtypeStruct((HEADS, 256, 128), F32),
            jax.ShapeDtypeStruct((3, HEADS, 256), F32),
        ],
        scratch_shapes=[pltpu.VMEM((TOK, 256), F32)],
        compiler_params=VMEM,
    )(normed, kv_weight, kv_weight, latents, d_attended)


def attend_grad_kernel(
    normed, k_in, v_in, wk, wv, q, up, lse, dots, centred, inverse, gain,
    grads, d_mixed, gain_grad, top, bot, left, right, dn_sc, nt_sc, l_sc, r_sc, c_sc,
):
    h = pl.program_id(0)

    @pl.when(h == 0)
    def _():
        nt_sc[...] = normed[...].T
        dn_sc[...] = jnp.zeros_like(dn_sc)

    w = jnp.concatenate([wk[...], wv[...]], axis=1)
    level = lse[pl.ds(h, 1), :]
    row_dots = dots[pl.ds(h, 1), :]
    qg = jnp.zeros((128, 256), F32)
    wg = jnp.zeros((256, 256), F32)
    for c in range(TOK // CHUNK):
        rows = slice(c * CHUNK, (c + 1) * CHUNK)
        k = k_in[rows, :]
        p = jnp.exp2(dot(k, q[...], NT) * SCALE2 - level)
        dp = dot(v_in[rows, :], up[...], NT)
        ds = (p * (dp - row_dots)).astype(BF)
        qg = qg + dot(k, ds, TN)
        kg = (dot(ds, q[...]) * SCALE).astype(BF)
        vg = dot(p.astype(BF), up[...]).astype(BF)
        d_proj = jnp.concatenate([kg, vg], axis=1)
        wg = wg + dot(nt_sc[:, rows], d_proj)
        dn_sc[rows, :] += dot(d_proj, w, NT)
    grads[0, 0] = qg.T * SCALE
    grads[1, 0] = wg[:, :128]
    grads[2, 0] = wg[:, 128:]

    @pl.when(h == HEADS - 1)
    def _():
        def body(n, total):
            rows = pl.ds(pl.multiple_of(n * BLOCK, BLOCK), BLOCK)
            x = centred[rows, :]
            inv = inverse[rows, :]
            dn = dn_sc[rows, :]
            total = total + jnp.sum(dn * x, axis=0, keepdims=True)
            g = dn * gain[...]
            mean = jnp.sum(g, axis=-1, keepdims=True) * (1.0 / CH)
            slope = jnp.sum(g * x, axis=-1, keepdims=True) * (1.0 / CH)
            inv = jnp.concatenate([inv, inv], axis=1)
            d_mixed[rows, :] = (inv * (g - mean - x * slope)).astype(BF)
            return total

        gain_grad[...] = lax.fori_loop(0, TOK // BLOCK, body, jnp.zeros((1, CH), F32))
        write_edges(d_mixed, top, bot, left, right, l_sc, r_sc, c_sc)


def attend_grad(normed, k, v, kv_weight, latents, d_attended, lse, dots, centred, inverse, gain):
    outs = pl.pallas_call(
        attend_grad_kernel,
        name="attend_grad",
        grid=(HEADS,),
        in_specs=[
            whole((TOK, CH)),
            column(TOK, 128),
            column(TOK, 128),
            column(CH, 128),
            column(CH, 128, HEADS),
            column(256, 128),
            column(256, 128),
            whole((HEADS, 256)),
            whole((HEADS, 256)),
            whole((TOK, CH)),
            whole((TOK, 128)),
            whole((1, CH)),
        ],
        out_specs=[
            pl.BlockSpec((3, 1, 256, 128), lambda h: (0, h, 0, 0)),
            whole((TOK, CH)),
            whole((1, CH)),
        ]
        + [whole(s.shape) for s in EDGE_SHAPES],
        out_shape=[
            jax.ShapeDtypeStruct((3, HEADS, 256, 128), F32),
            jax.ShapeDtypeStruct((TOK, CH), BF),
            jax.ShapeDtypeStruct((1, CH), F32),
        ]
        + EDGE_SHAPES,
        scratch_shapes=[pltpu.VMEM((TOK, CH), F32), pltpu.VMEM((CH, TOK), BF)] + EDGE_SCRATCH,
        compiler_params=VMEM,
        cost_estimate=COST,
    )(normed, k, v, kv_weight, kv_weight, latents, d_attended, lse, dots, centred, inverse, gain)
    return outs[:3], outs[3:]


def kernel_grad_body(wide, d_mixed, out, d_sc):
    d_sc[...] = d_mixed[...].astype(F32)
    for half in range(2):
        lanes = pl.ds(half * 128, 128)
        for i in range(KSIZE):

            def body(n, acc):
                acc = list(acc)
                for r in range(4):
                    a = 4 * n + r
                    xs = [wide[a + i, c, :, lanes] for c in range(WIDE)]
                    base = pl.multiple_of(a * COLS, COLS)
                    ds = [d_sc[pl.ds(base + cb * 8, 8), lanes] for cb in range(8)]
                    for cb in range(8):
                        for j in range(KSIZE):
                            acc[j] = acc[j] + xs[cb + j] * ds[cb]
                return tuple(acc)

            zero = jnp.zeros((8, 128), F32)
            acc = lax.fori_loop(0, ROWS // 4, body, (zero,) * KSIZE)
            for j in range(KSIZE):
                n = i * KSIZE + j
                out[n : n + 1, lanes] = jnp.sum(acc[j], axis=0, keepdims=True)


def kernel_grad(wide, d_mixed):
    return pl.pallas_call(
        kernel_grad_body,
        name="kernel_grad",
        out_shape=jax.ShapeDtypeStruct((KSIZE * KSIZE, CH), F32),
        scratch_shapes=[pltpu.VMEM((TOK, CH), F32)],
        compiler_params=VMEM,
        cost_estimate=COST,
    )(wide, d_mixed)


def conv_back_body(d_mixed, above, below, lh, rh, kern, z, patch_grad, bias_grad, wide, d_sc, w_sc, l_sc, r_sc, c_sc):
    assemble(wide, d_mixed, (above, below, lh, rh), l_sc, r_sc, c_sc)
    spread_weights(kern, w_sc)
    zero = jnp.zeros((8, 128), F32)

    def body(n, bias):
        bias = list(bias)
        for half in range(2):
            accs = conv_rows(wide, w_sc, 2 * n, half, True)
            for r in range(2):
                a = 2 * n + r
                acc = jnp.concatenate(accs[r], axis=0).astype(BF)
                d_sc[a & 7, pl.ds(pl.multiple_of((a >> 3) * 64, 64), 64), pl.ds(half * 128, 128)] = acc
                bias[half] = bias[half] + jnp.sum(acc.astype(F32).reshape(8, 8, 128), axis=0)
        return tuple(bias)

    bias = lax.fori_loop(0, ROWS // 2, body, (zero, zero))
    for half in range(2):
        bias_grad[:, half * 128 : (half + 1) * 128] = jnp.sum(bias[half], axis=0, keepdims=True)
    total = [jnp.zeros((16, CH), F32) for _ in range(4)]
    for a8 in range(8):
        part = dot(z[...], d_sc[a8], TN)
        for v in range(4):
            first = v * 128 + a8 * 16
            total[v] = total[v] + part[first : first + 16, :]
    for v in range(4):
        patch_grad[v] = total[v]


def conv_back(d_mixed, halo, conv_kernel, z):
    return pl.pallas_call(
        conv_back_body,
        name="conv_back",
        out_shape=[jax.ShapeDtypeStruct((4, 16, CH), F32), jax.ShapeDtypeStruct((1, CH), F32)],
        scratch_shapes=[
            pltpu.VMEM((ROWS + 2 * HALO, WIDE, 8, CH), F32),
            pltpu.VMEM((8, 256, CH), BF),
            pltpu.VMEM((KSIZE * KSIZE, 8, CH), F32),
        ]
        + EDGE_SCRATCH,
        compiler_params=VMEM,
        cost_estimate=COST,
    )(d_mixed, *halo, conv_kernel, z)


CHIPS = ("z", "x", "y")
ALL = ("z", "core", "x", "y")
PAIR = [(0, 1), (1, 0)]


def gather(x, axes):
    n = lax.axis_size(axes)
    copies = jnp.broadcast_to(x[None], (n,) + x.shape)
    return lax.all_to_all(copies, axes, 0, 0, tiled=True)


def combine_stats(stats):
    for axes in (("z", "core"), ("x", "y")):
        group = gather(stats, axes)
        peak = jnp.max(group[:, 0], axis=0)
        factors = jnp.exp2(group[:, 0] - peak)
        total = jnp.sum(group[:, 1] * factors, axis=0)
        dots = jnp.sum(group[:, 2] * factors, axis=0)
        stats = jnp.stack([peak, total, dots])
    return stats


def pair_sum(x):
    core = lax.axis_index("core")
    keep = lax.dynamic_index_in_dim(x, core, 0, keepdims=False)
    send = lax.dynamic_index_in_dim(x, 1 - core, 0, keepdims=False)
    return (keep + lax.ppermute(send, "core", PAIR)).astype(WIRE)


def swap(half):
    other = lax.ppermute(half, "core", PAIR)
    first = lax.axis_index("core") == 0
    return jnp.stack([jnp.where(first, half, other), jnp.where(first, other, half)]).astype(F32)


def block_sum(parts):
    return jnp.sum(parts.astype(F32), axis=0)


def copies(x):
    return jnp.broadcast_to(x.astype(WIRE)[None], (64,) + x.shape)


def send(x):
    return lax.all_to_all(x, CHIPS, 0, 0, tiled=True)


def small_sum(x):
    mine = jnp.sum(lax.all_to_all(x[:, None], ALL, 0, 0, tiled=True), axis=0)
    return lax.all_to_all(jnp.broadcast_to(mine[None], (128,) + mine.shape), ALL, 0, 0, tiled=True)[:, 0]


def blocks(x):
    return x.reshape(2, 64, -1, x.shape[-1])


def tie(x, *others):
    return lax.optimization_barrier((x,) + others)


def columns(x):
    return x.transpose(1, 0, 2).reshape(256, -1)


def per_device(
    pixels, patch_weight, patch_bias, conv_kernel, norm_gain, kv_weight, latents, d_attended
):
    gain = norm_gain.reshape(1, CH)
    emb, z, edges = embed(pixels, patch_weight, patch_bias)
    rows = exchange_rows(edges)
    halo = rows + exchange_cols(edges, *rows)
    wide, centred, inverse, normed = conv_forward(emb, halo, conv_kernel, gain)
    k, v, weighted, local = attend(normed, kv_weight, latents, d_attended)
    stats = combine_stats(local)
    lse = stats[0] + jnp.log2(stats[1])
    row_dots = stats[2] / stats[1]
    factor = jnp.exp2(local[0] - stats[0]) / stats[1]
    (grads, d_mixed, gain_grad), d_edges = attend_grad(
        normed, k, v, kv_weight, latents, d_attended, lse, row_dots, centred, inverse, gain
    )
    d_rows = exchange_rows(d_edges)
    sums = jnp.concatenate([(weighted * factor[:, :, None])[None], grads], axis=0)
    message = pair_sum(blocks(sums.reshape(8192, 128)))
    d_mixed, message, *d_rows = tie(d_mixed, message, *d_rows)
    message = send(message)
    d_cols = exchange_cols(d_edges, *d_rows)
    kern = kernel_grad(wide, d_mixed)
    d_mixed, message, kern, *d_cols = tie(d_mixed, message, kern, *d_cols)
    message = copies(block_sum(message))
    d_mixed, message = tie(d_mixed, message)
    message = send(message)
    patch, bias = conv_back(d_mixed, tuple(d_rows) + tuple(d_cols), conv_kernel, z)
    patch, bias, message = tie(patch, bias, message)
    small = jnp.concatenate([patch.reshape(64, CH), kern, gain_grad, bias], axis=0)
    small = small_sum(jnp.pad(small, ((0, 13), (0, 0))))
    sums = swap(message).reshape(4, HEADS, 256, 128)
    patch = small[:64].reshape(4, 16, CH)[:, :12].transpose(1, 0, 2).reshape(48, CH)
    return (
        columns(sums[0]),
        columns(sums[1]),
        columns(sums[2:].reshape(2 * HEADS, 256, 128)),
        small[64 + 49],
        small[64 : 64 + 49],
        patch,
        small[64 + 50],
    )


def solution(mesh):
    split = Mesh(mesh.devices.reshape(4, 2, 4, 4), ("z", "core", "x", "y"))
    return jax.shard_map(
        per_device,
        mesh=split,
        in_specs=(P(None, ("z", "core"), ("x", "y")), P(), P(), P(), P(), P(), P(), P()),
        out_specs=(P(), P(), P(), P(), P(), P(), P()),
        check_vma=False,
    )
```

```python
import jax
import jax.numpy as jnp
from jax import lax
from jax.experimental import pallas as pl
from jax.experimental.pallas import tpu as pltpu
from jax.sharding import Mesh
from jax.sharding import PartitionSpec as P

PATCH = 4
KSIZE = 7
HEADS = 8
HALO = 3
norm_eps = 1e-05
BF = jnp.bfloat16
F32 = jnp.float32
NT = (((1,), (1,)), ((), ()))
TN = (((0,), (0,)), ((), ()))
NN = (((1,), (0,)), ((), ()))
ROWS = 32
COLS = 64
CH = 256
TOK = ROWS * COLS
WIDE = 14
BLOCK = 256
WIRE = BF
ROW_AXES = ("z", "core")
COL_AXES = ("x", "y")
VMEM = pltpu.CompilerParams(vmem_limit_bytes=58 << 20)


def dot(a, b, dims=NN):
    return lax.dot_general(a, b, dims, preferred_element_type=F32)


def iota(shape, dim):
    return lax.broadcasted_iota(jnp.int32, shape, dim)


def write_edges(src, top, bot, left, right, l_sc, r_sc, c_sc):
    for a in range(ROWS):
        low = src[a * COLS : a * COLS + 32, :].astype(F32)
        high = src[a * COLS + 32 : a * COLS + 64, :].astype(F32)
        for k in range(HALO):
            l_sc[k * ROWS + a : k * ROWS + a + 1, :] = low[8 * k : 8 * k + 1, :]
            r_sc[k * ROWS + a : k * ROWS + a + 1, :] = high[8 * k + 15 : 8 * k + 16, :]
    left[...] = l_sc[...].astype(BF)
    right[...] = r_sc[...].astype(BF)
    c_sc[...] = jnp.zeros_like(c_sc)
    for k in range(HALO):
        for i in range(HALO):
            first = k * ROWS + i
            last = k * ROWS + ROWS - HALO + i
            row = k * HALO + i
            c_sc[0, row : row + 1, :] = l_sc[first : first + 1, :]
            c_sc[1, row : row + 1, :] = r_sc[first : first + 1, :]
            c_sc[2, row : row + 1, :] = l_sc[last : last + 1, :]
            c_sc[3, row : row + 1, :] = r_sc[last : last + 1, :]
    side = HALO * COLS
    top[:side, :] = src[0:side, :]
    bot[:side, :] = src[TOK - side : TOK, :]
    for n, ref in enumerate((top, bot)):
        ref[side : side + 16, :] = c_sc[2 * n].astype(BF)
        ref[side + 16 : side + 32, :] = c_sc[2 * n + 1].astype(BF)


EDGE_SHAPES = [
    jax.ShapeDtypeStruct((HALO * COLS + 32, CH), BF),
    jax.ShapeDtypeStruct((HALO * COLS + 32, CH), BF),
    jax.ShapeDtypeStruct((HALO * ROWS, CH), BF),
    jax.ShapeDtypeStruct((HALO * ROWS, CH), BF),
]
EDGE_SCRATCH = [
    pltpu.VMEM((HALO * ROWS, CH), F32),
    pltpu.VMEM((HALO * ROWS, CH), F32),
    pltpu.VMEM((4, 16, CH), F32),
]


def exchange_rows(edges):
    top, bot = edges[:2]
    n = lax.axis_size(ROW_AXES)
    above = lax.ppermute(bot, ROW_AXES, [(i, i + 1) for i in range(n - 1)])
    below = lax.ppermute(top, ROW_AXES, [(i + 1, i) for i in range(n - 1)])
    return above, below


def exchange_cols(edges, above, below):
    left, right = edges[2:]
    n = lax.axis_size(COL_AXES)
    side = HALO * COLS
    right = jnp.concatenate([right, above[side + 16 : side + 32], below[side + 16 : side + 32]])
    left = jnp.concatenate([left, above[side : side + 16], below[side : side + 16]])
    from_left = lax.ppermute(right, COL_AXES, [(i, i + 1) for i in range(n - 1)])
    from_right = lax.ppermute(left, COL_AXES, [(i + 1, i) for i in range(n - 1)])
    return from_left, from_right


def assemble(wide, own, halo, l_sc, r_sc, c_sc):
    above, below, left, right = halo
    edge = HALO * ROWS
    l_sc[...] = left[:edge, :].astype(F32)
    r_sc[...] = right[:edge, :].astype(F32)
    for n in range(2):
        c_sc[2 * n] = left[edge + 16 * n : edge + 16 * (n + 1), :].astype(F32)
        c_sc[2 * n + 1] = right[edge + 16 * n : edge + 16 * (n + 1), :].astype(F32)
    sub = iota((8, CH), 0)

    def put(row, x, lefts, rights):
        x = x.astype(F32).reshape(8, 8, CH)
        for cb in range(8):
            wide[row, HALO + cb] = x[cb]
        for k in range(HALO):
            wide[row, k] = jnp.where(sub == 0, lefts[k], pltpu.roll(x[5 + k], 1, 0))
            wide[row, 11 + k] = jnp.where(sub == 7, rights[k], pltpu.roll(x[k], 7, 0))

    for i in range(HALO):
        row = [k * HALO + i for k in range(HALO)]
        put(
            i,
            above[i * COLS : (i + 1) * COLS, :],
            [c_sc[0, n : n + 1, :] for n in row],
            [c_sc[1, n : n + 1, :] for n in row],
        )
        put(
            HALO + ROWS + i,
            below[i * COLS : (i + 1) * COLS, :],
            [c_sc[2, n : n + 1, :] for n in row],
            [c_sc[3, n : n + 1, :] for n in row],
        )

    def body(a, carry):
        put(
            a + HALO,
            own[pl.ds(pl.multiple_of(a * COLS, COLS), COLS), :],
            [l_sc[pl.ds(k * ROWS + a, 1), :] for k in range(HALO)],
            [r_sc[pl.ds(k * ROWS + a, 1), :] for k in range(HALO)],
        )
        return carry

    lax.fori_loop(0, ROWS, body, 0)


def spread_weights(kernel_ref, w_sc):
    for n in range(KSIZE * KSIZE):
        w_sc[n] = jnp.broadcast_to(kernel_ref[n : n + 1, :], (8, CH))


def conv_rows(wide, w_sc, a, half, flip):
    lanes = pl.ds(half * 128, 128)
    acc = [[wide[a + r + HALO, HALO + cb, :, lanes] for cb in range(8)] for r in range(2)]
    for i in range(KSIZE + 1):
        xs = [wide[a + i, c, :, lanes] for c in range(WIDE)]
        for r in range(2):
            if not 0 <= i - r < KSIZE:
                continue
            for j in range(KSIZE):
                n = (i - r) * KSIZE + j
                w = w_sc[KSIZE * KSIZE - 1 - n if flip else n, :, lanes]
                acc[r] = [acc[r][cb] + xs[cb + j] * w for cb in range(8)]
    return acc


def norm_rows(x):
    centre = x - jnp.sum(x, axis=-1, keepdims=True) * (1.0 / CH)
    variance = jnp.sum(centre * centre, axis=-1, keepdims=True) * (1.0 / CH)
    inverse = lax.rsqrt(variance + norm_eps)
    return centre * inverse, inverse


def embed_kernel(pixels, weights, bias, emb, z_ref, top, bot, left, right, w_sc, l_sc, r_sc, c_sc):
    out = iota((256, 256), 0)
    spread = (((out & 7) * 8 + ((out >> 3) & 7)) * 4 + (out >> 6)) == iota((256, 256), 1)
    spread = jnp.where(spread, 1.0, 0.0).astype(BF)
    by_cell = dot(spread, pixels[...], NT).astype(BF)
    row = iota((512, 384), 0)
    fu = row & 15
    target = (fu >> 2) * 128 + (row >> 4) * 4 + (fu & 3)
    order = jnp.where((target == iota((512, 384), 1)) & (fu < 12), 1.0, 0.0).astype(BF)
    z = dot(by_cell, order, NT).astype(BF)
    for g in range(4):
        for v in range(4):
            z_ref[g * 64 : (g + 1) * 64, v * 128 : (v + 1) * 128] = z[
                v * 64 : (v + 1) * 64, g * 128 : (g + 1) * 128
            ]
    w_sc[...] = jnp.zeros_like(w_sc)
    for v in range(4):
        for a8 in range(8):
            first = v * 128 + a8 * 16
            w_sc[first : first + 16, a8 * CH : (a8 + 1) * CH] = weights[v]
    for a8 in range(8):
        block = dot(z_ref[...], w_sc[:, a8 * CH : (a8 + 1) * CH]) + bias[...]
        block = block.astype(BF)
        for g in range(4):
            a = g * 8 + a8
            emb[a * COLS : (a + 1) * COLS, :] = block[g * 64 : (g + 1) * 64, :]
    write_edges(emb, top, bot, left, right, l_sc, r_sc, c_sc)


def embed(pixels, patch_weight, patch_bias):
    weights = patch_weight.reshape(12, 4, CH).transpose(1, 0, 2)
    weights = jnp.pad(weights, ((0, 0), (0, 4), (0, 0)))
    outs = pl.pallas_call(
        embed_kernel,
        name="embed",
        out_shape=[
            jax.ShapeDtypeStruct((TOK, CH), BF),
            jax.ShapeDtypeStruct((256, 512), BF),
        ]
        + EDGE_SHAPES,
        scratch_shapes=[pltpu.VMEM((512, 2048), BF)] + EDGE_SCRATCH,
        compiler_params=VMEM,
    )(pixels.reshape(384, 256), weights, patch_bias.reshape(1, CH))
    return outs[0], outs[1], outs[2:]


def conv_kernel_body(emb, above, below, lh, rh, kern, gain, wide, centred, inverse, normed, w_sc, l_sc, r_sc, c_sc):
    assemble(wide, emb, (above, below, lh, rh), l_sc, r_sc, c_sc)
    spread_weights(kern, w_sc)

    def body(n, carry):
        for half in range(2):
            acc = conv_rows(wide, w_sc, 2 * n, half, False)
            for r in range(2):
                for cb in range(8):
                    rows = pl.ds(pl.multiple_of((2 * n + r) * COLS + cb * 8, 8), 8)
                    centred[rows, pl.ds(half * 128, 128)] = acc[r][cb]
        return carry

    lax.fori_loop(0, ROWS // 2, body, 0)

    def norm_body(n, carry):
        rows = pl.ds(pl.multiple_of(n * BLOCK, BLOCK), BLOCK)
        out, inv = norm_rows(centred[rows, :])
        centred[rows, :] = out
        inverse[rows, :] = jnp.broadcast_to(inv, (BLOCK, 128))
        normed[rows, :] = (out * gain[...]).astype(BF)
        return carry

    lax.fori_loop(0, TOK // BLOCK, norm_body, 0)


def conv_forward(emb, halo, conv_kernel, gain):
    return pl.pallas_call(
        conv_kernel_body,
        name="conv_forward",
        out_shape=[
            jax.ShapeDtypeStruct((ROWS + 2 * HALO, WIDE, 8, CH), F32),
            jax.ShapeDtypeStruct((TOK, CH), F32),
            jax.ShapeDtypeStruct((TOK, 128), F32),
            jax.ShapeDtypeStruct((TOK, CH), BF),
        ],
        scratch_shapes=[pltpu.VMEM((KSIZE * KSIZE, 8, CH), F32)] + EDGE_SCRATCH,
        compiler_params=VMEM,
    )(emb, *halo, conv_kernel, gain)


CHUNK = 512
SCALE = 128**-0.5
SCALE2 = SCALE * 1.4426950408889634
COST = pl.CostEstimate(flops=14_000_000_000, transcendentals=0, bytes_accessed=16_000_000)


def attend_kernel(normed, wk, wv, q, up, k_out, v_out, weighted, stats, s_sc):
    h = pl.program_id(0)
    w = jnp.concatenate([wk[...], wv[...]], axis=1)
    peak = None
    for c in range(TOK // CHUNK):
        rows = slice(c * CHUNK, (c + 1) * CHUNK)
        kv = dot(normed[rows, :], w).astype(BF)
        k_out[rows, :] = kv[:, :128]
        v_out[rows, :] = kv[:, 128:]
        s = dot(kv[:, :128], q[...], NT)
        s_sc[rows, :] = s
        top = jnp.max(s, axis=0, keepdims=True)
        peak = top if peak is None else jnp.maximum(peak, top)
    level = peak * SCALE2
    total = jnp.zeros((1, 256), F32)
    acc = jnp.zeros((128, 256), F32)
    for c in range(TOK // CHUNK):
        rows = slice(c * CHUNK, (c + 1) * CHUNK)
        p = jnp.exp2(s_sc[rows, :] * SCALE2 - level)
        total = total + jnp.sum(p, axis=0, keepdims=True)
        acc = acc + dot(v_out[rows, :], p.astype(BF), TN)
    weighted[0] = acc
    dots = jnp.sum(acc * up[...].astype(F32).T, axis=0, keepdims=True)
    stats[0, pl.ds(h, 1), :] = level
    stats[1, pl.ds(h, 1), :] = total
    stats[2, pl.ds(h, 1), :] = dots


def whole(shape):
    return pl.BlockSpec(shape, lambda h: (0,) * len(shape))


def column(rows, width, first=0):
    return pl.BlockSpec((rows, width), lambda h: (0, h + first))


def attend(normed, kv_weight, latents, d_attended):
    return pl.pallas_call(
        attend_kernel,
        name="attend",
        grid=(HEADS,),
        in_specs=[
            whole((TOK, CH)),
            column(CH, 128),
            column(CH, 128, HEADS),
            column(256, 128),
            column(256, 128),
        ],
        out_specs=[
            column(TOK, 128),
            column(TOK, 128),
            pl.BlockSpec((1, 128, 256), lambda h: (h, 0, 0)),
            whole((3, HEADS, 256)),
        ],
        out_shape=[
            jax.ShapeDtypeStruct((TOK, 1024), BF),
            jax.ShapeDtypeStruct((TOK, 1024), BF),
            jax.ShapeDtypeStruct((HEADS, 128, 256), F32),
            jax.ShapeDtypeStruct((3, HEADS, 256), F32),
        ],
        scratch_shapes=[pltpu.VMEM((TOK, 256), F32)],
        compiler_params=VMEM,
    )(normed, kv_weight, kv_weight, latents, d_attended)


def head_at(step, core):
    return (step + HEADS // 2 * (1 - core[0])) & (HEADS - 1)


def attend_grad_kernel(
    core, normed, k_in, v_in, wk, wv, q, up, lse, dots, factor, weighted, centred, inverse, gain,
    send, keep, d_mixed, gain_grad, top, bot, left, right, dn_sc, nt_sc, l_sc, r_sc, c_sc,
):
    step = pl.program_id(0)
    h = head_at(step, core)

    @pl.when(step == 0)
    def _():
        nt_sc[...] = normed[...].T
        dn_sc[...] = jnp.zeros_like(dn_sc)

    w = jnp.concatenate([wk[...], wv[...]], axis=1)
    level = lse[pl.ds(h, 1), :]
    row_dots = dots[pl.ds(h, 1), :]
    qg = jnp.zeros((128, 256), F32)
    wg = jnp.zeros((256, 256), F32)
    for c in range(TOK // CHUNK):
        rows = slice(c * CHUNK, (c + 1) * CHUNK)
        k = k_in[rows, :]
        p = jnp.exp2(dot(k, q[...], NT) * SCALE2 - level)
        dp = dot(v_in[rows, :], up[...], NT)
        ds = (p * (dp - row_dots)).astype(BF)
        qg = qg + dot(k, ds, TN)
        kg = (dot(ds, q[...]) * SCALE).astype(BF)
        vg = dot(p.astype(BF), up[...]).astype(BF)
        d_proj = jnp.concatenate([kg, vg], axis=1)
        wg = wg + dot(nt_sc[:, rows], d_proj)
        dn_sc[rows, :] += dot(d_proj, w, NT)
    att = (weighted[0] * factor[pl.ds(h, 1), :]).T
    qg = (qg * SCALE).T

    def put(out):
        out[0, 0] = att
        out[1, 0] = qg
        out[2, 0] = wg[:, :128]
        out[3, 0] = wg[:, 128:]

    @pl.when(step < HEADS // 2)
    def _():
        put(send)

    @pl.when(step >= HEADS // 2)
    def _():
        put(keep)

    @pl.when(step == HEADS - 1)
    def _():
        def body(n, total):
            rows = pl.ds(pl.multiple_of(n * BLOCK, BLOCK), BLOCK)
            x = centred[rows, :]
            inv = inverse[rows, :]
            dn = dn_sc[rows, :]
            total = total + jnp.sum(dn * x, axis=0, keepdims=True)
            g = dn * gain[...]
            mean = jnp.sum(g, axis=-1, keepdims=True) * (1.0 / CH)
            slope = jnp.sum(g * x, axis=-1, keepdims=True) * (1.0 / CH)
            inv = jnp.concatenate([inv, inv], axis=1)
            d_mixed[rows, :] = (inv * (g - mean - x * slope)).astype(BF)
            return total

        gain_grad[...] = lax.fori_loop(0, TOK // BLOCK, body, jnp.zeros((1, CH), F32))
        write_edges(d_mixed, top, bot, left, right, l_sc, r_sc, c_sc)


def attend_grad(
    core, normed, k, v, kv_weight, latents, d_attended, lse, dots, factor, weighted, centred, inverse, gain
):
    def full(shape):
        return pl.BlockSpec(shape, lambda n, core: (0,) * len(shape))

    def head(rows, first=0):
        return pl.BlockSpec((rows, 128), lambda n, core: (0, head_at(n, core) + first))

    half = HEADS // 2
    part = jax.ShapeDtypeStruct((4, half, 256, 128), F32)
    outs = pl.pallas_call(
        attend_grad_kernel,
        name="attend_grad",
        grid_spec=pltpu.PrefetchScalarGridSpec(
            num_scalar_prefetch=1,
            grid=(HEADS,),
            in_specs=[
                full((TOK, CH)),
                head(TOK),
                head(TOK),
                head(CH),
                head(CH, HEADS),
                head(256),
                head(256),
                full((HEADS, 256)),
                full((HEADS, 256)),
                full((HEADS, 256)),
                pl.BlockSpec((1, 128, 256), lambda n, core: (head_at(n, core), 0, 0)),
                full((TOK, CH)),
                full((TOK, 128)),
                full((1, CH)),
            ],
            out_specs=[
                pl.BlockSpec((4, 1, 256, 128), lambda n, core: (0, jnp.minimum(n, half - 1), 0, 0)),
                pl.BlockSpec((4, 1, 256, 128), lambda n, core: (0, jnp.maximum(n - half, 0), 0, 0)),
                full((TOK, CH)),
                full((1, CH)),
            ]
            + [full(s.shape) for s in EDGE_SHAPES],
            scratch_shapes=[pltpu.VMEM((TOK, CH), F32), pltpu.VMEM((CH, TOK), BF)] + EDGE_SCRATCH,
        ),
        out_shape=[
            part,
            part,
            jax.ShapeDtypeStruct((TOK, CH), BF),
            jax.ShapeDtypeStruct((1, CH), F32),
        ]
        + EDGE_SHAPES,
        compiler_params=VMEM,
        cost_estimate=COST,
    )(core, normed, k, v, kv_weight, kv_weight, latents, d_attended, lse, dots, factor, weighted, centred, inverse, gain)
    return outs[:4], outs[4:]


def kernel_grad_body(wide, d_mixed, out, d_sc):
    d_sc[...] = d_mixed[...].astype(F32)
    for half in range(2):
        lanes = pl.ds(half * 128, 128)
        for i in range(KSIZE):

            def body(n, acc):
                acc = list(acc)
                for r in range(4):
                    a = 4 * n + r
                    xs = [wide[a + i, c, :, lanes] for c in range(WIDE)]
                    base = pl.multiple_of(a * COLS, COLS)
                    ds = [d_sc[pl.ds(base + cb * 8, 8), lanes] for cb in range(8)]
                    for cb in range(8):
                        for j in range(KSIZE):
                            acc[j] = acc[j] + xs[cb + j] * ds[cb]
                return tuple(acc)

            zero = jnp.zeros((8, 128), F32)
            acc = lax.fori_loop(0, ROWS // 4, body, (zero,) * KSIZE)
            for j in range(KSIZE):
                n = i * KSIZE + j
                out[n : n + 1, lanes] = jnp.sum(acc[j], axis=0, keepdims=True)


def kernel_grad(wide, d_mixed):
    return pl.pallas_call(
        kernel_grad_body,
        name="kernel_grad",
        out_shape=jax.ShapeDtypeStruct((KSIZE * KSIZE, CH), F32),
        scratch_shapes=[pltpu.VMEM((TOK, CH), F32)],
        compiler_params=VMEM,
        cost_estimate=COST,
    )(wide, d_mixed)


def conv_back_body(d_mixed, above, below, lh, rh, kern, z, patch_grad, bias_grad, wide, d_sc, w_sc, l_sc, r_sc, c_sc):
    assemble(wide, d_mixed, (above, below, lh, rh), l_sc, r_sc, c_sc)
    spread_weights(kern, w_sc)
    zero = jnp.zeros((8, 128), F32)

    def body(n, bias):
        bias = list(bias)
        for half in range(2):
            accs = conv_rows(wide, w_sc, 2 * n, half, True)
            for r in range(2):
                a = 2 * n + r
                acc = jnp.concatenate(accs[r], axis=0).astype(BF)
                d_sc[a & 7, pl.ds(pl.multiple_of((a >> 3) * 64, 64), 64), pl.ds(half * 128, 128)] = acc
                bias[half] = bias[half] + jnp.sum(acc.astype(F32).reshape(8, 8, 128), axis=0)
        return tuple(bias)

    bias = lax.fori_loop(0, ROWS // 2, body, (zero, zero))
    for half in range(2):
        bias_grad[:, half * 128 : (half + 1) * 128] = jnp.sum(bias[half], axis=0, keepdims=True)
    total = [jnp.zeros((16, CH), F32) for _ in range(4)]
    for a8 in range(8):
        part = dot(z[...], d_sc[a8], TN)
        for v in range(4):
            first = v * 128 + a8 * 16
            total[v] = total[v] + part[first : first + 16, :]
    for v in range(4):
        patch_grad[v] = total[v]


def conv_back(d_mixed, halo, conv_kernel, z):
    return pl.pallas_call(
        conv_back_body,
        name="conv_back",
        out_shape=[jax.ShapeDtypeStruct((4, 16, CH), F32), jax.ShapeDtypeStruct((1, CH), F32)],
        scratch_shapes=[
            pltpu.VMEM((ROWS + 2 * HALO, WIDE, 8, CH), F32),
            pltpu.VMEM((8, 256, CH), BF),
            pltpu.VMEM((KSIZE * KSIZE, 8, CH), F32),
        ]
        + EDGE_SCRATCH,
        compiler_params=VMEM,
        cost_estimate=COST,
    )(d_mixed, *halo, conv_kernel, z)


CHIPS = ("z", "x", "y")
ALL = ("z", "core", "x", "y")
PAIR = [(0, 1), (1, 0)]


def gather(x, axes):
    n = lax.axis_size(axes)
    copies = jnp.broadcast_to(x[None], (n,) + x.shape)
    return lax.all_to_all(copies, axes, 0, 0, tiled=True)


def combine_stats(stats):
    for axes in (("z", "core"), ("x", "y")):
        group = gather(stats, axes)
        peak = jnp.max(group[:, 0], axis=0)
        factors = jnp.exp2(group[:, 0] - peak)
        total = jnp.sum(group[:, 1] * factors, axis=0)
        dots = jnp.sum(group[:, 2] * factors, axis=0)
        stats = jnp.stack([peak, total, dots])
    return stats


def swap(half):
    other = lax.ppermute(half, "core", PAIR)
    first = lax.axis_index("core") == 0
    pair = [jnp.where(first, half, other), jnp.where(first, other, half)]
    return jnp.stack([x.reshape(4, HEADS // 2, 256, 128) for x in pair], axis=1)


def block_sum(parts):
    return jnp.sum(parts.astype(F32), axis=0)


def copies(x):
    return jnp.broadcast_to(x.astype(WIRE)[None], (64,) + x.shape)


def send(x):
    return lax.all_to_all(x, CHIPS, 0, 0, tiled=True)


def send_all(x):
    return lax.all_to_all(x, ALL, 0, 0, tiled=True)


def tie(x, *others):
    return lax.optimization_barrier((x,) + others)


def columns(x):
    return x.transpose(1, 0, 2).reshape(256, -1)


def per_device(
    pixels, patch_weight, patch_bias, conv_kernel, norm_gain, kv_weight, latents, d_attended
):
    gain = norm_gain.reshape(1, CH)
    emb, z, edges = embed(pixels, patch_weight, patch_bias)
    rows = exchange_rows(edges)
    halo = rows + exchange_cols(edges, *rows)
    wide, centred, inverse, normed = conv_forward(emb, halo, conv_kernel, gain)
    k, v, weighted, local = attend(normed, kv_weight, latents, d_attended)
    stats = combine_stats(local)
    lse = stats[0] + jnp.log2(stats[1])
    row_dots = stats[2] / stats[1]
    factor = jnp.exp2(local[0] - stats[0]) / stats[1]
    core = lax.axis_index("core").astype(jnp.int32).reshape(1)
    (away, keep, d_mixed, gain_grad), d_edges = attend_grad(
        core, normed, k, v, kv_weight, latents, d_attended, lse, row_dots, factor, weighted,
        centred, inverse, gain,
    )
    d_rows = exchange_rows(d_edges)
    message = (keep + lax.ppermute(away, "core", PAIR)).astype(BF).reshape(64, 64, 128)
    d_mixed, message, *d_rows = tie(d_mixed, message, *d_rows)
    message = send(message)
    d_cols = exchange_cols(d_edges, *d_rows)
    kern = kernel_grad(wide, d_mixed)
    d_mixed, message, kern, *d_cols = tie(d_mixed, message, kern, *d_cols)
    message = copies(block_sum(message))
    d_mixed, message = tie(d_mixed, message)
    message = send(message)
    patch, bias = conv_back(d_mixed, tuple(d_rows) + tuple(d_cols), conv_kernel, z)
    patch, bias, message = tie(patch, bias, message)
    small = jnp.concatenate([patch.reshape(64, CH), kern, gain_grad, bias], axis=0)
    mine = block_sum(send_all(jnp.pad(small, ((0, 13), (0, 0)))[:, None]))
    small = send_all(jnp.broadcast_to(mine[None], (128,) + mine.shape))
    sums = swap(message).astype(F32).reshape(4, HEADS, 256, 128)
    outs = (columns(sums[0]), columns(sums[1]), columns(sums[2:].reshape(2 * HEADS, 256, 128)))
    small, *outs = tie(small, *outs)
    small = small[:, 0]
    patch = small[:64].reshape(4, 16, CH)[:, :12].transpose(1, 0, 2).reshape(48, CH)
    return (
        *outs,
        small[64 + 49],
        small[64 : 64 + 49],
        patch,
        small[64 + 50],
    )


def solution(mesh):
    split = Mesh(mesh.devices.reshape(4, 2, 4, 4), ("z", "core", "x", "y"))
    return jax.shard_map(
        per_device,
        mesh=split,
        in_specs=(P(None, ("z", "core"), ("x", "y")), P(), P(), P(), P(), P(), P(), P()),
        out_specs=(P(), P(), P(), P(), P(), P(), P()),
        check_vma=False,
    )
```

```python
import jax
import jax.numpy as jnp
from jax import lax
from jax.experimental import pallas as pl
from jax.experimental.pallas import tpu as pltpu
from jax.sharding import Mesh
from jax.sharding import PartitionSpec as P

PATCH = 4
KSIZE = 7
HEADS = 8
HALO = 3
norm_eps = 1e-05
BF = jnp.bfloat16
F32 = jnp.float32
NT = (((1,), (1,)), ((), ()))
TN = (((0,), (0,)), ((), ()))
NN = (((1,), (0,)), ((), ()))
ROWS = 32
COLS = 64
CH = 256
TOK = ROWS * COLS
WIDE = 14
BLOCK = 1024
WIRE = BF
ROW_AXES = ("z", "core")
COL_AXES = ("x", "y")
VMEM = pltpu.CompilerParams(vmem_limit_bytes=58 << 20)


def dot(a, b, dims=NN):
    return lax.dot_general(a, b, dims, preferred_element_type=F32)


def iota(shape, dim):
    return lax.broadcasted_iota(jnp.int32, shape, dim)


def write_edges(src, top, bot, left, right, l_sc, r_sc, c_sc):
    for a in range(ROWS):
        low = src[a * COLS : a * COLS + 32, :].astype(F32)
        high = src[a * COLS + 32 : a * COLS + 64, :].astype(F32)
        for k in range(HALO):
            l_sc[k * ROWS + a : k * ROWS + a + 1, :] = low[8 * k : 8 * k + 1, :]
            r_sc[k * ROWS + a : k * ROWS + a + 1, :] = high[8 * k + 15 : 8 * k + 16, :]
    left[...] = l_sc[...].astype(BF)
    right[...] = r_sc[...].astype(BF)
    c_sc[...] = jnp.zeros_like(c_sc)
    for k in range(HALO):
        for i in range(HALO):
            first = k * ROWS + i
            last = k * ROWS + ROWS - HALO + i
            row = k * HALO + i
            c_sc[0, row : row + 1, :] = l_sc[first : first + 1, :]
            c_sc[1, row : row + 1, :] = r_sc[first : first + 1, :]
            c_sc[2, row : row + 1, :] = l_sc[last : last + 1, :]
            c_sc[3, row : row + 1, :] = r_sc[last : last + 1, :]
    side = HALO * COLS
    top[:side, :] = src[0:side, :]
    bot[:side, :] = src[TOK - side : TOK, :]
    for n, ref in enumerate((top, bot)):
        ref[side : side + 16, :] = c_sc[2 * n].astype(BF)
        ref[side + 16 : side + 32, :] = c_sc[2 * n + 1].astype(BF)


EDGE_SHAPES = [
    jax.ShapeDtypeStruct((HALO * COLS + 32, CH), BF),
    jax.ShapeDtypeStruct((HALO * COLS + 32, CH), BF),
    jax.ShapeDtypeStruct((HALO * ROWS, CH), BF),
    jax.ShapeDtypeStruct((HALO * ROWS, CH), BF),
]
EDGE_SCRATCH = [
    pltpu.VMEM((HALO * ROWS, CH), F32),
    pltpu.VMEM((HALO * ROWS, CH), F32),
    pltpu.VMEM((4, 16, CH), F32),
]


def exchange_rows(edges):
    top, bot = edges[:2]
    n = lax.axis_size(ROW_AXES)
    above = lax.ppermute(bot, ROW_AXES, [(i, i + 1) for i in range(n - 1)])
    below = lax.ppermute(top, ROW_AXES, [(i + 1, i) for i in range(n - 1)])
    return above, below


def exchange_cols(edges, above, below):
    left, right = edges[2:]
    n = lax.axis_size(COL_AXES)
    side = HALO * COLS
    right = jnp.concatenate([right, above[side + 16 : side + 32], below[side + 16 : side + 32]])
    left = jnp.concatenate([left, above[side : side + 16], below[side : side + 16]])
    from_left = lax.ppermute(right, COL_AXES, [(i, i + 1) for i in range(n - 1)])
    from_right = lax.ppermute(left, COL_AXES, [(i + 1, i) for i in range(n - 1)])
    return from_left, from_right


def assemble(wide, own, halo, l_sc, r_sc, c_sc):
    above, below, left, right = halo
    edge = HALO * ROWS
    l_sc[...] = left[:edge, :].astype(F32)
    r_sc[...] = right[:edge, :].astype(F32)
    for n in range(2):
        c_sc[2 * n] = left[edge + 16 * n : edge + 16 * (n + 1), :].astype(F32)
        c_sc[2 * n + 1] = right[edge + 16 * n : edge + 16 * (n + 1), :].astype(F32)
    sub = iota((8, CH), 0)

    def put(row, x, lefts, rights):
        x = x.astype(F32).reshape(8, 8, CH)
        for cb in range(8):
            wide[row, HALO + cb] = x[cb]
        for k in range(HALO):
            wide[row, k] = jnp.where(sub == 0, lefts[k], pltpu.roll(x[5 + k], 1, 0))
            wide[row, 11 + k] = jnp.where(sub == 7, rights[k], pltpu.roll(x[k], 7, 0))

    for i in range(HALO):
        row = [k * HALO + i for k in range(HALO)]
        put(
            i,
            above[i * COLS : (i + 1) * COLS, :],
            [c_sc[0, n : n + 1, :] for n in row],
            [c_sc[1, n : n + 1, :] for n in row],
        )
        put(
            HALO + ROWS + i,
            below[i * COLS : (i + 1) * COLS, :],
            [c_sc[2, n : n + 1, :] for n in row],
            [c_sc[3, n : n + 1, :] for n in row],
        )

    def body(a, carry):
        put(
            a + HALO,
            own[pl.ds(pl.multiple_of(a * COLS, COLS), COLS), :],
            [l_sc[pl.ds(k * ROWS + a, 1), :] for k in range(HALO)],
            [r_sc[pl.ds(k * ROWS + a, 1), :] for k in range(HALO)],
        )
        return carry

    lax.fori_loop(0, ROWS, body, 0)


def spread_weights(kernel_ref, w_sc):
    for n in range(KSIZE * KSIZE):
        w_sc[n] = jnp.broadcast_to(kernel_ref[n : n + 1, :], (8, CH))


def conv_rows(wide, w_sc, a, half, flip):
    lanes = pl.ds(half * 128, 128)
    acc = [[wide[a + r + HALO, HALO + cb, :, lanes] for cb in range(8)] for r in range(2)]
    for i in range(KSIZE + 1):
        xs = [wide[a + i, c, :, lanes] for c in range(WIDE)]
        for r in range(2):
            if not 0 <= i - r < KSIZE:
                continue
            for j in range(KSIZE):
                n = (i - r) * KSIZE + j
                w = w_sc[KSIZE * KSIZE - 1 - n if flip else n, :, lanes]
                acc[r] = [acc[r][cb] + xs[cb + j] * w for cb in range(8)]
    return acc


def norm_rows(x):
    centre = x - jnp.sum(x, axis=-1, keepdims=True) * (1.0 / CH)
    variance = jnp.sum(centre * centre, axis=-1, keepdims=True) * (1.0 / CH)
    inverse = lax.rsqrt(variance + norm_eps)
    return centre * inverse, inverse


def embed_kernel(pixels, weights, bias, emb, z_ref, top, bot, left, right, w_sc, l_sc, r_sc, c_sc):
    out = iota((256, 256), 0)
    spread = (((out & 7) * 8 + ((out >> 3) & 7)) * 4 + (out >> 6)) == iota((256, 256), 1)
    spread = jnp.where(spread, 1.0, 0.0).astype(BF)
    by_cell = dot(spread, pixels[...], NT).astype(BF)
    row = iota((512, 384), 0)
    fu = row & 15
    target = (fu >> 2) * 128 + (row >> 4) * 4 + (fu & 3)
    order = jnp.where((target == iota((512, 384), 1)) & (fu < 12), 1.0, 0.0).astype(BF)
    z = dot(by_cell, order, NT).astype(BF)
    for g in range(4):
        for v in range(4):
            z_ref[g * 64 : (g + 1) * 64, v * 128 : (v + 1) * 128] = z[
                v * 64 : (v + 1) * 64, g * 128 : (g + 1) * 128
            ]
    w_sc[...] = jnp.zeros_like(w_sc)
    for v in range(4):
        for a8 in range(8):
            first = v * 128 + a8 * 16
            w_sc[first : first + 16, a8 * CH : (a8 + 1) * CH] = weights[v]
    for a8 in range(8):
        block = dot(z_ref[...], w_sc[:, a8 * CH : (a8 + 1) * CH]) + bias[...]
        block = block.astype(BF)
        for g in range(4):
            a = g * 8 + a8
            emb[a * COLS : (a + 1) * COLS, :] = block[g * 64 : (g + 1) * 64, :]
    write_edges(emb, top, bot, left, right, l_sc, r_sc, c_sc)


def embed(pixels, patch_weight, patch_bias):
    weights = patch_weight.reshape(12, 4, CH).transpose(1, 0, 2)
    weights = jnp.pad(weights, ((0, 0), (0, 4), (0, 0)))
    outs = pl.pallas_call(
        embed_kernel,
        name="embed",
        out_shape=[
            jax.ShapeDtypeStruct((TOK, CH), BF),
            jax.ShapeDtypeStruct((256, 512), BF),
        ]
        + EDGE_SHAPES,
        scratch_shapes=[pltpu.VMEM((512, 2048), BF)] + EDGE_SCRATCH,
        compiler_params=VMEM,
    )(pixels.reshape(384, 256), weights, patch_bias.reshape(1, CH))
    return outs[0], outs[1], outs[2:]


def conv_kernel_body(emb, above, below, lh, rh, kern, gain, wide, centred, inverse, normed, w_sc, l_sc, r_sc, c_sc):
    assemble(wide, emb, (above, below, lh, rh), l_sc, r_sc, c_sc)
    spread_weights(kern, w_sc)

    def body(n, carry):
        for half in range(2):
            acc = conv_rows(wide, w_sc, 2 * n, half, False)
            for r in range(2):
                for cb in range(8):
                    rows = pl.ds(pl.multiple_of((2 * n + r) * COLS + cb * 8, 8), 8)
                    centred[rows, pl.ds(half * 128, 128)] = acc[r][cb]
        return carry

    lax.fori_loop(0, ROWS // 2, body, 0)

    def norm_body(n, carry):
        rows = pl.ds(pl.multiple_of(n * BLOCK, BLOCK), BLOCK)
        out, inv = norm_rows(centred[rows, :])
        centred[rows, :] = out
        inverse[rows, :] = jnp.broadcast_to(inv, (BLOCK, 128))
        normed[rows, :] = (out * gain[...]).astype(BF)
        return carry

    lax.fori_loop(0, TOK // BLOCK, norm_body, 0)


def conv_forward(emb, halo, conv_kernel, gain):
    return pl.pallas_call(
        conv_kernel_body,
        name="conv_forward",
        out_shape=[
            jax.ShapeDtypeStruct((ROWS + 2 * HALO, WIDE, 8, CH), F32),
            jax.ShapeDtypeStruct((TOK, CH), F32),
            jax.ShapeDtypeStruct((TOK, 128), F32),
            jax.ShapeDtypeStruct((TOK, CH), BF),
        ],
        scratch_shapes=[pltpu.VMEM((KSIZE * KSIZE, 8, CH), F32)] + EDGE_SCRATCH,
        compiler_params=VMEM,
    )(emb, *halo, conv_kernel, gain)


CHUNK = 1024
GROUP = 2
ACHUNK = 1024
WIDTH = 4
SCALE = 128**-0.5
SCALE2 = SCALE * 1.4426950408889634
COST = pl.CostEstimate(flops=14_000_000_000, transcendentals=0, bytes_accessed=16_000_000)


def lane(n):
    return slice(n * 128, (n + 1) * 128)


def attend_kernel(normed, wk, wv, q, up, k_out, v_out, weighted, stats, s_sc):
    step = pl.program_id(0)
    peak = [None] * WIDTH
    level = None
    for n in range(WIDTH + 1):
        total = jnp.zeros((1, 256), F32)
        acc = jnp.zeros((128, 256), F32)
        if n < WIDTH:
            w = jnp.concatenate([wk[:, lane(n)], wv[:, lane(n)]], axis=1)
        for c in range(TOK // ACHUNK):
            rows = slice(c * ACHUNK, (c + 1) * ACHUNK)
            if n < WIDTH:
                kv = dot(normed[rows, :], w).astype(BF)
                k_out[rows, lane(n)] = kv[:, :128]
                v_out[rows, lane(n)] = kv[:, 128:]
                s = dot(kv[:, :128], q[:, lane(n)], NT)
                s_sc[n % 2, rows, :] = s
                top = jnp.max(s, axis=0, keepdims=True)
                peak[n] = top if peak[n] is None else jnp.maximum(peak[n], top)
            if n > 0:
                p = jnp.exp2(s_sc[1 - n % 2, rows, :] * SCALE2 - level)
                total = total + jnp.sum(p, axis=0, keepdims=True)
                acc = acc + dot(v_out[rows, lane(n - 1)], p.astype(BF), TN)
        if n > 0:
            weighted[n - 1] = acc
            dots = jnp.sum(acc * up[:, lane(n - 1)].astype(F32).T, axis=0, keepdims=True)
            h = step * WIDTH + n - 1
            stats[0, pl.ds(h, 1), :] = level
            stats[1, pl.ds(h, 1), :] = total
            stats[2, pl.ds(h, 1), :] = dots
        if n < WIDTH:
            level = peak[n] * SCALE2


def whole(shape):
    return pl.BlockSpec(shape, lambda h: (0,) * len(shape))


def column(rows, first=0):
    return pl.BlockSpec((rows, 128 * WIDTH), lambda h: (0, h + first))


def attend(normed, kv_weight, latents, d_attended):
    return pl.pallas_call(
        attend_kernel,
        name="attend",
        grid=(HEADS // WIDTH,),
        in_specs=[
            whole((TOK, CH)),
            column(CH),
            column(CH, HEADS // WIDTH),
            column(256),
            column(256),
        ],
        out_specs=[
            column(TOK),
            column(TOK),
            pl.BlockSpec((WIDTH, 128, 256), lambda h: (h, 0, 0)),
            whole((3, HEADS, 256)),
        ],
        out_shape=[
            jax.ShapeDtypeStruct((TOK, 1024), BF),
            jax.ShapeDtypeStruct((TOK, 1024), BF),
            jax.ShapeDtypeStruct((HEADS, 128, 256), F32),
            jax.ShapeDtypeStruct((3, HEADS, 256), F32),
        ],
        scratch_shapes=[pltpu.VMEM((2, TOK, 256), F32)],
        compiler_params=VMEM,
    )(normed, kv_weight, kv_weight, latents, d_attended)


STEPS = HEADS // GROUP


def step_at(step, core):
    return (step + STEPS // 2 * (1 - core[0])) & (STEPS - 1)


def attend_grad_kernel(
    core, normed, k_in, v_in, wk, wv, q, up, lse, dots, factor, weighted, centred, inverse, gain,
    send, keep, d_mixed, gain_grad, top, bot, left, right, dn_sc, nt_sc, l_sc, r_sc, c_sc,
):
    step = pl.program_id(0)
    first = step_at(step, core) * GROUP

    @pl.when(step == 0)
    def _():
        nt_sc[...] = normed[...].T
        dn_sc[...] = jnp.zeros_like(dn_sc)

    w = jnp.concatenate([x[:, lane(n)] for n in range(GROUP) for x in (wk, wv)], axis=1)
    level = [lse[pl.ds(first + n, 1), :] for n in range(GROUP)]
    row_dots = [dots[pl.ds(first + n, 1), :] for n in range(GROUP)]
    qg = [jnp.zeros((128, 256), F32)] * GROUP
    wg = jnp.zeros((256, 256 * GROUP), F32)
    units = [(c, n) for c in range(TOK // CHUNK) for n in range(GROUP)]

    def products(c, n):
        rows = slice(c * CHUNK, (c + 1) * CHUNK)
        return (
            dot(k_in[rows, lane(n)], q[:, lane(n)], NT),
            dot(v_in[rows, lane(n)], up[:, lane(n)], NT),
        )

    d_proj = []
    ahead = products(*units[0])
    for at, (c, n) in enumerate(units):
        rows = slice(c * CHUNK, (c + 1) * CHUNK)
        s, dp = ahead
        if at + 1 < len(units):
            ahead = products(*units[at + 1])
        p = jnp.exp2(s * SCALE2 - level[n])
        ds = (p * (dp - row_dots[n])).astype(BF)
        qg[n] = qg[n] + dot(k_in[rows, lane(n)], ds, TN)
        d_proj.append((dot(ds, q[:, lane(n)]) * SCALE).astype(BF))
        d_proj.append(dot(p.astype(BF), up[:, lane(n)]).astype(BF))
        if n == GROUP - 1:
            d_proj = jnp.concatenate(d_proj, axis=1)
            wg = wg + dot(nt_sc[:, rows], d_proj)
            dn_sc[rows, :] += dot(d_proj, w, NT)
            d_proj = []
    att = [(weighted[n] * factor[pl.ds(first + n, 1), :]).T for n in range(GROUP)]
    qg = [(x * SCALE).T for x in qg]

    def put(out):
        for n in range(GROUP):
            out[0, n] = att[n]
            out[1, n] = qg[n]
            out[2, n] = wg[:, lane(2 * n)]
            out[3, n] = wg[:, lane(2 * n + 1)]

    @pl.when(step < STEPS // 2)
    def _():
        put(send)

    @pl.when(step >= STEPS // 2)
    def _():
        put(keep)

    @pl.when(step == STEPS - 1)
    def _():
        def body(n, total):
            rows = pl.ds(pl.multiple_of(n * BLOCK, BLOCK), BLOCK)
            x = centred[rows, :]
            inv = inverse[rows, :]
            dn = dn_sc[rows, :]
            total = total + jnp.sum(dn * x, axis=0, keepdims=True)
            g = dn * gain[...]
            mean = jnp.sum(g, axis=-1, keepdims=True) * (1.0 / CH)
            slope = jnp.sum(g * x, axis=-1, keepdims=True) * (1.0 / CH)
            inv = jnp.concatenate([inv, inv], axis=1)
            d_mixed[rows, :] = (inv * (g - mean - x * slope)).astype(BF)
            return total

        gain_grad[...] = lax.fori_loop(0, TOK // BLOCK, body, jnp.zeros((1, CH), F32))
        write_edges(d_mixed, top, bot, left, right, l_sc, r_sc, c_sc)


def attend_grad(
    core, normed, k, v, kv_weight, latents, d_attended, lse, dots, factor, weighted, centred, inverse, gain
):
    def full(shape):
        return pl.BlockSpec(shape, lambda n, core: (0,) * len(shape))

    def head(rows, first=0):
        return pl.BlockSpec((rows, 128 * GROUP), lambda n, core: (0, step_at(n, core) + first))

    half = STEPS // 2
    block = (4, GROUP, 256, 128)
    part = jax.ShapeDtypeStruct((4, HEADS // 2, 256, 128), F32)
    outs = pl.pallas_call(
        attend_grad_kernel,
        name="attend_grad",
        grid_spec=pltpu.PrefetchScalarGridSpec(
            num_scalar_prefetch=1,
            grid=(STEPS,),
            in_specs=[
                full((TOK, CH)),
                head(TOK),
                head(TOK),
                head(CH),
                head(CH, STEPS),
                head(256),
                head(256),
                full((HEADS, 256)),
                full((HEADS, 256)),
                full((HEADS, 256)),
                pl.BlockSpec((GROUP, 128, 256), lambda n, core: (step_at(n, core), 0, 0)),
                full((TOK, CH)),
                full((TOK, 128)),
                full((1, CH)),
            ],
            out_specs=[
                pl.BlockSpec(block, lambda n, core: (0, jnp.minimum(n, half - 1), 0, 0)),
                pl.BlockSpec(block, lambda n, core: (0, jnp.maximum(n - half, 0), 0, 0)),
                full((TOK, CH)),
                full((1, CH)),
            ]
            + [full(s.shape) for s in EDGE_SHAPES],
            scratch_shapes=[pltpu.VMEM((TOK, CH), F32), pltpu.VMEM((CH, TOK), BF)] + EDGE_SCRATCH,
        ),
        out_shape=[
            part,
            part,
            jax.ShapeDtypeStruct((TOK, CH), BF),
            jax.ShapeDtypeStruct((1, CH), F32),
        ]
        + EDGE_SHAPES,
        compiler_params=VMEM,
        cost_estimate=COST,
    )(core, normed, k, v, kv_weight, kv_weight, latents, d_attended, lse, dots, factor, weighted, centred, inverse, gain)
    return outs[:4], outs[4:]


def kernel_grad_body(wide, d_mixed, out, d_sc):
    d_sc[...] = d_mixed[...].astype(F32)
    for half in range(2):
        lanes = pl.ds(half * 128, 128)
        for i in range(KSIZE):

            def body(n, acc):
                acc = list(acc)
                for r in range(4):
                    a = 4 * n + r
                    xs = [wide[a + i, c, :, lanes] for c in range(WIDE)]
                    base = pl.multiple_of(a * COLS, COLS)
                    ds = [d_sc[pl.ds(base + cb * 8, 8), lanes] for cb in range(8)]
                    for cb in range(8):
                        for j in range(KSIZE):
                            acc[j] = acc[j] + xs[cb + j] * ds[cb]
                return tuple(acc)

            zero = jnp.zeros((8, 128), F32)
            acc = lax.fori_loop(0, ROWS // 4, body, (zero,) * KSIZE)
            for j in range(KSIZE):
                n = i * KSIZE + j
                out[n : n + 1, lanes] = jnp.sum(acc[j], axis=0, keepdims=True)


def kernel_grad(wide, d_mixed):
    return pl.pallas_call(
        kernel_grad_body,
        name="kernel_grad",
        out_shape=jax.ShapeDtypeStruct((KSIZE * KSIZE, CH), F32),
        scratch_shapes=[pltpu.VMEM((TOK, CH), F32)],
        compiler_params=VMEM,
        cost_estimate=COST,
    )(wide, d_mixed)


def conv_back_body(d_mixed, above, below, lh, rh, kern, z, patch_grad, bias_grad, wide, d_sc, w_sc, l_sc, r_sc, c_sc):
    assemble(wide, d_mixed, (above, below, lh, rh), l_sc, r_sc, c_sc)
    spread_weights(kern, w_sc)
    zero = jnp.zeros((8, 128), F32)

    def body(n, bias):
        bias = list(bias)
        for half in range(2):
            accs = conv_rows(wide, w_sc, 2 * n, half, True)
            for r in range(2):
                a = 2 * n + r
                acc = jnp.concatenate(accs[r], axis=0).astype(BF)
                d_sc[a & 7, pl.ds(pl.multiple_of((a >> 3) * 64, 64), 64), pl.ds(half * 128, 128)] = acc
                bias[half] = bias[half] + jnp.sum(acc.astype(F32).reshape(8, 8, 128), axis=0)
        return tuple(bias)

    bias = lax.fori_loop(0, ROWS // 2, body, (zero, zero))
    for half in range(2):
        bias_grad[:, half * 128 : (half + 1) * 128] = jnp.sum(bias[half], axis=0, keepdims=True)
    total = [jnp.zeros((16, CH), F32) for _ in range(4)]
    for a8 in range(8):
        part = dot(z[...], d_sc[a8], TN)
        for v in range(4):
            first = v * 128 + a8 * 16
            total[v] = total[v] + part[first : first + 16, :]
    for v in range(4):
        patch_grad[v] = total[v]


def conv_back(d_mixed, halo, conv_kernel, z):
    return pl.pallas_call(
        conv_back_body,
        name="conv_back",
        out_shape=[jax.ShapeDtypeStruct((4, 16, CH), F32), jax.ShapeDtypeStruct((1, CH), F32)],
        scratch_shapes=[
            pltpu.VMEM((ROWS + 2 * HALO, WIDE, 8, CH), F32),
            pltpu.VMEM((8, 256, CH), BF),
            pltpu.VMEM((KSIZE * KSIZE, 8, CH), F32),
        ]
        + EDGE_SCRATCH,
        compiler_params=VMEM,
        cost_estimate=COST,
    )(d_mixed, *halo, conv_kernel, z)


CHIPS = ("z", "x", "y")
ALL = ("z", "core", "x", "y")
PAIR = [(0, 1), (1, 0)]


def gather(x, axes):
    n = lax.axis_size(axes)
    copies = jnp.broadcast_to(x[None], (n,) + x.shape)
    return lax.all_to_all(copies, axes, 0, 0, tiled=True)


def combine_stats(stats):
    for axes in (("z", "core"), ("x", "y")):
        group = gather(stats, axes)
        peak = jnp.max(group[:, 0], axis=0)
        factors = jnp.exp2(group[:, 0] - peak)
        total = jnp.sum(group[:, 1] * factors, axis=0)
        dots = jnp.sum(group[:, 2] * factors, axis=0)
        stats = jnp.stack([peak, total, dots])
    return stats


def swap(half):
    other = lax.ppermute(half, "core", PAIR)
    first = lax.axis_index("core") == 0
    pair = [jnp.where(first, half, other), jnp.where(first, other, half)]
    return jnp.stack([x.reshape(4, HEADS // 2, 256, 128) for x in pair], axis=1)


def block_sum(parts):
    return jnp.sum(parts.astype(F32), axis=0)


def copies(x):
    return jnp.broadcast_to(x.astype(WIRE)[None], (64,) + x.shape)


def send(x):
    return lax.all_to_all(x, CHIPS, 0, 0, tiled=True)


def send_all(x):
    return lax.all_to_all(x, ALL, 0, 0, tiled=True)


def tie(x, *others):
    return lax.optimization_barrier((x,) + others)


def columns(x):
    return x.transpose(1, 0, 2).reshape(256, -1)


def per_device(
    pixels, patch_weight, patch_bias, conv_kernel, norm_gain, kv_weight, latents, d_attended
):
    gain = norm_gain.reshape(1, CH)
    emb, z, edges = embed(pixels, patch_weight, patch_bias)
    rows = exchange_rows(edges)
    halo = rows + exchange_cols(edges, *rows)
    wide, centred, inverse, normed = conv_forward(emb, halo, conv_kernel, gain)
    k, v, weighted, local = attend(normed, kv_weight, latents, d_attended)
    stats = combine_stats(local)
    lse = stats[0] + jnp.log2(stats[1])
    row_dots = stats[2] / stats[1]
    factor = jnp.exp2(local[0] - stats[0]) / stats[1]
    core = lax.axis_index("core").astype(jnp.int32).reshape(1)
    (away, keep, d_mixed, gain_grad), d_edges = attend_grad(
        core, normed, k, v, kv_weight, latents, d_attended, lse, row_dots, factor, weighted,
        centred, inverse, gain,
    )
    d_rows = exchange_rows(d_edges)
    message = (keep + lax.ppermute(away, "core", PAIR)).astype(BF).reshape(64, 64, 128)
    d_mixed, message, *d_rows = tie(d_mixed, message, *d_rows)
    message = send(message)
    d_cols = exchange_cols(d_edges, *d_rows)
    kern = kernel_grad(wide, d_mixed)
    d_mixed, message, kern, *d_cols = tie(d_mixed, message, kern, *d_cols)
    message = copies(block_sum(message))
    d_mixed, message = tie(d_mixed, message)
    message = send(message)
    patch, bias = conv_back(d_mixed, tuple(d_rows) + tuple(d_cols), conv_kernel, z)
    patch, bias, message = tie(patch, bias, message)
    small = jnp.concatenate([patch.reshape(64, CH), kern, gain_grad, bias], axis=0)
    mine = block_sum(send_all(jnp.pad(small, ((0, 13), (0, 0)))[:, None]))
    small = send_all(jnp.broadcast_to(mine[None], (128,) + mine.shape))
    sums = swap(message).astype(F32).reshape(4, HEADS, 256, 128)
    outs = (columns(sums[0]), columns(sums[1]), columns(sums[2:].reshape(2 * HEADS, 256, 128)))
    small, *outs = tie(small, *outs)
    small = small[:, 0]
    patch = small[:64].reshape(4, 16, CH)[:, :12].transpose(1, 0, 2).reshape(48, CH)
    return (
        *outs,
        small[64 + 49],
        small[64 : 64 + 49],
        patch,
        small[64 + 50],
    )


def solution(mesh):
    split = Mesh(mesh.devices.reshape(4, 2, 4, 4), ("z", "core", "x", "y"))
    return jax.shard_map(
        per_device,
        mesh=split,
        in_specs=(P(None, ("z", "core"), ("x", "y")), P(), P(), P(), P(), P(), P(), P()),
        out_specs=(P(), P(), P(), P(), P(), P(), P()),
        check_vma=False,
    )
```

```python
import jax
import jax.numpy as jnp
from jax import lax
from jax.experimental import pallas as pl
from jax.experimental.pallas import tpu as pltpu
from jax.sharding import Mesh
from jax.sharding import PartitionSpec as P

PATCH = 4
KSIZE = 7
HEADS = 8
HALO = 3
norm_eps = 1e-05
BF = jnp.bfloat16
F32 = jnp.float32
NT = (((1,), (1,)), ((), ()))
TN = (((0,), (0,)), ((), ()))
NN = (((1,), (0,)), ((), ()))
ROWS = 32
COLS = 64
CH = 256
TOK = ROWS * COLS
WIDE = 14
BLOCK = 1024
WIRE = BF
ROW_AXES = ("z", "core")
COL_AXES = ("x", "y")
VMEM = pltpu.CompilerParams(vmem_limit_bytes=58 << 20)


def dot(a, b, dims=NN):
    return lax.dot_general(a, b, dims, preferred_element_type=F32)


def iota(shape, dim):
    return lax.broadcasted_iota(jnp.int32, shape, dim)


def write_edges(src, top, bot, left, right, l_sc, r_sc, c_sc):
    for a in range(ROWS):
        low = src[a * COLS : a * COLS + 32, :].astype(F32)
        high = src[a * COLS + 32 : a * COLS + 64, :].astype(F32)
        for k in range(HALO):
            l_sc[k * ROWS + a : k * ROWS + a + 1, :] = low[8 * k : 8 * k + 1, :]
            r_sc[k * ROWS + a : k * ROWS + a + 1, :] = high[8 * k + 15 : 8 * k + 16, :]
    left[...] = l_sc[...].astype(BF)
    right[...] = r_sc[...].astype(BF)
    c_sc[...] = jnp.zeros_like(c_sc)
    for k in range(HALO):
        for i in range(HALO):
            first = k * ROWS + i
            last = k * ROWS + ROWS - HALO + i
            row = k * HALO + i
            c_sc[0, row : row + 1, :] = l_sc[first : first + 1, :]
            c_sc[1, row : row + 1, :] = r_sc[first : first + 1, :]
            c_sc[2, row : row + 1, :] = l_sc[last : last + 1, :]
            c_sc[3, row : row + 1, :] = r_sc[last : last + 1, :]
    side = HALO * COLS
    top[:side, :] = src[0:side, :]
    bot[:side, :] = src[TOK - side : TOK, :]
    for n, ref in enumerate((top, bot)):
        ref[side : side + 16, :] = c_sc[2 * n].astype(BF)
        ref[side + 16 : side + 32, :] = c_sc[2 * n + 1].astype(BF)


EDGE_SHAPES = [
    jax.ShapeDtypeStruct((HALO * COLS + 32, CH), BF),
    jax.ShapeDtypeStruct((HALO * COLS + 32, CH), BF),
    jax.ShapeDtypeStruct((HALO * ROWS, CH), BF),
    jax.ShapeDtypeStruct((HALO * ROWS, CH), BF),
]
EDGE_SCRATCH = [
    pltpu.VMEM((HALO * ROWS, CH), F32),
    pltpu.VMEM((HALO * ROWS, CH), F32),
    pltpu.VMEM((4, 16, CH), F32),
]


def exchange_rows(edges):
    top, bot = edges[:2]
    n = lax.axis_size(ROW_AXES)
    above = lax.ppermute(bot, ROW_AXES, [(i, i + 1) for i in range(n - 1)])
    below = lax.ppermute(top, ROW_AXES, [(i + 1, i) for i in range(n - 1)])
    return above, below


def exchange_cols(edges, above, below):
    left, right = edges[2:]
    n = lax.axis_size(COL_AXES)
    side = HALO * COLS
    right = jnp.concatenate([right, above[side + 16 : side + 32], below[side + 16 : side + 32]])
    left = jnp.concatenate([left, above[side : side + 16], below[side : side + 16]])
    from_left = lax.ppermute(right, COL_AXES, [(i, i + 1) for i in range(n - 1)])
    from_right = lax.ppermute(left, COL_AXES, [(i + 1, i) for i in range(n - 1)])
    return from_left, from_right


def assemble(wide, own, halo, l_sc, r_sc, c_sc):
    above, below, left, right = halo
    edge = HALO * ROWS
    l_sc[...] = left[:edge, :].astype(F32)
    r_sc[...] = right[:edge, :].astype(F32)
    for n in range(2):
        c_sc[2 * n] = left[edge + 16 * n : edge + 16 * (n + 1), :].astype(F32)
        c_sc[2 * n + 1] = right[edge + 16 * n : edge + 16 * (n + 1), :].astype(F32)
    sub = iota((8, CH), 0)

    def put(row, x, lefts, rights):
        x = x.astype(F32).reshape(8, 8, CH)
        for cb in range(8):
            wide[row, HALO + cb] = x[cb]
        for k in range(HALO):
            wide[row, k] = jnp.where(sub == 0, lefts[k], pltpu.roll(x[5 + k], 1, 0))
            wide[row, 11 + k] = jnp.where(sub == 7, rights[k], pltpu.roll(x[k], 7, 0))

    for i in range(HALO):
        row = [k * HALO + i for k in range(HALO)]
        put(
            i,
            above[i * COLS : (i + 1) * COLS, :],
            [c_sc[0, n : n + 1, :] for n in row],
            [c_sc[1, n : n + 1, :] for n in row],
        )
        put(
            HALO + ROWS + i,
            below[i * COLS : (i + 1) * COLS, :],
            [c_sc[2, n : n + 1, :] for n in row],
            [c_sc[3, n : n + 1, :] for n in row],
        )

    def body(a, carry):
        put(
            a + HALO,
            own[pl.ds(pl.multiple_of(a * COLS, COLS), COLS), :],
            [l_sc[pl.ds(k * ROWS + a, 1), :] for k in range(HALO)],
            [r_sc[pl.ds(k * ROWS + a, 1), :] for k in range(HALO)],
        )
        return carry

    lax.fori_loop(0, ROWS, body, 0)


def spread_weights(kernel_ref, w_sc):
    for n in range(KSIZE * KSIZE):
        w_sc[n] = jnp.broadcast_to(kernel_ref[n : n + 1, :], (8, CH))


def conv_rows(wide, w_sc, a, half, flip):
    lanes = pl.ds(half * 128, 128)
    acc = [[wide[a + r + HALO, HALO + cb, :, lanes] for cb in range(8)] for r in range(2)]
    for i in range(KSIZE + 1):
        xs = [wide[a + i, c, :, lanes] for c in range(WIDE)]
        for r in range(2):
            if not 0 <= i - r < KSIZE:
                continue
            for j in range(KSIZE):
                n = (i - r) * KSIZE + j
                w = w_sc[KSIZE * KSIZE - 1 - n if flip else n, :, lanes]
                acc[r] = [acc[r][cb] + xs[cb + j] * w for cb in range(8)]
    return acc


def norm_rows(x):
    centre = x - jnp.sum(x, axis=-1, keepdims=True) * (1.0 / CH)
    variance = jnp.sum(centre * centre, axis=-1, keepdims=True) * (1.0 / CH)
    inverse = lax.rsqrt(variance + norm_eps)
    return centre * inverse, inverse


def embed_kernel(pixels, weights, bias, emb, z_ref, top, bot, left, right, w_sc, l_sc, r_sc, c_sc):
    out = iota((256, 256), 0)
    spread = (((out & 7) * 8 + ((out >> 3) & 7)) * 4 + (out >> 6)) == iota((256, 256), 1)
    spread = jnp.where(spread, 1.0, 0.0).astype(BF)
    by_cell = dot(spread, pixels[...], NT).astype(BF)
    row = iota((512, 384), 0)
    fu = row & 15
    target = (fu >> 2) * 128 + (row >> 4) * 4 + (fu & 3)
    order = jnp.where((target == iota((512, 384), 1)) & (fu < 12), 1.0, 0.0).astype(BF)
    z = dot(by_cell, order, NT).astype(BF)
    for g in range(4):
        for v in range(4):
            z_ref[g * 64 : (g + 1) * 64, v * 128 : (v + 1) * 128] = z[
                v * 64 : (v + 1) * 64, g * 128 : (g + 1) * 128
            ]
    w_sc[...] = jnp.zeros_like(w_sc)
    for v in range(4):
        for a8 in range(8):
            first = v * 128 + a8 * 16
            w_sc[first : first + 16, a8 * CH : (a8 + 1) * CH] = weights[v]
    for a8 in range(8):
        block = dot(z_ref[...], w_sc[:, a8 * CH : (a8 + 1) * CH]) + bias[...]
        block = block.astype(BF)
        for g in range(4):
            a = g * 8 + a8
            emb[a * COLS : (a + 1) * COLS, :] = block[g * 64 : (g + 1) * 64, :]
    write_edges(emb, top, bot, left, right, l_sc, r_sc, c_sc)


def embed(pixels, patch_weight, patch_bias):
    weights = patch_weight.reshape(12, 4, CH).transpose(1, 0, 2)
    weights = jnp.pad(weights, ((0, 0), (0, 4), (0, 0)))
    outs = pl.pallas_call(
        embed_kernel,
        name="embed",
        out_shape=[
            jax.ShapeDtypeStruct((TOK, CH), BF),
            jax.ShapeDtypeStruct((256, 512), BF),
        ]
        + EDGE_SHAPES,
        scratch_shapes=[pltpu.VMEM((512, 2048), BF)] + EDGE_SCRATCH,
        compiler_params=VMEM,
    )(pixels.reshape(384, 256), weights, patch_bias.reshape(1, CH))
    return outs[0], outs[1], outs[2:]


def conv_kernel_body(emb, above, below, lh, rh, kern, gain, wide, centred, inverse, normed, w_sc, l_sc, r_sc, c_sc):
    assemble(wide, emb, (above, below, lh, rh), l_sc, r_sc, c_sc)
    spread_weights(kern, w_sc)

    def body(n, carry):
        for half in range(2):
            acc = conv_rows(wide, w_sc, 2 * n, half, False)
            for r in range(2):
                for cb in range(8):
                    rows = pl.ds(pl.multiple_of((2 * n + r) * COLS + cb * 8, 8), 8)
                    centred[rows, pl.ds(half * 128, 128)] = acc[r][cb]
        return carry

    lax.fori_loop(0, ROWS // 2, body, 0)

    def norm_body(n, carry):
        rows = pl.ds(pl.multiple_of(n * BLOCK, BLOCK), BLOCK)
        out, inv = norm_rows(centred[rows, :])
        centred[rows, :] = out
        inverse[rows, :] = jnp.broadcast_to(inv, (BLOCK, 128))
        normed[rows, :] = (out * gain[...]).astype(BF)
        return carry

    lax.fori_loop(0, TOK // BLOCK, norm_body, 0)


def conv_forward(emb, halo, conv_kernel, gain):
    return pl.pallas_call(
        conv_kernel_body,
        name="conv_forward",
        out_shape=[
            jax.ShapeDtypeStruct((ROWS + 2 * HALO, WIDE, 8, CH), F32),
            jax.ShapeDtypeStruct((TOK, CH), F32),
            jax.ShapeDtypeStruct((TOK, 128), F32),
            jax.ShapeDtypeStruct((TOK, CH), BF),
        ],
        scratch_shapes=[pltpu.VMEM((KSIZE * KSIZE, 8, CH), F32)] + EDGE_SCRATCH,
        compiler_params=VMEM,
    )(emb, *halo, conv_kernel, gain)


CHUNK = 1024
GROUP = 2
ACHUNK = 1024
WIDTH = 4
SCALE = 128**-0.5
SCALE2 = SCALE * 1.4426950408889634
COST = pl.CostEstimate(flops=14_000_000_000, transcendentals=0, bytes_accessed=16_000_000)


def lane(n):
    return slice(n * 128, (n + 1) * 128)


def attend_kernel(normed, wk, wv, q, up, k_out, v_out, weighted, stats, s_sc):
    step = pl.program_id(0)
    peak = [None] * WIDTH
    level = None
    for n in range(WIDTH + 1):
        total = jnp.zeros((1, 256), F32)
        acc = jnp.zeros((128, 256), F32)
        if n < WIDTH:
            w = jnp.concatenate([wk[:, lane(n)], wv[:, lane(n)]], axis=1)
        for c in range(TOK // ACHUNK):
            rows = slice(c * ACHUNK, (c + 1) * ACHUNK)
            if n < WIDTH:
                kv = dot(normed[rows, :], w).astype(BF)
                k_out[rows, lane(n)] = kv[:, :128]
                v_out[rows, lane(n)] = kv[:, 128:]
                s = dot(kv[:, :128], q[:, lane(n)], NT)
                s_sc[n % 2, rows, :] = s
                top = jnp.max(s, axis=0, keepdims=True)
                peak[n] = top if peak[n] is None else jnp.maximum(peak[n], top)
            if n > 0:
                p = jnp.exp2(s_sc[1 - n % 2, rows, :] * SCALE2 - level)
                total = total + jnp.sum(p, axis=0, keepdims=True)
                acc = acc + dot(v_out[rows, lane(n - 1)], p.astype(BF), TN)
        if n > 0:
            weighted[n - 1] = acc
            dots = jnp.sum(acc * up[:, lane(n - 1)].astype(F32).T, axis=0, keepdims=True)
            h = step * WIDTH + n - 1
            stats[0, pl.ds(h, 1), :] = level
            stats[1, pl.ds(h, 1), :] = total
            stats[2, pl.ds(h, 1), :] = dots
        if n < WIDTH:
            level = peak[n] * SCALE2


def whole(shape):
    return pl.BlockSpec(shape, lambda h: (0,) * len(shape))


def column(rows, first=0):
    return pl.BlockSpec((rows, 128 * WIDTH), lambda h: (0, h + first))


def attend(normed, kv_weight, latents, d_attended):
    return pl.pallas_call(
        attend_kernel,
        name="attend",
        grid=(HEADS // WIDTH,),
        in_specs=[
            whole((TOK, CH)),
            column(CH),
            column(CH, HEADS // WIDTH),
            column(256),
            column(256),
        ],
        out_specs=[
            column(TOK),
            column(TOK),
            pl.BlockSpec((WIDTH, 128, 256), lambda h: (h, 0, 0)),
            whole((3, HEADS, 256)),
        ],
        out_shape=[
            jax.ShapeDtypeStruct((TOK, 1024), BF),
            jax.ShapeDtypeStruct((TOK, 1024), BF),
            jax.ShapeDtypeStruct((HEADS, 128, 256), F32),
            jax.ShapeDtypeStruct((3, HEADS, 256), F32),
        ],
        scratch_shapes=[pltpu.VMEM((2, TOK, 256), F32)],
        compiler_params=VMEM,
    )(normed, kv_weight, kv_weight, latents, d_attended)


STEPS = HEADS // GROUP


def step_at(step, core):
    return (step + STEPS // 2 * (1 - core[0])) & (STEPS - 1)


def attend_grad_kernel(
    core, normed, k_in, v_in, wk, wv, q, up, lse, dots, factor, weighted, centred, inverse, gain,
    send, keep, d_mixed, gain_grad, top, bot, left, right, dn_sc, nt_sc, l_sc, r_sc, c_sc,
):
    step = pl.program_id(0)
    first = step_at(step, core) * GROUP

    @pl.when(step == 0)
    def _():
        nt_sc[...] = normed[...].T
        dn_sc[...] = jnp.zeros_like(dn_sc)

    w = jnp.concatenate([x[:, lane(n)] for n in range(GROUP) for x in (wk, wv)], axis=1)
    level = [lse[pl.ds(first + n, 1), :] for n in range(GROUP)]
    row_dots = [dots[pl.ds(first + n, 1), :] for n in range(GROUP)]
    qg = [jnp.zeros((128, 256), F32)] * GROUP
    wg = jnp.zeros((256, 256 * GROUP), F32)
    units = [(c, n) for c in range(TOK // CHUNK) for n in range(GROUP)]

    def products(c, n):
        rows = slice(c * CHUNK, (c + 1) * CHUNK)
        return (
            dot(k_in[rows, lane(n)], q[:, lane(n)], NT),
            dot(v_in[rows, lane(n)], up[:, lane(n)], NT),
        )

    d_proj = []
    ahead = products(*units[0])
    for at, (c, n) in enumerate(units):
        rows = slice(c * CHUNK, (c + 1) * CHUNK)
        s, dp = ahead
        if at + 1 < len(units):
            ahead = products(*units[at + 1])
        p = jnp.exp2(s * SCALE2 - level[n])
        ds = (p * (dp - row_dots[n])).astype(BF)
        qg[n] = qg[n] + dot(k_in[rows, lane(n)], ds, TN)
        d_proj.append((dot(ds, q[:, lane(n)]) * SCALE).astype(BF))
        d_proj.append(dot(p.astype(BF), up[:, lane(n)]).astype(BF))
        if n == GROUP - 1:
            d_proj = jnp.concatenate(d_proj, axis=1)
            wg = wg + dot(nt_sc[:, rows], d_proj)
            dn_sc[rows, :] += dot(d_proj, w, NT)
            d_proj = []
    att = [(weighted[n] * factor[pl.ds(first + n, 1), :]).T for n in range(GROUP)]
    qg = [(x * SCALE).T for x in qg]

    def put(out):
        for n in range(GROUP):
            out[0, n] = att[n]
            out[1, n] = qg[n]
            out[2, n] = wg[:, lane(2 * n)]
            out[3, n] = wg[:, lane(2 * n + 1)]

    @pl.when(step < STEPS // 2)
    def _():
        put(send)

    @pl.when(step >= STEPS // 2)
    def _():
        put(keep)

    @pl.when(step == STEPS - 1)
    def _():
        def body(n, total):
            rows = pl.ds(pl.multiple_of(n * BLOCK, BLOCK), BLOCK)
            x = centred[rows, :]
            inv = inverse[rows, :]
            dn = dn_sc[rows, :]
            total = total + jnp.sum(dn * x, axis=0, keepdims=True)
            g = dn * gain[...]
            mean = jnp.sum(g, axis=-1, keepdims=True) * (1.0 / CH)
            slope = jnp.sum(g * x, axis=-1, keepdims=True) * (1.0 / CH)
            inv = jnp.concatenate([inv, inv], axis=1)
            d_mixed[rows, :] = (inv * (g - mean - x * slope)).astype(BF)
            return total

        gain_grad[...] = lax.fori_loop(0, TOK // BLOCK, body, jnp.zeros((1, CH), F32))
        write_edges(d_mixed, top, bot, left, right, l_sc, r_sc, c_sc)


def attend_grad(
    core, normed, k, v, kv_weight, latents, d_attended, lse, dots, factor, weighted, centred, inverse, gain
):
    def full(shape):
        return pl.BlockSpec(shape, lambda n, core: (0,) * len(shape))

    def head(rows, first=0):
        return pl.BlockSpec((rows, 128 * GROUP), lambda n, core: (0, step_at(n, core) + first))

    half = STEPS // 2
    block = (4, GROUP, 256, 128)
    part = jax.ShapeDtypeStruct((4, HEADS // 2, 256, 128), F32)
    outs = pl.pallas_call(
        attend_grad_kernel,
        name="attend_grad",
        grid_spec=pltpu.PrefetchScalarGridSpec(
            num_scalar_prefetch=1,
            grid=(STEPS,),
            in_specs=[
                full((TOK, CH)),
                head(TOK),
                head(TOK),
                head(CH),
                head(CH, STEPS),
                head(256),
                head(256),
                full((HEADS, 256)),
                full((HEADS, 256)),
                full((HEADS, 256)),
                pl.BlockSpec((GROUP, 128, 256), lambda n, core: (step_at(n, core), 0, 0)),
                full((TOK, CH)),
                full((TOK, 128)),
                full((1, CH)),
            ],
            out_specs=[
                pl.BlockSpec(block, lambda n, core: (0, jnp.minimum(n, half - 1), 0, 0)),
                pl.BlockSpec(block, lambda n, core: (0, jnp.maximum(n - half, 0), 0, 0)),
                full((TOK, CH)),
                full((1, CH)),
            ]
            + [full(s.shape) for s in EDGE_SHAPES],
            scratch_shapes=[pltpu.VMEM((TOK, CH), F32), pltpu.VMEM((CH, TOK), BF)] + EDGE_SCRATCH,
        ),
        out_shape=[
            part,
            part,
            jax.ShapeDtypeStruct((TOK, CH), BF),
            jax.ShapeDtypeStruct((1, CH), F32),
        ]
        + EDGE_SHAPES,
        compiler_params=VMEM,
        cost_estimate=COST,
    )(core, normed, k, v, kv_weight, kv_weight, latents, d_attended, lse, dots, factor, weighted, centred, inverse, gain)
    return outs[:4], outs[4:]


def kernel_grad_body(wide, d_mixed, out, d_sc):
    d_sc[...] = d_mixed[...].astype(F32)
    for half in range(2):
        lanes = pl.ds(half * 128, 128)
        for i in range(KSIZE):

            def body(n, acc):
                acc = list(acc)
                for r in range(4):
                    a = 4 * n + r
                    xs = [wide[a + i, c, :, lanes] for c in range(WIDE)]
                    base = pl.multiple_of(a * COLS, COLS)
                    ds = [d_sc[pl.ds(base + cb * 8, 8), lanes] for cb in range(8)]
                    for cb in range(8):
                        for j in range(KSIZE):
                            acc[j] = acc[j] + xs[cb + j] * ds[cb]
                return tuple(acc)

            zero = jnp.zeros((8, 128), F32)
            acc = lax.fori_loop(0, ROWS // 4, body, (zero,) * KSIZE)
            for j in range(KSIZE):
                n = i * KSIZE + j
                out[n : n + 1, lanes] = jnp.sum(acc[j], axis=0, keepdims=True)


def kernel_grad(wide, d_mixed):
    return pl.pallas_call(
        kernel_grad_body,
        name="kernel_grad",
        out_shape=jax.ShapeDtypeStruct((KSIZE * KSIZE, CH), F32),
        scratch_shapes=[pltpu.VMEM((TOK, CH), F32)],
        compiler_params=VMEM,
        cost_estimate=COST,
    )(wide, d_mixed)


def conv_back_body(d_mixed, above, below, lh, rh, kern, z, kern_grad, gain_grad, small, wide, d_sc, w_sc, l_sc, r_sc, c_sc):
    assemble(wide, d_mixed, (above, below, lh, rh), l_sc, r_sc, c_sc)
    spread_weights(kern, w_sc)
    zero = jnp.zeros((8, 128), F32)

    def body(n, bias):
        bias = list(bias)
        for half in range(2):
            accs = conv_rows(wide, w_sc, 2 * n, half, True)
            for r in range(2):
                a = 2 * n + r
                acc = jnp.concatenate(accs[r], axis=0).astype(BF)
                d_sc[a & 7, pl.ds(pl.multiple_of((a >> 3) * 64, 64), 64), pl.ds(half * 128, 128)] = acc
                bias[half] = bias[half] + jnp.sum(acc.astype(F32).reshape(8, 8, 128), axis=0)
        return tuple(bias)

    bias = lax.fori_loop(0, ROWS // 2, body, (zero, zero))
    for half in range(2):
        small[98, :, half * 128 : (half + 1) * 128] = jnp.sum(bias[half], axis=0, keepdims=True)
    for n in range(KSIZE * KSIZE):
        small[48 + n] = kern_grad[n : n + 1, :]
    small[97] = gain_grad[...]
    small[99:128] = jnp.zeros((29, 1, CH), F32)
    total = [jnp.zeros((16, CH), F32) for _ in range(4)]
    for a8 in range(8):
        part = dot(z[...], d_sc[a8], TN)
        for v in range(4):
            first = v * 128 + a8 * 16
            total[v] = total[v] + part[first : first + 16, :]
    for v in range(4):
        for fu in range(12):
            small[fu * 4 + v] = total[v][fu : fu + 1, :]


def conv_back(d_mixed, halo, conv_kernel, z, kern_grad, gain_grad):
    return pl.pallas_call(
        conv_back_body,
        name="conv_back",
        out_shape=jax.ShapeDtypeStruct((128, 1, CH), F32),
        scratch_shapes=[
            pltpu.VMEM((ROWS + 2 * HALO, WIDE, 8, CH), F32),
            pltpu.VMEM((8, 256, CH), BF),
            pltpu.VMEM((KSIZE * KSIZE, 8, CH), F32),
        ]
        + EDGE_SCRATCH,
        compiler_params=VMEM,
        cost_estimate=COST,
    )(d_mixed, *halo, conv_kernel, z, kern_grad, gain_grad)


CHIPS = ("z", "x", "y")
ALL = ("z", "core", "x", "y")
PAIR = [(0, 1), (1, 0)]
STAGES = (("z", "core"), ("x", "y"))


def gather(x, axes):
    n = lax.axis_size(axes)
    copies = jnp.broadcast_to(x[None], (n,) + x.shape)
    return lax.all_to_all(copies, axes, 0, 0, tiled=True)


def combine_stats(stats):
    for axes in STAGES:
        group = gather(stats, axes)
        peak = jnp.max(group[:, 0], axis=0)
        factors = jnp.exp2(group[:, 0] - peak)
        total = jnp.sum(group[:, 1] * factors, axis=0)
        dots = jnp.sum(group[:, 2] * factors, axis=0)
        stats = jnp.stack([peak, total, dots])
    return stats


def collect_body(core, own, other, attended, q_grad, kv_grad):
    h = pl.program_id(0)
    mine = (h // (HEADS // 2)) == core[0]

    def put(x):
        attended[...] = x[0, 0].astype(F32)
        q_grad[...] = x[1, 0].astype(F32)
        kv_grad[:, pl.ds(pl.multiple_of(h * 128, 128), 128)] = x[2, 0].astype(F32)
        kv_grad[:, pl.ds(pl.multiple_of((HEADS + h) * 128, 128), 128)] = x[3, 0].astype(F32)

    @pl.when(mine)
    def _():
        put(own)

    @pl.when(jnp.logical_not(mine))
    def _():
        put(other)


def collect(core, own, other):
    shape = (4, HEADS // 2, 256, 128)
    block = pl.BlockSpec((4, 1, 256, 128), lambda h, core: (0, h % (HEADS // 2), 0, 0))
    heads = pl.BlockSpec((256, 128), lambda h, core: (0, h))
    return pl.pallas_call(
        collect_body,
        name="collect",
        grid_spec=pltpu.PrefetchScalarGridSpec(
            num_scalar_prefetch=1,
            grid=(HEADS,),
            in_specs=[block, block],
            out_specs=[heads, heads, pl.BlockSpec((256, 2048), lambda h, core: (0, 0))],
        ),
        out_shape=[
            jax.ShapeDtypeStruct((256, 1024), F32),
            jax.ShapeDtypeStruct((256, 1024), F32),
            jax.ShapeDtypeStruct((256, 2048), F32),
        ],
        compiler_params=VMEM,
    )(core, own.reshape(shape), other.reshape(shape))


def split_small_body(small, patch, kern, gain, bias):
    for n in range(48):
        patch[n : n + 1, :] = small[n]
    for n in range(KSIZE * KSIZE):
        kern[n : n + 1, :] = small[48 + n]
    gain[...] = small[97, 0]
    bias[...] = small[98, 0]


def split_small(small):
    return pl.pallas_call(
        split_small_body,
        name="split_small",
        out_shape=[
            jax.ShapeDtypeStruct((48, CH), F32),
            jax.ShapeDtypeStruct((KSIZE * KSIZE, CH), F32),
            jax.ShapeDtypeStruct((CH,), F32),
            jax.ShapeDtypeStruct((CH,), F32),
        ],
        compiler_params=VMEM,
    )(small)


def block_sum(parts):
    return jnp.sum(parts.astype(F32), axis=0)


def copies(x):
    return jnp.broadcast_to(x.astype(WIRE)[None], (64,) + x.shape)


def send(x):
    return lax.all_to_all(x, CHIPS, 0, 0, tiled=True)


def send_all(x):
    return lax.all_to_all(x, ALL, 0, 0, tiled=True)


def tie(x, *others):
    return lax.optimization_barrier((x,) + others)


def per_device(
    pixels, patch_weight, patch_bias, conv_kernel, norm_gain, kv_weight, latents, d_attended
):
    gain = norm_gain.reshape(1, CH)
    emb, z, edges = embed(pixels, patch_weight, patch_bias)
    rows = exchange_rows(edges)
    halo = rows + exchange_cols(edges, *rows)
    wide, centred, inverse, normed = conv_forward(emb, halo, conv_kernel, gain)
    k, v, weighted, local = attend(normed, kv_weight, latents, d_attended)
    stats = combine_stats(local)
    lse = stats[0] + jnp.log2(stats[1])
    row_dots = stats[2] / stats[1]
    factor = jnp.exp2(local[0] - stats[0]) / stats[1]
    core = lax.axis_index("core").astype(jnp.int32).reshape(1)
    (away, keep, d_mixed, gain_grad), d_edges = attend_grad(
        core, normed, k, v, kv_weight, latents, d_attended, lse, row_dots, factor, weighted,
        centred, inverse, gain,
    )
    d_rows = exchange_rows(d_edges)
    message = (keep + lax.ppermute(away, "core", PAIR)).astype(BF).reshape(64, 64, 128)
    d_mixed, message, *d_rows = tie(d_mixed, message, *d_rows)
    message = send(message)
    kern = kernel_grad(wide, d_mixed)
    d_mixed, message, kern = tie(d_mixed, message, kern)
    message = copies(block_sum(message))
    d_mixed, message, *d_rows = tie(d_mixed, message, *d_rows)
    message = send(message)
    d_cols = exchange_cols(d_edges, *d_rows)
    small = conv_back(d_mixed, tuple(d_rows) + tuple(d_cols), conv_kernel, z, kern, gain_grad)
    small, message = tie(small, message)
    mine = block_sum(send_all(small))
    small = send_all(jnp.broadcast_to(mine[None], (128,) + mine.shape))
    outs = collect(core, message, lax.ppermute(message, "core", PAIR))
    small, *outs = tie(small, *outs)
    patch, kern, gain, bias = split_small(small)
    return (*outs, gain, kern, patch, bias)


def solution(mesh):
    split = Mesh(mesh.devices.reshape(4, 2, 4, 4), ("z", "core", "x", "y"))
    return jax.shard_map(
        per_device,
        mesh=split,
        in_specs=(P(None, ("z", "core"), ("x", "y")), P(), P(), P(), P(), P(), P(), P()),
        out_specs=(P(), P(), P(), P(), P(), P(), P()),
        check_vma=False,
    )
```

```python
import jax
import jax.numpy as jnp
from jax import lax
from jax.experimental import pallas as pl
from jax.experimental.pallas import tpu as pltpu
from jax.sharding import Mesh
from jax.sharding import PartitionSpec as P

PATCH = 4
KSIZE = 7
HEADS = 8
HALO = 3
norm_eps = 1e-05
BF = jnp.bfloat16
F32 = jnp.float32
NT = (((1,), (1,)), ((), ()))
TN = (((0,), (0,)), ((), ()))
NN = (((1,), (0,)), ((), ()))
ROWS = 32
COLS = 64
CH = 256
TOK = ROWS * COLS
WIDE = 14
BLOCK = 1024
WIRE = BF
ROW_AXES = ("z", "core")
COL_AXES = ("x", "y")
VMEM = pltpu.CompilerParams(vmem_limit_bytes=58 << 20)


def dot(a, b, dims=NN):
    return lax.dot_general(a, b, dims, preferred_element_type=F32)


def iota(shape, dim):
    return lax.broadcasted_iota(jnp.int32, shape, dim)


def write_edges(src, top, bot, left, right, l_sc, r_sc, c_sc):
    for a in range(ROWS):
        low = src[a * COLS : a * COLS + 32, :].astype(F32)
        high = src[a * COLS + 32 : a * COLS + 64, :].astype(F32)
        for k in range(HALO):
            l_sc[k * ROWS + a : k * ROWS + a + 1, :] = low[8 * k : 8 * k + 1, :]
            r_sc[k * ROWS + a : k * ROWS + a + 1, :] = high[8 * k + 15 : 8 * k + 16, :]
    left[...] = l_sc[...].astype(BF)
    right[...] = r_sc[...].astype(BF)
    c_sc[...] = jnp.zeros_like(c_sc)
    for k in range(HALO):
        for i in range(HALO):
            first = k * ROWS + i
            last = k * ROWS + ROWS - HALO + i
            row = k * HALO + i
            c_sc[0, row : row + 1, :] = l_sc[first : first + 1, :]
            c_sc[1, row : row + 1, :] = r_sc[first : first + 1, :]
            c_sc[2, row : row + 1, :] = l_sc[last : last + 1, :]
            c_sc[3, row : row + 1, :] = r_sc[last : last + 1, :]
    side = HALO * COLS
    top[:side, :] = src[0:side, :]
    bot[:side, :] = src[TOK - side : TOK, :]
    for n, ref in enumerate((top, bot)):
        ref[side : side + 16, :] = c_sc[2 * n].astype(BF)
        ref[side + 16 : side + 32, :] = c_sc[2 * n + 1].astype(BF)


EDGE_SHAPES = [
    jax.ShapeDtypeStruct((HALO * COLS + 32, CH), BF),
    jax.ShapeDtypeStruct((HALO * COLS + 32, CH), BF),
    jax.ShapeDtypeStruct((HALO * ROWS, CH), BF),
    jax.ShapeDtypeStruct((HALO * ROWS, CH), BF),
]
EDGE_SCRATCH = [
    pltpu.VMEM((HALO * ROWS, CH), F32),
    pltpu.VMEM((HALO * ROWS, CH), F32),
    pltpu.VMEM((4, 16, CH), F32),
]


def exchange_rows(edges):
    top, bot = edges[:2]
    n = lax.axis_size(ROW_AXES)
    above = lax.ppermute(bot, ROW_AXES, [(i, i + 1) for i in range(n - 1)])
    below = lax.ppermute(top, ROW_AXES, [(i + 1, i) for i in range(n - 1)])
    return above, below


def exchange_cols(edges, above, below):
    left, right = edges[2:]
    n = lax.axis_size(COL_AXES)
    side = HALO * COLS
    right = jnp.concatenate([right, above[side + 16 : side + 32], below[side + 16 : side + 32]])
    left = jnp.concatenate([left, above[side : side + 16], below[side : side + 16]])
    from_left = lax.ppermute(right, COL_AXES, [(i, i + 1) for i in range(n - 1)])
    from_right = lax.ppermute(left, COL_AXES, [(i + 1, i) for i in range(n - 1)])
    return from_left, from_right


def assemble(wide, own, halo, l_sc, r_sc, c_sc):
    above, below, left, right = halo
    edge = HALO * ROWS
    l_sc[...] = left[:edge, :].astype(F32)
    r_sc[...] = right[:edge, :].astype(F32)
    for n in range(2):
        c_sc[2 * n] = left[edge + 16 * n : edge + 16 * (n + 1), :].astype(F32)
        c_sc[2 * n + 1] = right[edge + 16 * n : edge + 16 * (n + 1), :].astype(F32)
    sub = iota((8, CH), 0)

    def put(row, x, lefts, rights):
        x = x.astype(F32).reshape(8, 8, CH)
        for cb in range(8):
            wide[row, HALO + cb] = x[cb]
        for k in range(HALO):
            wide[row, k] = jnp.where(sub == 0, lefts[k], pltpu.roll(x[5 + k], 1, 0))
            wide[row, 11 + k] = jnp.where(sub == 7, rights[k], pltpu.roll(x[k], 7, 0))

    for i in range(HALO):
        row = [k * HALO + i for k in range(HALO)]
        put(
            i,
            above[i * COLS : (i + 1) * COLS, :],
            [c_sc[0, n : n + 1, :] for n in row],
            [c_sc[1, n : n + 1, :] for n in row],
        )
        put(
            HALO + ROWS + i,
            below[i * COLS : (i + 1) * COLS, :],
            [c_sc[2, n : n + 1, :] for n in row],
            [c_sc[3, n : n + 1, :] for n in row],
        )

    def body(a, carry):
        put(
            a + HALO,
            own[pl.ds(pl.multiple_of(a * COLS, COLS), COLS), :],
            [l_sc[pl.ds(k * ROWS + a, 1), :] for k in range(HALO)],
            [r_sc[pl.ds(k * ROWS + a, 1), :] for k in range(HALO)],
        )
        return carry

    lax.fori_loop(0, ROWS, body, 0)


def spread_weights(kernel_ref, w_sc):
    for n in range(KSIZE * KSIZE):
        w_sc[n] = jnp.broadcast_to(kernel_ref[n : n + 1, :], (8, CH))


def conv_rows(wide, w_sc, a, half, flip):
    lanes = pl.ds(half * 128, 128)
    acc = [[wide[a + r + HALO, HALO + cb, :, lanes] for cb in range(8)] for r in range(2)]
    for i in range(KSIZE + 1):
        xs = [wide[a + i, c, :, lanes] for c in range(WIDE)]
        for r in range(2):
            if not 0 <= i - r < KSIZE:
                continue
            for j in range(KSIZE):
                n = (i - r) * KSIZE + j
                w = w_sc[KSIZE * KSIZE - 1 - n if flip else n, :, lanes]
                acc[r] = [acc[r][cb] + xs[cb + j] * w for cb in range(8)]
    return acc


def norm_rows(x):
    centre = x - jnp.sum(x, axis=-1, keepdims=True) * (1.0 / CH)
    variance = jnp.sum(centre * centre, axis=-1, keepdims=True) * (1.0 / CH)
    inverse = lax.rsqrt(variance + norm_eps)
    return centre * inverse, inverse


def embed_kernel(pixels, weights, bias, emb, z_ref, top, bot, left, right, w_sc, l_sc, r_sc, c_sc):
    out = iota((256, 256), 0)
    spread = (((out & 7) * 8 + ((out >> 3) & 7)) * 4 + (out >> 6)) == iota((256, 256), 1)
    spread = jnp.where(spread, 1.0, 0.0).astype(BF)
    by_cell = dot(spread, pixels[...], NT).astype(BF)
    row = iota((512, 384), 0)
    fu = row & 15
    target = (fu >> 2) * 128 + (row >> 4) * 4 + (fu & 3)
    order = jnp.where((target == iota((512, 384), 1)) & (fu < 12), 1.0, 0.0).astype(BF)
    z = dot(by_cell, order, NT).astype(BF)
    for g in range(4):
        for v in range(4):
            z_ref[g * 64 : (g + 1) * 64, v * 128 : (v + 1) * 128] = z[
                v * 64 : (v + 1) * 64, g * 128 : (g + 1) * 128
            ]
    w_sc[...] = jnp.zeros_like(w_sc)
    for v in range(4):
        for a8 in range(8):
            first = v * 128 + a8 * 16
            w_sc[first : first + 16, a8 * CH : (a8 + 1) * CH] = weights[v]
    for a8 in range(8):
        block = dot(z_ref[...], w_sc[:, a8 * CH : (a8 + 1) * CH]) + bias[...]
        block = block.astype(BF)
        for g in range(4):
            a = g * 8 + a8
            emb[a * COLS : (a + 1) * COLS, :] = block[g * 64 : (g + 1) * 64, :]
    write_edges(emb, top, bot, left, right, l_sc, r_sc, c_sc)


def embed(pixels, patch_weight, patch_bias):
    weights = patch_weight.reshape(12, 4, CH).transpose(1, 0, 2)
    weights = jnp.pad(weights, ((0, 0), (0, 4), (0, 0)))
    outs = pl.pallas_call(
        embed_kernel,
        name="embed",
        out_shape=[
            jax.ShapeDtypeStruct((TOK, CH), BF),
            jax.ShapeDtypeStruct((256, 512), BF),
        ]
        + EDGE_SHAPES,
        scratch_shapes=[pltpu.VMEM((512, 2048), BF)] + EDGE_SCRATCH,
        compiler_params=VMEM,
    )(pixels.reshape(384, 256), weights, patch_bias.reshape(1, CH))
    return outs[0], outs[1], outs[2:]


def conv_kernel_body(emb, above, below, lh, rh, kern, gain, wide, centred, inverse, normed, w_sc, l_sc, r_sc, c_sc):
    assemble(wide, emb, (above, below, lh, rh), l_sc, r_sc, c_sc)
    spread_weights(kern, w_sc)

    def body(n, carry):
        for half in range(2):
            acc = conv_rows(wide, w_sc, 2 * n, half, False)
            for r in range(2):
                for cb in range(8):
                    rows = pl.ds(pl.multiple_of((2 * n + r) * COLS + cb * 8, 8), 8)
                    centred[rows, pl.ds(half * 128, 128)] = acc[r][cb]
        return carry

    lax.fori_loop(0, ROWS // 2, body, 0)

    def norm_body(n, carry):
        rows = pl.ds(pl.multiple_of(n * BLOCK, BLOCK), BLOCK)
        out, inv = norm_rows(centred[rows, :])
        centred[rows, :] = out
        inverse[rows, :] = jnp.broadcast_to(inv, (BLOCK, 128))
        normed[rows, :] = (out * gain[...]).astype(BF)
        return carry

    lax.fori_loop(0, TOK // BLOCK, norm_body, 0)


def conv_forward(emb, halo, conv_kernel, gain):
    return pl.pallas_call(
        conv_kernel_body,
        name="conv_forward",
        out_shape=[
            jax.ShapeDtypeStruct((ROWS + 2 * HALO, WIDE, 8, CH), F32),
            jax.ShapeDtypeStruct((TOK, CH), F32),
            jax.ShapeDtypeStruct((TOK, 128), F32),
            jax.ShapeDtypeStruct((TOK, CH), BF),
        ],
        scratch_shapes=[pltpu.VMEM((KSIZE * KSIZE, 8, CH), F32)] + EDGE_SCRATCH,
        compiler_params=VMEM,
    )(emb, *halo, conv_kernel, gain)


CHUNK = 1024
GROUP = 2
ACHUNK = 1024
WIDTH = 4
SCALE = 128**-0.5
SCALE2 = SCALE * 1.4426950408889634
COST = pl.CostEstimate(flops=14_000_000_000, transcendentals=0, bytes_accessed=16_000_000)


def lane(n):
    return slice(n * 128, (n + 1) * 128)


def attend_kernel(normed, wk, wv, q, up, k_out, v_out, weighted, stats, s_sc):
    step = pl.program_id(0)
    peak = [None] * WIDTH
    level = None
    for n in range(WIDTH + 1):
        total = jnp.zeros((1, 256), F32)
        acc = jnp.zeros((128, 256), F32)
        if n < WIDTH:
            w = jnp.concatenate([wk[:, lane(n)], wv[:, lane(n)]], axis=1)
        for c in range(TOK // ACHUNK):
            rows = slice(c * ACHUNK, (c + 1) * ACHUNK)
            if n < WIDTH:
                kv = dot(normed[rows, :], w).astype(BF)
                k_out[rows, lane(n)] = kv[:, :128]
                v_out[rows, lane(n)] = kv[:, 128:]
                s = dot(kv[:, :128], q[:, lane(n)], NT)
                s_sc[n % 2, rows, :] = s
                top = jnp.max(s, axis=0, keepdims=True)
                peak[n] = top if peak[n] is None else jnp.maximum(peak[n], top)
            if n > 0:
                p = jnp.exp2(s_sc[1 - n % 2, rows, :] * SCALE2 - level)
                total = total + jnp.sum(p, axis=0, keepdims=True)
                acc = acc + dot(v_out[rows, lane(n - 1)], p.astype(BF), TN)
        if n > 0:
            weighted[n - 1] = acc
            dots = jnp.sum(acc * up[:, lane(n - 1)].astype(F32).T, axis=0, keepdims=True)
            h = step * WIDTH + n - 1
            stats[0, pl.ds(h, 1), :] = level
            stats[1, pl.ds(h, 1), :] = total
            stats[2, pl.ds(h, 1), :] = dots
        if n < WIDTH:
            level = peak[n] * SCALE2


def whole(shape):
    return pl.BlockSpec(shape, lambda h: (0,) * len(shape))


def column(rows, first=0):
    return pl.BlockSpec((rows, 128 * WIDTH), lambda h: (0, h + first))


def attend(normed, kv_weight, latents, d_attended):
    return pl.pallas_call(
        attend_kernel,
        name="attend",
        grid=(HEADS // WIDTH,),
        in_specs=[
            whole((TOK, CH)),
            column(CH),
            column(CH, HEADS // WIDTH),
            column(256),
            column(256),
        ],
        out_specs=[
            column(TOK),
            column(TOK),
            pl.BlockSpec((WIDTH, 128, 256), lambda h: (h, 0, 0)),
            whole((3, HEADS, 256)),
        ],
        out_shape=[
            jax.ShapeDtypeStruct((TOK, 1024), BF),
            jax.ShapeDtypeStruct((TOK, 1024), BF),
            jax.ShapeDtypeStruct((HEADS, 128, 256), F32),
            jax.ShapeDtypeStruct((3, HEADS, 256), F32),
        ],
        scratch_shapes=[pltpu.VMEM((2, TOK, 256), F32)],
        compiler_params=VMEM,
    )(normed, kv_weight, kv_weight, latents, d_attended)


STEPS = HEADS // GROUP


def step_at(step, core):
    return (step + STEPS // 2 * (1 - core[0])) & (STEPS - 1)


def attend_grad_kernel(
    core, normed, k_in, v_in, wk, wv, q, up, lse, dots, factor, weighted,
    send, keep, dn_sc, nt_sc,
):
    step = pl.program_id(0)
    first = step_at(step, core) * GROUP

    @pl.when(step == 0)
    def _():
        nt_sc[...] = normed[...].T
        dn_sc[...] = jnp.zeros_like(dn_sc)

    w = jnp.concatenate([x[:, lane(n)] for n in range(GROUP) for x in (wk, wv)], axis=1)
    level = [lse[pl.ds(first + n, 1), :] for n in range(GROUP)]
    row_dots = [dots[pl.ds(first + n, 1), :] for n in range(GROUP)]
    qg = [jnp.zeros((128, 256), F32)] * GROUP
    wg = jnp.zeros((256, 256 * GROUP), F32)
    units = [(c, n) for c in range(TOK // CHUNK) for n in range(GROUP)]

    def products(c, n):
        rows = slice(c * CHUNK, (c + 1) * CHUNK)
        return (
            dot(k_in[rows, lane(n)], q[:, lane(n)], NT),
            dot(v_in[rows, lane(n)], up[:, lane(n)], NT),
        )

    d_proj = []
    ahead = products(*units[0])
    for at, (c, n) in enumerate(units):
        rows = slice(c * CHUNK, (c + 1) * CHUNK)
        s, dp = ahead
        if at + 1 < len(units):
            ahead = products(*units[at + 1])
        p = jnp.exp2(s * SCALE2 - level[n])
        ds = (p * (dp - row_dots[n])).astype(BF)
        qg[n] = qg[n] + dot(k_in[rows, lane(n)], ds, TN)
        d_proj.append((dot(ds, q[:, lane(n)]) * SCALE).astype(BF))
        d_proj.append(dot(p.astype(BF), up[:, lane(n)]).astype(BF))
        if n == GROUP - 1:
            d_proj = jnp.concatenate(d_proj, axis=1)
            wg = wg + dot(nt_sc[:, rows], d_proj)
            dn_sc[rows, :] += dot(d_proj, w, NT)
            d_proj = []
    att = [(weighted[n] * factor[pl.ds(first + n, 1), :]).T for n in range(GROUP)]
    qg = [(x * SCALE).T for x in qg]

    def put(out):
        for n in range(GROUP):
            out[0, n] = att[n]
            out[1, n] = qg[n]
            out[2, n] = wg[:, lane(2 * n)]
            out[3, n] = wg[:, lane(2 * n + 1)]

    @pl.when(step < STEPS // 2)
    def _():
        put(send)

    @pl.when(step >= STEPS // 2)
    def _():
        put(keep)


def norm_grad_kernel(dn_in, centred, inverse, gain, d_mixed, gain_grad, top, bot, left, right, l_sc, r_sc, c_sc):
    def body(n, total):
        rows = pl.ds(pl.multiple_of(n * BLOCK, BLOCK), BLOCK)
        x = centred[rows, :]
        inv = inverse[rows, :]
        dn = dn_in[rows, :]
        total = total + jnp.sum(dn * x, axis=0, keepdims=True)
        g = dn * gain[...]
        mean = jnp.sum(g, axis=-1, keepdims=True) * (1.0 / CH)
        slope = jnp.sum(g * x, axis=-1, keepdims=True) * (1.0 / CH)
        inv = jnp.concatenate([inv, inv], axis=1)
        d_mixed[rows, :] = (inv * (g - mean - x * slope)).astype(BF)
        return total

    gain_grad[...] = lax.fori_loop(0, TOK // BLOCK, body, jnp.zeros((1, CH), F32))
    write_edges(d_mixed, top, bot, left, right, l_sc, r_sc, c_sc)


def norm_grad(dn, centred, inverse, gain):
    outs = pl.pallas_call(
        norm_grad_kernel,
        name="norm_grad",
        out_shape=[jax.ShapeDtypeStruct((TOK, CH), BF), jax.ShapeDtypeStruct((1, CH), F32)] + EDGE_SHAPES,
        scratch_shapes=EDGE_SCRATCH,
        compiler_params=VMEM,
        cost_estimate=COST,
    )(dn, centred, inverse, gain)
    return outs[0], outs[1], outs[2:]


def attend_grad(
    core, normed, k, v, kv_weight, latents, d_attended, lse, dots, factor, weighted
):
    def full(shape):
        return pl.BlockSpec(shape, lambda n, core: (0,) * len(shape))

    def head(rows, first=0):
        return pl.BlockSpec((rows, 128 * GROUP), lambda n, core: (0, step_at(n, core) + first))

    half = STEPS // 2
    block = (4, GROUP, 256, 128)
    part = jax.ShapeDtypeStruct((4, HEADS // 2, 256, 128), F32)
    outs = pl.pallas_call(
        attend_grad_kernel,
        name="attend_grad",
        grid_spec=pltpu.PrefetchScalarGridSpec(
            num_scalar_prefetch=1,
            grid=(STEPS,),
            in_specs=[
                full((TOK, CH)),
                head(TOK),
                head(TOK),
                head(CH),
                head(CH, STEPS),
                head(256),
                head(256),
                full((HEADS, 256)),
                full((HEADS, 256)),
                full((HEADS, 256)),
                pl.BlockSpec((GROUP, 128, 256), lambda n, core: (step_at(n, core), 0, 0)),
            ],
            out_specs=[
                pl.BlockSpec(block, lambda n, core: (0, jnp.minimum(n, half - 1), 0, 0)),
                pl.BlockSpec(block, lambda n, core: (0, jnp.maximum(n - half, 0), 0, 0)),
                full((TOK, CH)),
            ],
            scratch_shapes=[pltpu.VMEM((CH, TOK), BF)],
        ),
        out_shape=[
            part,
            part,
            jax.ShapeDtypeStruct((TOK, CH), F32),
        ],
        compiler_params=VMEM,
        cost_estimate=COST,
    )(core, normed, k, v, kv_weight, kv_weight, latents, d_attended, lse, dots, factor, weighted)
    return outs


def kernel_grad_body(wide, d_mixed, out, d_sc):
    d_sc[...] = d_mixed[...].astype(F32)
    for half in range(2):
        lanes = pl.ds(half * 128, 128)
        for i in range(KSIZE):

            def body(n, acc):
                acc = list(acc)
                for r in range(4):
                    a = 4 * n + r
                    xs = [wide[a + i, c, :, lanes] for c in range(WIDE)]
                    base = pl.multiple_of(a * COLS, COLS)
                    ds = [d_sc[pl.ds(base + cb * 8, 8), lanes] for cb in range(8)]
                    for cb in range(8):
                        for j in range(KSIZE):
                            acc[j] = acc[j] + xs[cb + j] * ds[cb]
                return tuple(acc)

            zero = jnp.zeros((8, 128), F32)
            acc = lax.fori_loop(0, ROWS // 4, body, (zero,) * KSIZE)
            for j in range(KSIZE):
                n = i * KSIZE + j
                out[n : n + 1, lanes] = jnp.sum(acc[j], axis=0, keepdims=True)


def kernel_grad(wide, d_mixed):
    return pl.pallas_call(
        kernel_grad_body,
        name="kernel_grad",
        out_shape=jax.ShapeDtypeStruct((KSIZE * KSIZE, CH), F32),
        scratch_shapes=[pltpu.VMEM((TOK, CH), F32)],
        compiler_params=VMEM,
        cost_estimate=COST,
    )(wide, d_mixed)


def conv_back_body(d_mixed, above, below, lh, rh, kern, z, kern_grad, gain_grad, small, wide, d_sc, w_sc, l_sc, r_sc, c_sc):
    assemble(wide, d_mixed, (above, below, lh, rh), l_sc, r_sc, c_sc)
    spread_weights(kern, w_sc)
    zero = jnp.zeros((8, 128), F32)

    def body(n, bias):
        bias = list(bias)
        for half in range(2):
            accs = conv_rows(wide, w_sc, 2 * n, half, True)
            for r in range(2):
                a = 2 * n + r
                acc = jnp.concatenate(accs[r], axis=0).astype(BF)
                d_sc[a & 7, pl.ds(pl.multiple_of((a >> 3) * 64, 64), 64), pl.ds(half * 128, 128)] = acc
                bias[half] = bias[half] + jnp.sum(acc.astype(F32).reshape(8, 8, 128), axis=0)
        return tuple(bias)

    bias = lax.fori_loop(0, ROWS // 2, body, (zero, zero))
    for half in range(2):
        small[98, :, half * 128 : (half + 1) * 128] = jnp.sum(bias[half], axis=0, keepdims=True)
    for n in range(KSIZE * KSIZE):
        small[48 + n] = kern_grad[n : n + 1, :]
    small[97] = gain_grad[...]
    small[99:128] = jnp.zeros((29, 1, CH), F32)
    total = [jnp.zeros((16, CH), F32) for _ in range(4)]
    for a8 in range(8):
        part = dot(z[...], d_sc[a8], TN)
        for v in range(4):
            first = v * 128 + a8 * 16
            total[v] = total[v] + part[first : first + 16, :]
    for v in range(4):
        for fu in range(12):
            small[fu * 4 + v] = total[v][fu : fu + 1, :]


def conv_back(d_mixed, halo, conv_kernel, z, kern_grad, gain_grad):
    return pl.pallas_call(
        conv_back_body,
        name="conv_back",
        out_shape=jax.ShapeDtypeStruct((128, 1, CH), F32),
        scratch_shapes=[
            pltpu.VMEM((ROWS + 2 * HALO, WIDE, 8, CH), F32),
            pltpu.VMEM((8, 256, CH), BF),
            pltpu.VMEM((KSIZE * KSIZE, 8, CH), F32),
        ]
        + EDGE_SCRATCH,
        compiler_params=VMEM,
        cost_estimate=COST,
    )(d_mixed, *halo, conv_kernel, z, kern_grad, gain_grad)


CHIPS = ("z", "x", "y")
ALL = ("z", "core", "x", "y")
PAIR = [(0, 1), (1, 0)]
STAGES = (("z", "core"), ("x", "y"))


def gather(x, axes):
    n = lax.axis_size(axes)
    copies = jnp.broadcast_to(x[None], (n,) + x.shape)
    return lax.all_to_all(copies, axes, 0, 0, tiled=True)


def combine_stats(stats):
    for axes in STAGES:
        group = gather(stats, axes)
        peak = jnp.max(group[:, 0], axis=0)
        factors = jnp.exp2(group[:, 0] - peak)
        total = jnp.sum(group[:, 1] * factors, axis=0)
        dots = jnp.sum(group[:, 2] * factors, axis=0)
        stats = jnp.stack([peak, total, dots])
    return stats


def collect_body(core, own, other, attended, q_grad, kv_grad):
    h = pl.program_id(0)
    mine = (h // (HEADS // 2)) == core[0]

    def put(x):
        attended[...] = x[0, 0].astype(F32)
        q_grad[...] = x[1, 0].astype(F32)
        kv_grad[:, pl.ds(pl.multiple_of(h * 128, 128), 128)] = x[2, 0].astype(F32)
        kv_grad[:, pl.ds(pl.multiple_of((HEADS + h) * 128, 128), 128)] = x[3, 0].astype(F32)

    @pl.when(mine)
    def _():
        put(own)

    @pl.when(jnp.logical_not(mine))
    def _():
        put(other)


def collect(core, own, other):
    shape = (4, HEADS // 2, 256, 128)
    block = pl.BlockSpec((4, 1, 256, 128), lambda h, core: (0, h % (HEADS // 2), 0, 0))
    heads = pl.BlockSpec((256, 128), lambda h, core: (0, h))
    return pl.pallas_call(
        collect_body,
        name="collect",
        grid_spec=pltpu.PrefetchScalarGridSpec(
            num_scalar_prefetch=1,
            grid=(HEADS,),
            in_specs=[block, block],
            out_specs=[heads, heads, pl.BlockSpec((256, 2048), lambda h, core: (0, 0))],
        ),
        out_shape=[
            jax.ShapeDtypeStruct((256, 1024), F32),
            jax.ShapeDtypeStruct((256, 1024), F32),
            jax.ShapeDtypeStruct((256, 2048), F32),
        ],
        compiler_params=VMEM,
    )(core, own.reshape(shape), other.reshape(shape))


def split_small_body(small, patch, kern, gain, bias):
    for n in range(48):
        patch[n : n + 1, :] = small[n]
    for n in range(KSIZE * KSIZE):
        kern[n : n + 1, :] = small[48 + n]
    gain[...] = small[97, 0]
    bias[...] = small[98, 0]


def split_small(small):
    return pl.pallas_call(
        split_small_body,
        name="split_small",
        out_shape=[
            jax.ShapeDtypeStruct((48, CH), F32),
            jax.ShapeDtypeStruct((KSIZE * KSIZE, CH), F32),
            jax.ShapeDtypeStruct((CH,), F32),
            jax.ShapeDtypeStruct((CH,), F32),
        ],
        compiler_params=VMEM,
    )(small)


def block_sum(parts):
    return jnp.sum(parts.astype(F32), axis=0)


def copies(x):
    return jnp.broadcast_to(x.astype(WIRE)[None], (64,) + x.shape)


def send(x):
    return lax.all_to_all(x, CHIPS, 0, 0, tiled=True)


def send_all(x):
    return lax.all_to_all(x, ALL, 0, 0, tiled=True)


def tie(x, *others):
    return lax.optimization_barrier((x,) + others)


def per_device(
    pixels, patch_weight, patch_bias, conv_kernel, norm_gain, kv_weight, latents, d_attended
):
    gain = norm_gain.reshape(1, CH)
    emb, z, edges = embed(pixels, patch_weight, patch_bias)
    rows = exchange_rows(edges)
    halo = rows + exchange_cols(edges, *rows)
    wide, centred, inverse, normed = conv_forward(emb, halo, conv_kernel, gain)
    k, v, weighted, local = attend(normed, kv_weight, latents, d_attended)
    stats = combine_stats(local)
    lse = stats[0] + jnp.log2(stats[1])
    row_dots = stats[2] / stats[1]
    factor = jnp.exp2(local[0] - stats[0]) / stats[1]
    core = lax.axis_index("core").astype(jnp.int32).reshape(1)
    away, keep, dn = attend_grad(
        core, normed, k, v, kv_weight, latents, d_attended, lse, row_dots, factor, weighted
    )
    away = lax.ppermute(away, "core", PAIR)
    d_mixed, gain_grad, d_edges = norm_grad(dn, centred, inverse, gain)
    d_mixed, away, *d_edges = tie(d_mixed, away, *d_edges)
    message = (keep + away).astype(BF).reshape(64, 64, 128)
    d_mixed, message, *d_edges = tie(d_mixed, message, *d_edges)
    message = send(message)
    d_rows = exchange_rows(d_edges)
    kern = kernel_grad(wide, d_mixed)
    d_mixed, message, kern, *d_rows = tie(d_mixed, message, kern, *d_rows)
    message = copies(block_sum(message))
    d_mixed, message, *d_rows = tie(d_mixed, message, *d_rows)
    message = send(message)
    d_cols = exchange_cols(d_edges, *d_rows)
    small = conv_back(d_mixed, tuple(d_rows) + tuple(d_cols), conv_kernel, z, kern, gain_grad)
    small, message = tie(small, message)
    mine = block_sum(send_all(small))
    small = send_all(jnp.broadcast_to(mine[None], (128,) + mine.shape))
    outs = collect(core, message, lax.ppermute(message, "core", PAIR))
    small, *outs = tie(small, *outs)
    patch, kern, gain, bias = split_small(small)
    return (*outs, gain, kern, patch, bias)


def solution(mesh):
    split = Mesh(mesh.devices.reshape(4, 2, 4, 4), ("z", "core", "x", "y"))
    return jax.shard_map(
        per_device,
        mesh=split,
        in_specs=(P(None, ("z", "core"), ("x", "y")), P(), P(), P(), P(), P(), P(), P()),
        out_specs=(P(), P(), P(), P(), P(), P(), P()),
        check_vma=False,
    )
```

```python
import jax
import jax.numpy as jnp
from jax import lax
from jax.experimental import pallas as pl
from jax.experimental.pallas import tpu as pltpu
from jax.sharding import Mesh
from jax.sharding import PartitionSpec as P

PATCH = 4
KSIZE = 7
HEADS = 8
HALO = 3
norm_eps = 1e-05
BF = jnp.bfloat16
F32 = jnp.float32
NT = (((1,), (1,)), ((), ()))
TN = (((0,), (0,)), ((), ()))
NN = (((1,), (0,)), ((), ()))
ROWS = 32
COLS = 64
CH = 256
TOK = ROWS * COLS
WIDE = 14
BLOCK = 1024
WIRE = BF
ROW_AXES = ("z", "core")
COL_AXES = ("x", "y")
VMEM = pltpu.CompilerParams(vmem_limit_bytes=58 << 20)


def dot(a, b, dims=NN):
    return lax.dot_general(a, b, dims, preferred_element_type=F32)


def iota(shape, dim):
    return lax.broadcasted_iota(jnp.int32, shape, dim)


def write_edges(src, top, bot, left, right, l_sc, r_sc, c_sc):
    for a in range(ROWS):
        low = src[a * COLS : a * COLS + 32, :].astype(F32)
        high = src[a * COLS + 32 : a * COLS + 64, :].astype(F32)
        for k in range(HALO):
            l_sc[k * ROWS + a : k * ROWS + a + 1, :] = low[8 * k : 8 * k + 1, :]
            r_sc[k * ROWS + a : k * ROWS + a + 1, :] = high[8 * k + 15 : 8 * k + 16, :]
    left[...] = l_sc[...].astype(BF)
    right[...] = r_sc[...].astype(BF)
    c_sc[...] = jnp.zeros_like(c_sc)
    for k in range(HALO):
        for i in range(HALO):
            first = k * ROWS + i
            last = k * ROWS + ROWS - HALO + i
            row = k * HALO + i
            c_sc[0, row : row + 1, :] = l_sc[first : first + 1, :]
            c_sc[1, row : row + 1, :] = r_sc[first : first + 1, :]
            c_sc[2, row : row + 1, :] = l_sc[last : last + 1, :]
            c_sc[3, row : row + 1, :] = r_sc[last : last + 1, :]
    side = HALO * COLS
    top[:side, :] = src[0:side, :]
    bot[:side, :] = src[TOK - side : TOK, :]
    for n, ref in enumerate((top, bot)):
        ref[side : side + 16, :] = c_sc[2 * n].astype(BF)
        ref[side + 16 : side + 32, :] = c_sc[2 * n + 1].astype(BF)


EDGE_SHAPES = [
    jax.ShapeDtypeStruct((HALO * COLS + 32, CH), BF),
    jax.ShapeDtypeStruct((HALO * COLS + 32, CH), BF),
    jax.ShapeDtypeStruct((HALO * ROWS, CH), BF),
    jax.ShapeDtypeStruct((HALO * ROWS, CH), BF),
]
EDGE_SCRATCH = [
    pltpu.VMEM((HALO * ROWS, CH), F32),
    pltpu.VMEM((HALO * ROWS, CH), F32),
    pltpu.VMEM((4, 16, CH), F32),
]


def exchange_rows(edges):
    top, bot = edges[:2]
    n = lax.axis_size(ROW_AXES)
    above = lax.ppermute(bot, ROW_AXES, [(i, i + 1) for i in range(n - 1)])
    below = lax.ppermute(top, ROW_AXES, [(i + 1, i) for i in range(n - 1)])
    return above, below


def exchange_cols(edges, above, below):
    left, right = edges[2:]
    n = lax.axis_size(COL_AXES)
    side = HALO * COLS
    right = jnp.concatenate([right, above[side + 16 : side + 32], below[side + 16 : side + 32]])
    left = jnp.concatenate([left, above[side : side + 16], below[side : side + 16]])
    from_left = lax.ppermute(right, COL_AXES, [(i, i + 1) for i in range(n - 1)])
    from_right = lax.ppermute(left, COL_AXES, [(i + 1, i) for i in range(n - 1)])
    return from_left, from_right


def assemble(wide, own, halo, l_sc, r_sc, c_sc):
    above, below, left, right = halo
    edge = HALO * ROWS
    l_sc[...] = left[:edge, :].astype(F32)
    r_sc[...] = right[:edge, :].astype(F32)
    for n in range(2):
        c_sc[2 * n] = left[edge + 16 * n : edge + 16 * (n + 1), :].astype(F32)
        c_sc[2 * n + 1] = right[edge + 16 * n : edge + 16 * (n + 1), :].astype(F32)
    sub = iota((8, CH), 0)

    def put(row, x, lefts, rights):
        x = x.astype(F32).reshape(8, 8, CH)
        for cb in range(8):
            wide[row, HALO + cb] = x[cb]
        for k in range(HALO):
            wide[row, k] = jnp.where(sub == 0, lefts[k], pltpu.roll(x[5 + k], 1, 0))
            wide[row, 11 + k] = jnp.where(sub == 7, rights[k], pltpu.roll(x[k], 7, 0))

    for i in range(HALO):
        row = [k * HALO + i for k in range(HALO)]
        put(
            i,
            above[i * COLS : (i + 1) * COLS, :],
            [c_sc[0, n : n + 1, :] for n in row],
            [c_sc[1, n : n + 1, :] for n in row],
        )
        put(
            HALO + ROWS + i,
            below[i * COLS : (i + 1) * COLS, :],
            [c_sc[2, n : n + 1, :] for n in row],
            [c_sc[3, n : n + 1, :] for n in row],
        )

    def body(a, carry):
        put(
            a + HALO,
            own[pl.ds(pl.multiple_of(a * COLS, COLS), COLS), :],
            [l_sc[pl.ds(k * ROWS + a, 1), :] for k in range(HALO)],
            [r_sc[pl.ds(k * ROWS + a, 1), :] for k in range(HALO)],
        )
        return carry

    lax.fori_loop(0, ROWS, body, 0)


def spread_weights(kernel_ref, w_sc):
    for n in range(KSIZE * KSIZE):
        w_sc[n] = jnp.broadcast_to(kernel_ref[n : n + 1, :], (8, CH))


def conv_rows(wide, w_sc, a, half, flip):
    lanes = pl.ds(half * 128, 128)
    acc = [[wide[a + r + HALO, HALO + cb, :, lanes] for cb in range(8)] for r in range(2)]
    for i in range(KSIZE + 1):
        xs = [wide[a + i, c, :, lanes] for c in range(WIDE)]
        for r in range(2):
            if not 0 <= i - r < KSIZE:
                continue
            for j in range(KSIZE):
                n = (i - r) * KSIZE + j
                w = w_sc[KSIZE * KSIZE - 1 - n if flip else n, :, lanes]
                acc[r] = [acc[r][cb] + xs[cb + j] * w for cb in range(8)]
    return acc


def norm_rows(x):
    centre = x - jnp.sum(x, axis=-1, keepdims=True) * (1.0 / CH)
    variance = jnp.sum(centre * centre, axis=-1, keepdims=True) * (1.0 / CH)
    inverse = lax.rsqrt(variance + norm_eps)
    return centre * inverse, inverse


def embed_kernel(pixels, weights, bias, emb, z_ref, top, bot, left, right, w_sc, l_sc, r_sc, c_sc):
    out = iota((256, 256), 0)
    spread = (((out & 7) * 8 + ((out >> 3) & 7)) * 4 + (out >> 6)) == iota((256, 256), 1)
    spread = jnp.where(spread, 1.0, 0.0).astype(BF)
    by_cell = dot(spread, pixels[...], NT).astype(BF)
    row = iota((512, 384), 0)
    fu = row & 15
    target = (fu >> 2) * 128 + (row >> 4) * 4 + (fu & 3)
    order = jnp.where((target == iota((512, 384), 1)) & (fu < 12), 1.0, 0.0).astype(BF)
    z = dot(by_cell, order, NT).astype(BF)
    for g in range(4):
        for v in range(4):
            z_ref[g * 64 : (g + 1) * 64, v * 128 : (v + 1) * 128] = z[
                v * 64 : (v + 1) * 64, g * 128 : (g + 1) * 128
            ]
    w_sc[...] = jnp.zeros_like(w_sc)
    for v in range(4):
        for a8 in range(8):
            first = v * 128 + a8 * 16
            w_sc[first : first + 16, a8 * CH : (a8 + 1) * CH] = weights[v]
    for a8 in range(8):
        block = dot(z_ref[...], w_sc[:, a8 * CH : (a8 + 1) * CH]) + bias[...]
        block = block.astype(BF)
        for g in range(4):
            a = g * 8 + a8
            emb[a * COLS : (a + 1) * COLS, :] = block[g * 64 : (g + 1) * 64, :]
    write_edges(emb, top, bot, left, right, l_sc, r_sc, c_sc)


def embed(pixels, patch_weight, patch_bias):
    weights = patch_weight.reshape(12, 4, CH).transpose(1, 0, 2)
    weights = jnp.pad(weights, ((0, 0), (0, 4), (0, 0)))
    outs = pl.pallas_call(
        embed_kernel,
        name="embed",
        out_shape=[
            jax.ShapeDtypeStruct((TOK, CH), BF),
            jax.ShapeDtypeStruct((256, 512), BF),
        ]
        + EDGE_SHAPES,
        scratch_shapes=[pltpu.VMEM((512, 2048), BF)] + EDGE_SCRATCH,
        compiler_params=VMEM,
    )(pixels.reshape(384, 256), weights, patch_bias.reshape(1, CH))
    return outs[0], outs[1], outs[2:]


def conv_kernel_body(emb, above, below, lh, rh, kern, gain, centred, inverse, normed, wide, w_sc, l_sc, r_sc, c_sc):
    assemble(wide, emb, (above, below, lh, rh), l_sc, r_sc, c_sc)
    spread_weights(kern, w_sc)

    def body(n, carry):
        for half in range(2):
            acc = conv_rows(wide, w_sc, 2 * n, half, False)
            for r in range(2):
                for cb in range(8):
                    rows = pl.ds(pl.multiple_of((2 * n + r) * COLS + cb * 8, 8), 8)
                    centred[rows, pl.ds(half * 128, 128)] = acc[r][cb]
        return carry

    lax.fori_loop(0, ROWS // 2, body, 0)

    def norm_body(n, carry):
        rows = pl.ds(pl.multiple_of(n * BLOCK, BLOCK), BLOCK)
        out, inv = norm_rows(centred[rows, :])
        centred[rows, :] = out
        inverse[rows, :] = jnp.broadcast_to(inv, (BLOCK, 128))
        normed[rows, :] = (out * gain[...]).astype(BF)
        return carry

    lax.fori_loop(0, TOK // BLOCK, norm_body, 0)


def conv_forward(emb, halo, conv_kernel, gain):
    return pl.pallas_call(
        conv_kernel_body,
        name="conv_forward",
        out_shape=[
            jax.ShapeDtypeStruct((TOK, CH), F32),
            jax.ShapeDtypeStruct((TOK, 128), F32),
            jax.ShapeDtypeStruct((TOK, CH), BF),
        ],
        scratch_shapes=[
            pltpu.VMEM((ROWS + 2 * HALO, WIDE, 8, CH), F32),
            pltpu.VMEM((KSIZE * KSIZE, 8, CH), F32),
        ]
        + EDGE_SCRATCH,
        compiler_params=VMEM,
    )(emb, *halo, conv_kernel, gain)


CHUNK = 1024
GROUP = 2
ACHUNK = 1024
WIDTH = 4
SCALE = 128**-0.5
SCALE2 = SCALE * 1.4426950408889634
COST = pl.CostEstimate(flops=14_000_000_000, transcendentals=0, bytes_accessed=16_000_000)


def lane(n):
    return slice(n * 128, (n + 1) * 128)


def attend_kernel(normed, wk, wv, q, up, k_out, v_out, weighted, stats, s_sc):
    step = pl.program_id(0)
    peak = [None] * WIDTH
    level = None
    for n in range(WIDTH + 1):
        total = jnp.zeros((1, 256), F32)
        acc = jnp.zeros((128, 256), F32)
        if n < WIDTH:
            w = jnp.concatenate([wk[:, lane(n)], wv[:, lane(n)]], axis=1)
        for c in range(TOK // ACHUNK):
            rows = slice(c * ACHUNK, (c + 1) * ACHUNK)
            if n < WIDTH:
                kv = dot(normed[rows, :], w).astype(BF)
                k_out[rows, lane(n)] = kv[:, :128]
                v_out[rows, lane(n)] = kv[:, 128:]
                s = dot(kv[:, :128], q[:, lane(n)], NT)
                s_sc[n % 2, rows, :] = s
                top = jnp.max(s, axis=0, keepdims=True)
                peak[n] = top if peak[n] is None else jnp.maximum(peak[n], top)
            if n > 0:
                p = jnp.exp2(s_sc[1 - n % 2, rows, :] * SCALE2 - level)
                total = total + jnp.sum(p, axis=0, keepdims=True)
                acc = acc + dot(v_out[rows, lane(n - 1)], p.astype(BF), TN)
        if n > 0:
            weighted[n - 1] = acc
            dots = jnp.sum(acc * up[:, lane(n - 1)].astype(F32).T, axis=0, keepdims=True)
            h = step * WIDTH + n - 1
            stats[0, pl.ds(h, 1), :] = level
            stats[1, pl.ds(h, 1), :] = total
            stats[2, pl.ds(h, 1), :] = dots
        if n < WIDTH:
            level = peak[n] * SCALE2


def whole(shape):
    return pl.BlockSpec(shape, lambda h: (0,) * len(shape))


def column(rows, first=0):
    return pl.BlockSpec((rows, 128 * WIDTH), lambda h: (0, h + first))


def attend(normed, kv_weight, latents, d_attended):
    return pl.pallas_call(
        attend_kernel,
        name="attend",
        grid=(HEADS // WIDTH,),
        in_specs=[
            whole((TOK, CH)),
            column(CH),
            column(CH, HEADS // WIDTH),
            column(256),
            column(256),
        ],
        out_specs=[
            column(TOK),
            column(TOK),
            pl.BlockSpec((WIDTH, 128, 256), lambda h: (h, 0, 0)),
            whole((3, HEADS, 256)),
        ],
        out_shape=[
            jax.ShapeDtypeStruct((TOK, 1024), BF),
            jax.ShapeDtypeStruct((TOK, 1024), BF),
            jax.ShapeDtypeStruct((HEADS, 128, 256), F32),
            jax.ShapeDtypeStruct((3, HEADS, 256), F32),
        ],
        scratch_shapes=[pltpu.VMEM((2, TOK, 256), F32)],
        compiler_params=VMEM,
    )(normed, kv_weight, kv_weight, latents, d_attended)


STEPS = HEADS // GROUP


def step_at(step, core):
    return (step + STEPS // 2 * (1 - core[0])) & (STEPS - 1)


def attend_grad_kernel(
    core, normed, k_in, v_in, wk, wv, q, up, lse, dots, factor, weighted,
    send, keep, dn_sc, nt_sc,
):
    step = pl.program_id(0)
    first = step_at(step, core) * GROUP

    @pl.when(step == 0)
    def _():
        nt_sc[...] = normed[...].T
        dn_sc[...] = jnp.zeros_like(dn_sc)

    w = jnp.concatenate([x[:, lane(n)] for n in range(GROUP) for x in (wk, wv)], axis=1)
    level = [lse[pl.ds(first + n, 1), :] for n in range(GROUP)]
    row_dots = [dots[pl.ds(first + n, 1), :] for n in range(GROUP)]
    qg = [jnp.zeros((128, 256), F32)] * GROUP
    wg = jnp.zeros((256, 256 * GROUP), F32)
    units = [(c, n) for c in range(TOK // CHUNK) for n in range(GROUP)]

    def products(c, n):
        rows = slice(c * CHUNK, (c + 1) * CHUNK)
        return (
            dot(k_in[rows, lane(n)], q[:, lane(n)], NT),
            dot(v_in[rows, lane(n)], up[:, lane(n)], NT),
        )

    d_proj = []
    ahead = products(*units[0])
    for at, (c, n) in enumerate(units):
        rows = slice(c * CHUNK, (c + 1) * CHUNK)
        s, dp = ahead
        if at + 1 < len(units):
            ahead = products(*units[at + 1])
        p = jnp.exp2(s * SCALE2 - level[n])
        ds = (p * (dp - row_dots[n])).astype(BF)
        qg[n] = qg[n] + dot(k_in[rows, lane(n)], ds, TN)
        d_proj.append((dot(ds, q[:, lane(n)]) * SCALE).astype(BF))
        d_proj.append(dot(p.astype(BF), up[:, lane(n)]).astype(BF))
        if n == GROUP - 1:
            d_proj = jnp.concatenate(d_proj, axis=1)
            wg = wg + dot(nt_sc[:, rows], d_proj)
            dn_sc[rows, :] += dot(d_proj, w, NT)
            d_proj = []
    att = [(weighted[n] * factor[pl.ds(first + n, 1), :]).T for n in range(GROUP)]
    qg = [(x * SCALE).T for x in qg]

    def put(out):
        for n in range(GROUP):
            out[0, n] = att[n]
            out[1, n] = qg[n]
            out[2, n] = wg[:, lane(2 * n)]
            out[3, n] = wg[:, lane(2 * n + 1)]

    @pl.when(step < STEPS // 2)
    def _():
        put(send)

    @pl.when(step >= STEPS // 2)
    def _():
        put(keep)


def norm_grad_kernel(dn_in, centred, inverse, gain, d_mixed, gain_grad, top, bot, left, right, l_sc, r_sc, c_sc):
    def body(n, total):
        rows = pl.ds(pl.multiple_of(n * BLOCK, BLOCK), BLOCK)
        x = centred[rows, :]
        inv = inverse[rows, :]
        dn = dn_in[rows, :]
        total = total + jnp.sum(dn * x, axis=0, keepdims=True)
        g = dn * gain[...]
        mean = jnp.sum(g, axis=-1, keepdims=True) * (1.0 / CH)
        slope = jnp.sum(g * x, axis=-1, keepdims=True) * (1.0 / CH)
        inv = jnp.concatenate([inv, inv], axis=1)
        d_mixed[rows, :] = (inv * (g - mean - x * slope)).astype(BF)
        return total

    gain_grad[...] = lax.fori_loop(0, TOK // BLOCK, body, jnp.zeros((1, CH), F32))
    write_edges(d_mixed, top, bot, left, right, l_sc, r_sc, c_sc)


def norm_grad(dn, centred, inverse, gain):
    outs = pl.pallas_call(
        norm_grad_kernel,
        name="norm_grad",
        out_shape=[jax.ShapeDtypeStruct((TOK, CH), BF), jax.ShapeDtypeStruct((1, CH), F32)] + EDGE_SHAPES,
        scratch_shapes=EDGE_SCRATCH,
        compiler_params=VMEM,
        cost_estimate=COST,
    )(dn, centred, inverse, gain)
    return outs[0], outs[1], outs[2:]


def attend_grad(
    core, normed, k, v, kv_weight, latents, d_attended, lse, dots, factor, weighted
):
    def full(shape):
        return pl.BlockSpec(shape, lambda n, core: (0,) * len(shape))

    def head(rows, first=0):
        return pl.BlockSpec((rows, 128 * GROUP), lambda n, core: (0, step_at(n, core) + first))

    half = STEPS // 2
    block = (4, GROUP, 256, 128)
    part = jax.ShapeDtypeStruct((4, HEADS // 2, 256, 128), F32)
    outs = pl.pallas_call(
        attend_grad_kernel,
        name="attend_grad",
        grid_spec=pltpu.PrefetchScalarGridSpec(
            num_scalar_prefetch=1,
            grid=(STEPS,),
            in_specs=[
                full((TOK, CH)),
                head(TOK),
                head(TOK),
                head(CH),
                head(CH, STEPS),
                head(256),
                head(256),
                full((HEADS, 256)),
                full((HEADS, 256)),
                full((HEADS, 256)),
                pl.BlockSpec((GROUP, 128, 256), lambda n, core: (step_at(n, core), 0, 0)),
            ],
            out_specs=[
                pl.BlockSpec(block, lambda n, core: (0, jnp.minimum(n, half - 1), 0, 0)),
                pl.BlockSpec(block, lambda n, core: (0, jnp.maximum(n - half, 0), 0, 0)),
                full((TOK, CH)),
            ],
            scratch_shapes=[pltpu.VMEM((CH, TOK), BF)],
        ),
        out_shape=[
            part,
            part,
            jax.ShapeDtypeStruct((TOK, CH), F32),
        ],
        compiler_params=VMEM,
        cost_estimate=COST,
    )(core, normed, k, v, kv_weight, kv_weight, latents, d_attended, lse, dots, factor, weighted)
    return outs


def kernel_grad_body(emb, above, below, lh, rh, d_mixed, out, wide, d_sc, l_sc, r_sc, c_sc):
    assemble(wide, emb, (above, below, lh, rh), l_sc, r_sc, c_sc)
    d_sc[...] = d_mixed[...].astype(F32)
    for half in range(2):
        lanes = pl.ds(half * 128, 128)
        for i in range(KSIZE):

            def body(n, acc):
                acc = list(acc)
                for r in range(4):
                    a = 4 * n + r
                    xs = [wide[a + i, c, :, lanes] for c in range(WIDE)]
                    base = pl.multiple_of(a * COLS, COLS)
                    ds = [d_sc[pl.ds(base + cb * 8, 8), lanes] for cb in range(8)]
                    for cb in range(8):
                        for j in range(KSIZE):
                            acc[j] = acc[j] + xs[cb + j] * ds[cb]
                return tuple(acc)

            zero = jnp.zeros((8, 128), F32)
            acc = lax.fori_loop(0, ROWS // 4, body, (zero,) * KSIZE)
            for j in range(KSIZE):
                n = i * KSIZE + j
                out[n : n + 1, lanes] = jnp.sum(acc[j], axis=0, keepdims=True)


def kernel_grad(emb, halo, d_mixed):
    return pl.pallas_call(
        kernel_grad_body,
        name="kernel_grad",
        out_shape=jax.ShapeDtypeStruct((KSIZE * KSIZE, CH), F32),
        scratch_shapes=[pltpu.VMEM((ROWS + 2 * HALO, WIDE, 8, CH), F32), pltpu.VMEM((TOK, CH), F32)]
        + EDGE_SCRATCH,
        compiler_params=VMEM,
        cost_estimate=COST,
    )(emb, *halo, d_mixed)


def conv_back_body(d_mixed, above, below, lh, rh, kern, z, kern_grad, gain_grad, small, wide, d_sc, w_sc, l_sc, r_sc, c_sc):
    assemble(wide, d_mixed, (above, below, lh, rh), l_sc, r_sc, c_sc)
    spread_weights(kern, w_sc)
    zero = jnp.zeros((8, 128), F32)

    def body(n, bias):
        bias = list(bias)
        for half in range(2):
            accs = conv_rows(wide, w_sc, 2 * n, half, True)
            for r in range(2):
                a = 2 * n + r
                acc = jnp.concatenate(accs[r], axis=0).astype(BF)
                d_sc[a & 7, pl.ds(pl.multiple_of((a >> 3) * 64, 64), 64), pl.ds(half * 128, 128)] = acc
                bias[half] = bias[half] + jnp.sum(acc.astype(F32).reshape(8, 8, 128), axis=0)
        return tuple(bias)

    bias = lax.fori_loop(0, ROWS // 2, body, (zero, zero))
    for half in range(2):
        small[98, :, half * 128 : (half + 1) * 128] = jnp.sum(bias[half], axis=0, keepdims=True)
    for n in range(KSIZE * KSIZE):
        small[48 + n] = kern_grad[n : n + 1, :]
    small[97] = gain_grad[...]
    small[99:128] = jnp.zeros((29, 1, CH), F32)
    total = [jnp.zeros((16, CH), F32) for _ in range(4)]
    for a8 in range(8):
        part = dot(z[...], d_sc[a8], TN)
        for v in range(4):
            first = v * 128 + a8 * 16
            total[v] = total[v] + part[first : first + 16, :]
    for v in range(4):
        for fu in range(12):
            small[fu * 4 + v] = total[v][fu : fu + 1, :]


def conv_back(d_mixed, halo, conv_kernel, z, kern_grad, gain_grad):
    return pl.pallas_call(
        conv_back_body,
        name="conv_back",
        out_shape=jax.ShapeDtypeStruct((128, 1, CH), F32),
        scratch_shapes=[
            pltpu.VMEM((ROWS + 2 * HALO, WIDE, 8, CH), F32),
            pltpu.VMEM((8, 256, CH), BF),
            pltpu.VMEM((KSIZE * KSIZE, 8, CH), F32),
        ]
        + EDGE_SCRATCH,
        compiler_params=VMEM,
        cost_estimate=COST,
    )(d_mixed, *halo, conv_kernel, z, kern_grad, gain_grad)


CHIPS = ("z", "x", "y")
ALL = ("z", "core", "x", "y")
PAIR = [(0, 1), (1, 0)]
STAGES = (("z", "core"), ("x", "y"))


def gather(x, axes):
    n = lax.axis_size(axes)
    copies = jnp.broadcast_to(x[None], (n,) + x.shape)
    return lax.all_to_all(copies, axes, 0, 0, tiled=True)


def combine_stats(stats):
    for axes in STAGES:
        group = gather(stats, axes)
        peak = jnp.max(group[:, 0], axis=0)
        factors = jnp.exp2(group[:, 0] - peak)
        total = jnp.sum(group[:, 1] * factors, axis=0)
        dots = jnp.sum(group[:, 2] * factors, axis=0)
        stats = jnp.stack([peak, total, dots])
    return stats


def collect_body(core, own, other, attended, q_grad, kv_grad):
    h = pl.program_id(0)
    mine = (h // (HEADS // 2)) == core[0]

    def put(x):
        attended[...] = x[0, 0].astype(F32)
        q_grad[...] = x[1, 0].astype(F32)
        kv_grad[:, pl.ds(pl.multiple_of(h * 128, 128), 128)] = x[2, 0].astype(F32)
        kv_grad[:, pl.ds(pl.multiple_of((HEADS + h) * 128, 128), 128)] = x[3, 0].astype(F32)

    @pl.when(mine)
    def _():
        put(own)

    @pl.when(jnp.logical_not(mine))
    def _():
        put(other)


def collect(core, own, other):
    shape = (4, HEADS // 2, 256, 128)
    block = pl.BlockSpec((4, 1, 256, 128), lambda h, core: (0, h % (HEADS // 2), 0, 0))
    heads = pl.BlockSpec((256, 128), lambda h, core: (0, h))
    return pl.pallas_call(
        collect_body,
        name="collect",
        grid_spec=pltpu.PrefetchScalarGridSpec(
            num_scalar_prefetch=1,
            grid=(HEADS,),
            in_specs=[block, block],
            out_specs=[heads, heads, pl.BlockSpec((256, 2048), lambda h, core: (0, 0))],
        ),
        out_shape=[
            jax.ShapeDtypeStruct((256, 1024), F32),
            jax.ShapeDtypeStruct((256, 1024), F32),
            jax.ShapeDtypeStruct((256, 2048), F32),
        ],
        compiler_params=VMEM,
    )(core, own.reshape(shape), other.reshape(shape))


def split_small_body(small, patch, kern, gain, bias):
    for n in range(48):
        patch[n : n + 1, :] = small[n]
    for n in range(KSIZE * KSIZE):
        kern[n : n + 1, :] = small[48 + n]
    gain[...] = small[97, 0]
    bias[...] = small[98, 0]


def split_small(small):
    return pl.pallas_call(
        split_small_body,
        name="split_small",
        out_shape=[
            jax.ShapeDtypeStruct((48, CH), F32),
            jax.ShapeDtypeStruct((KSIZE * KSIZE, CH), F32),
            jax.ShapeDtypeStruct((CH,), F32),
            jax.ShapeDtypeStruct((CH,), F32),
        ],
        compiler_params=VMEM,
    )(small)


def block_sum(parts):
    return jnp.sum(parts.astype(F32), axis=0)


def copies(x):
    return jnp.broadcast_to(x.astype(WIRE)[None], (64,) + x.shape)


def send(x):
    return lax.all_to_all(x, CHIPS, 0, 0, tiled=True)


def send_all(x):
    return lax.all_to_all(x, ALL, 0, 0, tiled=True)


def tie(x, *others):
    return lax.optimization_barrier((x,) + others)


def per_device(
    pixels, patch_weight, patch_bias, conv_kernel, norm_gain, kv_weight, latents, d_attended
):
    gain = norm_gain.reshape(1, CH)
    emb, z, edges = embed(pixels, patch_weight, patch_bias)
    rows = exchange_rows(edges)
    halo = rows + exchange_cols(edges, *rows)
    centred, inverse, normed = conv_forward(emb, halo, conv_kernel, gain)
    k, v, weighted, local = attend(normed, kv_weight, latents, d_attended)
    stats = combine_stats(local)
    lse = stats[0] + jnp.log2(stats[1])
    row_dots = stats[2] / stats[1]
    factor = jnp.exp2(local[0] - stats[0]) / stats[1]
    core = lax.axis_index("core").astype(jnp.int32).reshape(1)
    away, keep, dn = attend_grad(
        core, normed, k, v, kv_weight, latents, d_attended, lse, row_dots, factor, weighted
    )
    away = lax.ppermute(away, "core", PAIR)
    d_mixed, gain_grad, d_edges = norm_grad(dn, centred, inverse, gain)
    d_mixed, away, *d_edges = tie(d_mixed, away, *d_edges)
    message = (keep + away).astype(BF).reshape(64, 64, 128)
    d_mixed, message, *d_edges = tie(d_mixed, message, *d_edges)
    message = send(message)
    d_rows = exchange_rows(d_edges)
    kern = kernel_grad(emb, halo, d_mixed)
    d_mixed, message, kern, *d_rows = tie(d_mixed, message, kern, *d_rows)
    message = copies(block_sum(message))
    d_mixed, message, *d_rows = tie(d_mixed, message, *d_rows)
    message = send(message)
    d_cols = exchange_cols(d_edges, *d_rows)
    small = conv_back(d_mixed, tuple(d_rows) + tuple(d_cols), conv_kernel, z, kern, gain_grad)
    small, message = tie(small, message)
    mine = block_sum(send_all(small))
    small = send_all(jnp.broadcast_to(mine[None], (128,) + mine.shape))
    outs = collect(core, message, lax.ppermute(message, "core", PAIR))
    small, *outs = tie(small, *outs)
    patch, kern, gain, bias = split_small(small)
    return (*outs, gain, kern, patch, bias)


def solution(mesh):
    split = Mesh(mesh.devices.reshape(4, 2, 4, 4), ("z", "core", "x", "y"))
    return jax.shard_map(
        per_device,
        mesh=split,
        in_specs=(P(None, ("z", "core"), ("x", "y")), P(), P(), P(), P(), P(), P(), P()),
        out_specs=(P(), P(), P(), P(), P(), P(), P()),
        check_vma=False,
    )
```

```python
import jax
import jax.numpy as jnp
from jax import lax
from jax.experimental import pallas as pl
from jax.experimental.pallas import tpu as pltpu
from jax.sharding import Mesh
from jax.sharding import PartitionSpec as P

PATCH = 4
KSIZE = 7
HEADS = 8
HALO = 3
norm_eps = 1e-05
BF = jnp.bfloat16
F32 = jnp.float32
NT = (((1,), (1,)), ((), ()))
TN = (((0,), (0,)), ((), ()))
NN = (((1,), (0,)), ((), ()))
ROWS = 32
COLS = 64
CH = 256
TOK = ROWS * COLS
WIDE = 14
BLOCK = 2048
WIRE = BF
ROW_AXES = ("z", "core")
COL_AXES = ("x", "y")
VMEM = pltpu.CompilerParams(vmem_limit_bytes=58 << 20)


def dot(a, b, dims=NN):
    return lax.dot_general(a, b, dims, preferred_element_type=F32)


def iota(shape, dim):
    return lax.broadcasted_iota(jnp.int32, shape, dim)


def write_edges(src, top, bot, left, right, l_sc, r_sc, c_sc):
    for a in range(ROWS):
        low = src[a * COLS : a * COLS + 32, :].astype(F32)
        high = src[a * COLS + 32 : a * COLS + 64, :].astype(F32)
        for k in range(HALO):
            l_sc[k * ROWS + a : k * ROWS + a + 1, :] = low[8 * k : 8 * k + 1, :]
            r_sc[k * ROWS + a : k * ROWS + a + 1, :] = high[8 * k + 15 : 8 * k + 16, :]
    left[...] = l_sc[...].astype(BF)
    right[...] = r_sc[...].astype(BF)
    c_sc[...] = jnp.zeros_like(c_sc)
    for k in range(HALO):
        for i in range(HALO):
            first = k * ROWS + i
            last = k * ROWS + ROWS - HALO + i
            row = k * HALO + i
            c_sc[0, row : row + 1, :] = l_sc[first : first + 1, :]
            c_sc[1, row : row + 1, :] = r_sc[first : first + 1, :]
            c_sc[2, row : row + 1, :] = l_sc[last : last + 1, :]
            c_sc[3, row : row + 1, :] = r_sc[last : last + 1, :]
    side = HALO * COLS
    top[:side, :] = src[0:side, :]
    bot[:side, :] = src[TOK - side : TOK, :]
    for n, ref in enumerate((top, bot)):
        ref[side : side + 16, :] = c_sc[2 * n].astype(BF)
        ref[side + 16 : side + 32, :] = c_sc[2 * n + 1].astype(BF)


EDGE_SHAPES = [
    jax.ShapeDtypeStruct((HALO * COLS + 32, CH), BF),
    jax.ShapeDtypeStruct((HALO * COLS + 32, CH), BF),
    jax.ShapeDtypeStruct((HALO * ROWS, CH), BF),
    jax.ShapeDtypeStruct((HALO * ROWS, CH), BF),
]
EDGE_SCRATCH = [
    pltpu.VMEM((HALO * ROWS, CH), F32),
    pltpu.VMEM((HALO * ROWS, CH), F32),
    pltpu.VMEM((4, 16, CH), F32),
]


def exchange_rows(edges):
    top, bot = edges[:2]
    n = lax.axis_size(ROW_AXES)
    above = lax.ppermute(bot, ROW_AXES, [(i, i + 1) for i in range(n - 1)])
    below = lax.ppermute(top, ROW_AXES, [(i + 1, i) for i in range(n - 1)])
    return above, below


def exchange_cols(edges, above, below):
    left, right = edges[2:]
    n = lax.axis_size(COL_AXES)
    side = HALO * COLS
    right = jnp.concatenate([right, above[side + 16 : side + 32], below[side + 16 : side + 32]])
    left = jnp.concatenate([left, above[side : side + 16], below[side : side + 16]])
    from_left = lax.ppermute(right, COL_AXES, [(i, i + 1) for i in range(n - 1)])
    from_right = lax.ppermute(left, COL_AXES, [(i + 1, i) for i in range(n - 1)])
    return from_left, from_right


def assemble(wide, own, halo, l_sc, r_sc, c_sc):
    above, below, left, right = halo
    edge = HALO * ROWS
    l_sc[...] = left[:edge, :].astype(F32)
    r_sc[...] = right[:edge, :].astype(F32)
    for n in range(2):
        c_sc[2 * n] = left[edge + 16 * n : edge + 16 * (n + 1), :].astype(F32)
        c_sc[2 * n + 1] = right[edge + 16 * n : edge + 16 * (n + 1), :].astype(F32)
    sub = iota((8, CH), 0)

    def put(row, x, lefts, rights):
        x = x.astype(F32).reshape(8, 8, CH)
        for cb in range(8):
            wide[row, HALO + cb] = x[cb]
        for k in range(HALO):
            wide[row, k] = jnp.where(sub == 0, lefts[k], pltpu.roll(x[5 + k], 1, 0))
            wide[row, 11 + k] = jnp.where(sub == 7, rights[k], pltpu.roll(x[k], 7, 0))

    for i in range(HALO):
        row = [k * HALO + i for k in range(HALO)]
        put(
            i,
            above[i * COLS : (i + 1) * COLS, :],
            [c_sc[0, n : n + 1, :] for n in row],
            [c_sc[1, n : n + 1, :] for n in row],
        )
        put(
            HALO + ROWS + i,
            below[i * COLS : (i + 1) * COLS, :],
            [c_sc[2, n : n + 1, :] for n in row],
            [c_sc[3, n : n + 1, :] for n in row],
        )

    def body(a, carry):
        put(
            a + HALO,
            own[pl.ds(pl.multiple_of(a * COLS, COLS), COLS), :],
            [l_sc[pl.ds(k * ROWS + a, 1), :] for k in range(HALO)],
            [r_sc[pl.ds(k * ROWS + a, 1), :] for k in range(HALO)],
        )
        return carry

    lax.fori_loop(0, ROWS, body, 0)


def spread_weights(kernel_ref, w_sc):
    for n in range(KSIZE * KSIZE):
        w_sc[n] = jnp.broadcast_to(kernel_ref[n : n + 1, :], (8, CH))


def conv_rows(wide, w_sc, a, half, flip):
    lanes = pl.ds(half * 128, 128)
    acc = [[wide[a + r + HALO, HALO + cb, :, lanes] for cb in range(8)] for r in range(2)]
    for i in range(KSIZE + 1):
        xs = [wide[a + i, c, :, lanes] for c in range(WIDE)]
        for r in range(2):
            if not 0 <= i - r < KSIZE:
                continue
            for j in range(KSIZE):
                n = (i - r) * KSIZE + j
                w = w_sc[KSIZE * KSIZE - 1 - n if flip else n, :, lanes]
                acc[r] = [acc[r][cb] + xs[cb + j] * w for cb in range(8)]
    return acc


def norm_rows(x):
    centre = x - jnp.sum(x, axis=-1, keepdims=True) * (1.0 / CH)
    variance = jnp.sum(centre * centre, axis=-1, keepdims=True) * (1.0 / CH)
    inverse = lax.rsqrt(variance + norm_eps)
    return centre * inverse, inverse


def embed_kernel(pixels, weights, bias, emb, z_ref, top, bot, left, right, w_sc, l_sc, r_sc, c_sc):
    out = iota((256, 256), 0)
    spread = (((out & 7) * 8 + ((out >> 3) & 7)) * 4 + (out >> 6)) == iota((256, 256), 1)
    spread = jnp.where(spread, 1.0, 0.0).astype(BF)
    by_cell = dot(spread, pixels[...], NT).astype(BF)
    row = iota((512, 384), 0)
    fu = row & 15
    target = (fu >> 2) * 128 + (row >> 4) * 4 + (fu & 3)
    order = jnp.where((target == iota((512, 384), 1)) & (fu < 12), 1.0, 0.0).astype(BF)
    z = dot(by_cell, order, NT).astype(BF)
    for g in range(4):
        for v in range(4):
            z_ref[g * 64 : (g + 1) * 64, v * 128 : (v + 1) * 128] = z[
                v * 64 : (v + 1) * 64, g * 128 : (g + 1) * 128
            ]
    w_sc[...] = jnp.zeros_like(w_sc)
    for v in range(4):
        for a8 in range(8):
            first = v * 128 + a8 * 16
            w_sc[first : first + 16, a8 * CH : (a8 + 1) * CH] = weights[v]
    for a8 in range(8):
        block = dot(z_ref[...], w_sc[:, a8 * CH : (a8 + 1) * CH]) + bias[...]
        block = block.astype(BF)
        for g in range(4):
            a = g * 8 + a8
            emb[a * COLS : (a + 1) * COLS, :] = block[g * 64 : (g + 1) * 64, :]
    write_edges(emb, top, bot, left, right, l_sc, r_sc, c_sc)


def embed(pixels, patch_weight, patch_bias):
    weights = patch_weight.reshape(12, 4, CH).transpose(1, 0, 2)
    weights = jnp.pad(weights, ((0, 0), (0, 4), (0, 0)))
    outs = pl.pallas_call(
        embed_kernel,
        name="embed",
        out_shape=[
            jax.ShapeDtypeStruct((TOK, CH), BF),
            jax.ShapeDtypeStruct((256, 512), BF),
        ]
        + EDGE_SHAPES,
        scratch_shapes=[pltpu.VMEM((512, 2048), BF)] + EDGE_SCRATCH,
        compiler_params=VMEM,
    )(pixels.reshape(384, 256), weights, patch_bias.reshape(1, CH))
    return outs[0], outs[1], outs[2:]


def conv_kernel_body(emb, above, below, lh, rh, kern, gain, centred, inverse, normed, wide, w_sc, l_sc, r_sc, c_sc):
    assemble(wide, emb, (above, below, lh, rh), l_sc, r_sc, c_sc)
    spread_weights(kern, w_sc)

    def body(n, carry):
        for half in range(2):
            acc = conv_rows(wide, w_sc, 2 * n, half, False)
            for r in range(2):
                for cb in range(8):
                    rows = pl.ds(pl.multiple_of((2 * n + r) * COLS + cb * 8, 8), 8)
                    centred[rows, pl.ds(half * 128, 128)] = acc[r][cb]
        return carry

    lax.fori_loop(0, ROWS // 2, body, 0)

    def norm_body(n, carry):
        rows = pl.ds(pl.multiple_of(n * BLOCK, BLOCK), BLOCK)
        out, inv = norm_rows(centred[rows, :])
        centred[rows, :] = out
        inverse[rows, :] = jnp.broadcast_to(inv, (BLOCK, 128))
        normed[rows, :] = (out * gain[...]).astype(BF)
        return carry

    lax.fori_loop(0, TOK // BLOCK, norm_body, 0)


def conv_forward(emb, halo, conv_kernel, gain):
    return pl.pallas_call(
        conv_kernel_body,
        name="conv_forward",
        out_shape=[
            jax.ShapeDtypeStruct((TOK, CH), F32),
            jax.ShapeDtypeStruct((TOK, 128), F32),
            jax.ShapeDtypeStruct((TOK, CH), BF),
        ],
        scratch_shapes=[
            pltpu.VMEM((ROWS + 2 * HALO, WIDE, 8, CH), F32),
            pltpu.VMEM((KSIZE * KSIZE, 8, CH), F32),
        ]
        + EDGE_SCRATCH,
        compiler_params=VMEM,
    )(emb, *halo, conv_kernel, gain)


CHUNK = 1024
GROUP = 2
ACHUNK = 1024
WIDTH = 4
SCALE = 128**-0.5
SCALE2 = SCALE * 1.4426950408889634
COST = pl.CostEstimate(flops=14_000_000_000, transcendentals=0, bytes_accessed=16_000_000)


def lane(n):
    return slice(n * 128, (n + 1) * 128)


def attend_kernel(normed, wk, wv, q, up, k_out, v_out, weighted, stats, s_sc):
    step = pl.program_id(0)
    peak = [None] * WIDTH
    level = None
    for n in range(WIDTH + 1):
        total = jnp.zeros((1, 256), F32)
        acc = jnp.zeros((128, 256), F32)
        if n < WIDTH:
            w = jnp.concatenate([wk[:, lane(n)], wv[:, lane(n)]], axis=1)
        for c in range(TOK // ACHUNK):
            rows = slice(c * ACHUNK, (c + 1) * ACHUNK)
            if n < WIDTH:
                kv = dot(normed[rows, :], w).astype(BF)
                k_out[rows, lane(n)] = kv[:, :128]
                v_out[rows, lane(n)] = kv[:, 128:]
                s = dot(kv[:, :128], q[:, lane(n)], NT)
                s_sc[n % 2, rows, :] = s
                top = jnp.max(s, axis=0, keepdims=True)
                peak[n] = top if peak[n] is None else jnp.maximum(peak[n], top)
            if n > 0:
                p = jnp.exp2(s_sc[1 - n % 2, rows, :] * SCALE2 - level)
                total = total + jnp.sum(p, axis=0, keepdims=True)
                acc = acc + dot(v_out[rows, lane(n - 1)], p.astype(BF), TN)
        if n > 0:
            weighted[n - 1] = acc
            dots = jnp.sum(acc * up[:, lane(n - 1)].astype(F32).T, axis=0, keepdims=True)
            h = step * WIDTH + n - 1
            stats[0, pl.ds(h, 1), :] = level
            stats[1, pl.ds(h, 1), :] = total
            stats[2, pl.ds(h, 1), :] = dots
        if n < WIDTH:
            level = peak[n] * SCALE2


def whole(shape):
    return pl.BlockSpec(shape, lambda h: (0,) * len(shape))


def column(rows, first=0):
    return pl.BlockSpec((rows, 128 * WIDTH), lambda h: (0, h + first))


def attend(normed, kv_weight, latents, d_attended):
    return pl.pallas_call(
        attend_kernel,
        name="attend",
        grid=(HEADS // WIDTH,),
        in_specs=[
            whole((TOK, CH)),
            column(CH),
            column(CH, HEADS // WIDTH),
            column(256),
            column(256),
        ],
        out_specs=[
            column(TOK),
            column(TOK),
            pl.BlockSpec((WIDTH, 128, 256), lambda h: (h, 0, 0)),
            whole((3, HEADS, 256)),
        ],
        out_shape=[
            jax.ShapeDtypeStruct((TOK, 1024), BF),
            jax.ShapeDtypeStruct((TOK, 1024), BF),
            jax.ShapeDtypeStruct((HEADS, 128, 256), F32),
            jax.ShapeDtypeStruct((3, HEADS, 256), F32),
        ],
        scratch_shapes=[pltpu.VMEM((2, TOK, 256), F32)],
        compiler_params=VMEM,
    )(normed, kv_weight, kv_weight, latents, d_attended)


STEPS = HEADS // GROUP


def step_at(step, core):
    return (step + STEPS // 2 * (1 - core[0])) & (STEPS - 1)


def attend_grad_kernel(
    core, normed, k_in, v_in, wk, wv, q, up, lse, dots, factor, weighted,
    send, keep, dn_sc, nt_sc,
):
    step = pl.program_id(0)
    first = step_at(step, core) * GROUP

    @pl.when(step == 0)
    def _():
        nt_sc[...] = normed[...].T
        dn_sc[...] = jnp.zeros_like(dn_sc)

    w = jnp.concatenate([x[:, lane(n)] for n in range(GROUP) for x in (wk, wv)], axis=1)
    level = [lse[pl.ds(first + n, 1), :] for n in range(GROUP)]
    row_dots = [dots[pl.ds(first + n, 1), :] for n in range(GROUP)]
    qg = [jnp.zeros((128, 256), F32)] * GROUP
    wg = jnp.zeros((256, 256 * GROUP), F32)
    units = [(c, n) for c in range(TOK // CHUNK) for n in range(GROUP)]

    def products(c, n):
        rows = slice(c * CHUNK, (c + 1) * CHUNK)
        return (
            dot(k_in[rows, lane(n)], q[:, lane(n)], NT),
            dot(v_in[rows, lane(n)], up[:, lane(n)], NT),
        )

    d_proj = []
    ahead = products(*units[0])
    for at, (c, n) in enumerate(units):
        rows = slice(c * CHUNK, (c + 1) * CHUNK)
        s, dp = ahead
        if at + 1 < len(units):
            ahead = products(*units[at + 1])
        p = jnp.exp2(s * SCALE2 - level[n])
        ds = (p * (dp - row_dots[n])).astype(BF)
        qg[n] = qg[n] + dot(k_in[rows, lane(n)], ds, TN)
        d_proj.append((dot(ds, q[:, lane(n)]) * SCALE).astype(BF))
        d_proj.append(dot(p.astype(BF), up[:, lane(n)]).astype(BF))
        if n == GROUP - 1:
            d_proj = jnp.concatenate(d_proj, axis=1)
            wg = wg + dot(nt_sc[:, rows], d_proj)
            dn_sc[rows, :] += dot(d_proj, w, NT)
            d_proj = []
    att = [(weighted[n] * factor[pl.ds(first + n, 1), :]).T for n in range(GROUP)]
    qg = [(x * SCALE).T for x in qg]

    def put(out):
        for n in range(GROUP):
            out[0, n] = att[n]
            out[1, n] = qg[n]
            out[2, n] = wg[:, lane(2 * n)]
            out[3, n] = wg[:, lane(2 * n + 1)]

    @pl.when(step < STEPS // 2)
    def _():
        put(send)

    @pl.when(step >= STEPS // 2)
    def _():
        put(keep)


def norm_grad_kernel(dn_in, centred, inverse, gain, d_mixed, gain_grad, top, bot, left, right, l_sc, r_sc, c_sc):
    def body(n, total):
        rows = pl.ds(pl.multiple_of(n * BLOCK, BLOCK), BLOCK)
        x = centred[rows, :]
        inv = inverse[rows, :]
        dn = dn_in[rows, :]
        total = total + jnp.sum(dn * x, axis=0, keepdims=True)
        g = dn * gain[...]
        mean = jnp.sum(g, axis=-1, keepdims=True) * (1.0 / CH)
        slope = jnp.sum(g * x, axis=-1, keepdims=True) * (1.0 / CH)
        inv = jnp.concatenate([inv, inv], axis=1)
        d_mixed[rows, :] = (inv * (g - mean - x * slope)).astype(BF)
        return total

    gain_grad[...] = lax.fori_loop(0, TOK // BLOCK, body, jnp.zeros((1, CH), F32))
    write_edges(d_mixed, top, bot, left, right, l_sc, r_sc, c_sc)


def norm_grad(dn, centred, inverse, gain):
    outs = pl.pallas_call(
        norm_grad_kernel,
        name="norm_grad",
        out_shape=[jax.ShapeDtypeStruct((TOK, CH), BF), jax.ShapeDtypeStruct((1, CH), F32)] + EDGE_SHAPES,
        scratch_shapes=EDGE_SCRATCH,
        compiler_params=VMEM,
        cost_estimate=COST,
    )(dn, centred, inverse, gain)
    return outs[0], outs[1], outs[2:]


def attend_grad(
    core, normed, k, v, kv_weight, latents, d_attended, lse, dots, factor, weighted
):
    def full(shape):
        return pl.BlockSpec(shape, lambda n, core: (0,) * len(shape))

    def head(rows, first=0):
        return pl.BlockSpec((rows, 128 * GROUP), lambda n, core: (0, step_at(n, core) + first))

    half = STEPS // 2
    block = (4, GROUP, 256, 128)
    part = jax.ShapeDtypeStruct((4, HEADS // 2, 256, 128), F32)
    outs = pl.pallas_call(
        attend_grad_kernel,
        name="attend_grad",
        grid_spec=pltpu.PrefetchScalarGridSpec(
            num_scalar_prefetch=1,
            grid=(STEPS,),
            in_specs=[
                full((TOK, CH)),
                head(TOK),
                head(TOK),
                head(CH),
                head(CH, STEPS),
                head(256),
                head(256),
                full((HEADS, 256)),
                full((HEADS, 256)),
                full((HEADS, 256)),
                pl.BlockSpec((GROUP, 128, 256), lambda n, core: (step_at(n, core), 0, 0)),
            ],
            out_specs=[
                pl.BlockSpec(block, lambda n, core: (0, jnp.minimum(n, half - 1), 0, 0)),
                pl.BlockSpec(block, lambda n, core: (0, jnp.maximum(n - half, 0), 0, 0)),
                full((TOK, CH)),
            ],
            scratch_shapes=[pltpu.VMEM((CH, TOK), BF)],
        ),
        out_shape=[
            part,
            part,
            jax.ShapeDtypeStruct((TOK, CH), F32),
        ],
        compiler_params=VMEM,
        cost_estimate=COST,
    )(core, normed, k, v, kv_weight, kv_weight, latents, d_attended, lse, dots, factor, weighted)
    return outs


def kernel_grad_body(emb, above, below, lh, rh, d_mixed, out, wide, d_sc, l_sc, r_sc, c_sc):
    assemble(wide, emb, (above, below, lh, rh), l_sc, r_sc, c_sc)
    d_sc[...] = d_mixed[...].astype(F32)
    for half in range(2):
        lanes = pl.ds(half * 128, 128)
        for i in range(KSIZE):

            def body(n, acc):
                acc = list(acc)
                for r in range(4):
                    a = 4 * n + r
                    xs = [wide[a + i, c, :, lanes] for c in range(WIDE)]
                    base = pl.multiple_of(a * COLS, COLS)
                    ds = [d_sc[pl.ds(base + cb * 8, 8), lanes] for cb in range(8)]
                    for cb in range(8):
                        for j in range(KSIZE):
                            acc[j] = acc[j] + xs[cb + j] * ds[cb]
                return tuple(acc)

            zero = jnp.zeros((8, 128), F32)
            acc = lax.fori_loop(0, ROWS // 4, body, (zero,) * KSIZE)
            for j in range(KSIZE):
                n = i * KSIZE + j
                out[n : n + 1, lanes] = jnp.sum(acc[j], axis=0, keepdims=True)


def kernel_grad(emb, halo, d_mixed):
    return pl.pallas_call(
        kernel_grad_body,
        name="kernel_grad",
        out_shape=jax.ShapeDtypeStruct((KSIZE * KSIZE, CH), F32),
        scratch_shapes=[pltpu.VMEM((ROWS + 2 * HALO, WIDE, 8, CH), F32), pltpu.VMEM((TOK, CH), F32)]
        + EDGE_SCRATCH,
        compiler_params=VMEM,
        cost_estimate=COST,
    )(emb, *halo, d_mixed)


def conv_back_body(d_mixed, above, below, lh, rh, kern, z, kern_grad, gain_grad, small, wide, d_sc, w_sc, l_sc, r_sc, c_sc):
    assemble(wide, d_mixed, (above, below, lh, rh), l_sc, r_sc, c_sc)
    spread_weights(kern, w_sc)
    zero = jnp.zeros((8, 128), F32)

    def body(n, bias):
        bias = list(bias)
        for half in range(2):
            accs = conv_rows(wide, w_sc, 2 * n, half, True)
            for r in range(2):
                a = 2 * n + r
                acc = jnp.concatenate(accs[r], axis=0).astype(BF)
                d_sc[a & 7, pl.ds(pl.multiple_of((a >> 3) * 64, 64), 64), pl.ds(half * 128, 128)] = acc
                bias[half] = bias[half] + jnp.sum(acc.astype(F32).reshape(8, 8, 128), axis=0)
        return tuple(bias)

    bias = lax.fori_loop(0, ROWS // 2, body, (zero, zero))
    for half in range(2):
        small[98, :, half * 128 : (half + 1) * 128] = jnp.sum(bias[half], axis=0, keepdims=True)
    for n in range(KSIZE * KSIZE):
        small[48 + n] = kern_grad[n : n + 1, :]
    small[97] = gain_grad[...]
    small[99:128] = jnp.zeros((29, 1, CH), F32)
    total = [jnp.zeros((16, CH), F32) for _ in range(4)]
    for a8 in range(8):
        part = dot(z[...], d_sc[a8], TN)
        for v in range(4):
            first = v * 128 + a8 * 16
            total[v] = total[v] + part[first : first + 16, :]
    for v in range(4):
        for fu in range(12):
            small[fu * 4 + v] = total[v][fu : fu + 1, :]


def conv_back(d_mixed, halo, conv_kernel, z, kern_grad, gain_grad):
    return pl.pallas_call(
        conv_back_body,
        name="conv_back",
        out_shape=jax.ShapeDtypeStruct((128, 1, CH), F32),
        scratch_shapes=[
            pltpu.VMEM((ROWS + 2 * HALO, WIDE, 8, CH), F32),
            pltpu.VMEM((8, 256, CH), BF),
            pltpu.VMEM((KSIZE * KSIZE, 8, CH), F32),
        ]
        + EDGE_SCRATCH,
        compiler_params=VMEM,
        cost_estimate=COST,
    )(d_mixed, *halo, conv_kernel, z, kern_grad, gain_grad)


CHIPS = ("z", "x", "y")
ALL = ("z", "core", "x", "y")
PAIR = [(0, 1), (1, 0)]
STAGES = (("z", "core"), ("x", "y"))


def gather(x, axes):
    n = lax.axis_size(axes)
    copies = jnp.broadcast_to(x[None], (n,) + x.shape)
    return lax.all_to_all(copies, axes, 0, 0, tiled=True)


def combine_stats(stats):
    for axes in STAGES:
        group = gather(stats, axes)
        peak = jnp.max(group[:, 0], axis=0)
        factors = jnp.exp2(group[:, 0] - peak)
        total = jnp.sum(group[:, 1] * factors, axis=0)
        dots = jnp.sum(group[:, 2] * factors, axis=0)
        stats = jnp.stack([peak, total, dots])
    return stats


def collect_body(core, own, other, attended, q_grad, kv_grad):
    h = pl.program_id(0)
    mine = (h // (HEADS // 2)) == core[0]

    def put(x):
        attended[...] = x[0, 0].astype(F32)
        q_grad[...] = x[1, 0].astype(F32)
        kv_grad[:, pl.ds(pl.multiple_of(h * 128, 128), 128)] = x[2, 0].astype(F32)
        kv_grad[:, pl.ds(pl.multiple_of((HEADS + h) * 128, 128), 128)] = x[3, 0].astype(F32)

    @pl.when(mine)
    def _():
        put(own)

    @pl.when(jnp.logical_not(mine))
    def _():
        put(other)


def collect(core, own, other):
    shape = (4, HEADS // 2, 256, 128)
    block = pl.BlockSpec((4, 1, 256, 128), lambda h, core: (0, h % (HEADS // 2), 0, 0))
    heads = pl.BlockSpec((256, 128), lambda h, core: (0, h))
    return pl.pallas_call(
        collect_body,
        name="collect",
        grid_spec=pltpu.PrefetchScalarGridSpec(
            num_scalar_prefetch=1,
            grid=(HEADS,),
            in_specs=[block, block],
            out_specs=[heads, heads, pl.BlockSpec((256, 2048), lambda h, core: (0, 0))],
        ),
        out_shape=[
            jax.ShapeDtypeStruct((256, 1024), F32),
            jax.ShapeDtypeStruct((256, 1024), F32),
            jax.ShapeDtypeStruct((256, 2048), F32),
        ],
        compiler_params=VMEM,
    )(core, own.reshape(shape), other.reshape(shape))


def split_small_body(small, patch, kern, gain, bias):
    for n in range(48):
        patch[n : n + 1, :] = small[n]
    for n in range(KSIZE * KSIZE):
        kern[n : n + 1, :] = small[48 + n]
    gain[...] = small[97, 0]
    bias[...] = small[98, 0]


def split_small(small):
    return pl.pallas_call(
        split_small_body,
        name="split_small",
        out_shape=[
            jax.ShapeDtypeStruct((48, CH), F32),
            jax.ShapeDtypeStruct((KSIZE * KSIZE, CH), F32),
            jax.ShapeDtypeStruct((CH,), F32),
            jax.ShapeDtypeStruct((CH,), F32),
        ],
        compiler_params=VMEM,
    )(small)


def block_sum(parts):
    return jnp.sum(parts.astype(F32), axis=0)


def copies(x):
    return jnp.broadcast_to(x.astype(WIRE)[None], (64,) + x.shape)


def send(x):
    return lax.all_to_all(x, CHIPS, 0, 0, tiled=True)


def send_all(x):
    return lax.all_to_all(x, ALL, 0, 0, tiled=True)


def tie(x, *others):
    return lax.optimization_barrier((x,) + others)


def per_device(
    pixels, patch_weight, patch_bias, conv_kernel, norm_gain, kv_weight, latents, d_attended
):
    gain = norm_gain.reshape(1, CH)
    emb, z, edges = embed(pixels, patch_weight, patch_bias)
    rows = exchange_rows(edges)
    halo = rows + exchange_cols(edges, *rows)
    centred, inverse, normed = conv_forward(emb, halo, conv_kernel, gain)
    k, v, weighted, local = attend(normed, kv_weight, latents, d_attended)
    stats = combine_stats(local)
    lse = stats[0] + jnp.log2(stats[1])
    row_dots = stats[2] / stats[1]
    factor = jnp.exp2(local[0] - stats[0]) / stats[1]
    core = lax.axis_index("core").astype(jnp.int32).reshape(1)
    away, keep, dn = attend_grad(
        core, normed, k, v, kv_weight, latents, d_attended, lse, row_dots, factor, weighted
    )
    away = lax.ppermute(away, "core", PAIR)
    d_mixed, gain_grad, d_edges = norm_grad(dn, centred, inverse, gain)
    d_mixed, away, *d_edges = tie(d_mixed, away, *d_edges)
    message = (keep + away).astype(BF).reshape(64, 64, 128)
    d_mixed, message, *d_edges = tie(d_mixed, message, *d_edges)
    message = send(message)
    d_rows = exchange_rows(d_edges)
    kern = kernel_grad(emb, halo, d_mixed)
    d_mixed, message, kern, *d_rows = tie(d_mixed, message, kern, *d_rows)
    message = copies(block_sum(message))
    d_mixed, message, *d_rows = tie(d_mixed, message, *d_rows)
    message = send(message)
    d_cols = exchange_cols(d_edges, *d_rows)
    small = conv_back(d_mixed, tuple(d_rows) + tuple(d_cols), conv_kernel, z, kern, gain_grad)
    small, message = tie(small, message)
    mine = block_sum(send_all(small))
    small = send_all(jnp.broadcast_to(mine[None], (128,) + mine.shape))
    outs = collect(core, message, lax.ppermute(message, "core", PAIR))
    small, *outs = tie(small, *outs)
    patch, kern, gain, bias = split_small(small)
    return (*outs, gain, kern, patch, bias)


def solution(mesh):
    split = Mesh(mesh.devices.reshape(4, 2, 4, 4), ("z", "core", "x", "y"))
    return jax.shard_map(
        per_device,
        mesh=split,
        in_specs=(P(None, ("z", "core"), ("x", "y")), P(), P(), P(), P(), P(), P(), P()),
        out_specs=(P(), P(), P(), P(), P(), P(), P()),
        check_vma=False,
    )
```
